128 devices in a mesh: seq: 16 (over x, y), exp: 8 (over z, core).
Axes of the slice: x: 4, y: 4, z: 4, core: 2. Of those that a mesh axis runs over, the one named last changes fastest.
Arguments:
- hidden_in: float32 [48, 4, 2048], P('seq'), may hold values from -6 to 6
- cache_lens: int32 [48], replicated, may hold values from 64 to 16384, as said below
- slot_request: int32 [496], P('seq'), may hold values from -1 to 47, as said below
- slot_block: int32 [496], P('seq'), may hold values from 0 to 128, as said below
- key_cache: bfloat16 [496, 128, 2048], P('seq', None, 'exp'), may hold values from -70 to 70
- value_cache: bfloat16 [496, 128, 2048], P('seq', None, 'exp'), may hold values from -6 to 6
- attn_gain: float32 [2048], replicated, may hold values from 0.5 to 1.5
- query_weight: bfloat16 [2048, 2048], P(None, 'exp'), may hold values from -0.125 to 0.125
- key_weight: bfloat16 [2048, 2048], P(None, 'exp'), may hold values from -0.125 to 0.125
- value_weight: bfloat16 [2048, 2048], P(None, 'exp'), may hold values from -0.125 to 0.125
- out_weight: bfloat16 [2048, 2048], P('exp'), may hold values from -0.125 to 0.125
- ffn_gain: float32 [2048], replicated, may hold values from 0.5 to 1.5
- expert_ids: int32 [48, 4, 6], P('seq'), may hold values from 0 to 63, all different within a row; in each aligned block of 12 rows (0 to 11, 12 to 23, ..., all dimensions but the last counted through in order) at most 3 rows name the same one
- expert_weights: float32 [48, 4, 6], P('seq'), may hold values from 0.05 to 0.6
- gate_experts: bfloat16 [64, 2048, 1408], P('seq', None, 'exp'), may hold values from -0.125 to 0.125
- up_experts: bfloat16 [64, 2048, 1408], P('seq', None, 'exp'), may hold values from -0.125 to 0.125
- down_experts: bfloat16 [64, 1408, 2048], P('seq', 'exp'), may hold values from -0.15625 to 0.15625
- gate_shared: bfloat16 [2048, 2816], P(None, 'exp'), may hold values from -0.125 to 0.125
- up_shared: bfloat16 [2048, 2816], P(None, 'exp'), may hold values from -0.125 to 0.125
- down_shared: bfloat16 [2816, 2048], P('exp'), may hold values from -0.109375 to 0.109375
Outputs:
- hidden_out: float32 [48, 4, 2048], P('seq', None, 'exp')
- key_cache_out: bfloat16 [496, 128, 2048], P('seq', None, 'exp')
- value_cache_out: bfloat16 [496, 128, 2048], P('seq', None, 'exp')
The draws below stay inside these ranges and needn't reach their ends.
Inputs may be any that keep to these rules, and one draw needn't show every extreme that they name: `cache_lens`: exactly two requests have 16384 positions and one has 512; the others lie between 64 and 512. `slot_request`: each block of 128 positions of each request, up to position cache_lens + 3, is held by exactly one slot; -1 marks an empty slot. `slot_block`: empty slots carry 0. `expert_ids`: among the rows of one index of seq, no expert is named more than 3 times.
All inputs are finite; a program needn't handle non-finite values.
Results may differ from the reference program's by a relative error of at most 0.02.
Values may be sent and summed in bfloat16 or wider, within the bound.
A program may use at most 128 MiB of HBM per device.

```python
import math
import jax
import jax.numpy as jnp
import numpy as np
from jax import lax

D = 2048
H = 16
HD = 128
EXPERTS = 64
FE = 1408
TOP = 6
SHARED_FF = 2816
STEPS = 4
BLK = 128
LONGLEN = 16384
SHORTMIN = 64
SHORTMAX = 512
REQ_DEV = 3
REQUESTS = 48
POOL = 31
CAP = 3
N_SEQ = 16


def lengths_and_slots(key):
    base = jax.random.fold_in(key, 101)
    length_key, pick_key, place_key = jax.random.split(base, 3)
    lengths = jax.random.randint(length_key, (REQUESTS,), SHORTMIN, SHORTMAX + 1, dtype=jnp.int32)
    chosen = jax.random.permutation(pick_key, REQUESTS).astype(jnp.int32)
    lengths = lengths.at[chosen[0]].set(LONGLEN).at[chosen[1]].set(LONGLEN).at[chosen[2]].set(SHORTMAX)
    block_counts = (lengths + STEPS + BLK - 1) // BLK
    ends = jnp.cumsum(block_counts).astype(jnp.int32)
    starts = ends - block_counts
    total_slots = N_SEQ * POOL
    listing = jnp.arange(total_slots, dtype=jnp.int32)
    owner = jnp.sum((starts[None, :] <= listing[:, None]).astype(jnp.int32), axis=1) - 1
    filled = listing < ends[-1]
    block_number = listing - starts[owner]
    owner = jnp.where(filled, owner, -1).astype(jnp.int32)
    block_number = jnp.where(filled, block_number, 0).astype(jnp.int32)
    placement = jax.random.permutation(place_key, total_slots).astype(jnp.int32)
    return (lengths, owner[placement], block_number[placement])


def draw_cache_lens(key, part):
    return lengths_and_slots(key)[0]


def draw_slot_request(key, part):
    return lengths_and_slots(key)[1]


def draw_slot_block(key, part):
    return lengths_and_slots(key)[2]


def draw_key_cache(key, part):
    total_slots = N_SEQ * POOL
    shape = (total_slots, BLK, H * HD)
    result = jnp.clip(jax.random.normal(key, shape, jnp.float32), -4.0, 4.0)
    return result.astype(jnp.bfloat16)


def block_levels(rng, shape, shards, low, top_value):
    def one(position, blocks):
        heights = jax.random.uniform(jax.random.fold_in(jax.random.fold_in(rng, 6), position), (blocks,), jnp.float32, low / len(shards), top_value / len(shards))
        return jnp.repeat(jnp.exp(heights), shape[position] // blocks).reshape((-1,) + (1,) * (len(shape) - position - 1))

    level = one(*shards[0])
    for cut in shards[1:]:
        level = level * one(*cut)
    return level


def routed_block(rng, own, number, rows, amount, top, reach, lean):
    order = jax.random.permutation(rng, amount)
    packed, common = portions_of(amount, rows * top, reach, lean, True), portions_of(amount, rows * top, reach, lean, False)
    places = jnp.arange(amount)

    def named(sizes, turn):
        used = int((sizes > 0).sum())
        fixed = max(1, used // 4)
        passed = fixed + (places - fixed + turn * (used - fixed)) % max(1, amount - fixed)
        return jnp.zeros((amount,), jnp.int32).at[order[jnp.where(places < fixed, places, passed)]].set(jnp.asarray(sizes, jnp.int32))

    sizes = jnp.where(number % 4 == 0, named(packed, number // 4), named(common, number - number // 4 - 1))
    mixed = jax.random.permutation(jax.random.fold_in(own, 3), amount)
    source_of, receiver = mixed[0:amount // 2 * 2:2], mixed[1:amount // 2 * 2:2]
    room = jnp.minimum(sizes[source_of] - 1, reach - sizes[receiver]) // 2
    room = jnp.where((source_of == order[0]) | (receiver == order[0]) | (sizes[receiver] == 0), 0, jnp.maximum(room, 0))
    passed = jax.random.randint(jax.random.fold_in(own, 4), (amount // 2,), 0, 1 << 20) % (room + 1)
    sizes = sizes.at[source_of].add(-passed).at[receiver].add(passed)
    items = jnp.searchsorted(jnp.cumsum(sizes), jnp.arange(rows * top), side="right").astype(jnp.int32)
    table = items.reshape(top, rows).T
    table = table[jax.random.permutation(jax.random.fold_in(own, 1), rows)]
    turn = jax.random.randint(jax.random.fold_in(own, 2), (rows, 1), 0, top)
    return jnp.take_along_axis(table, (jnp.arange(top)[None, :] + turn) % top, axis=1)


def portions_of(amount, total, bound, lean, full):
    loads = [(1 << 20) // math.isqrt(grade ** lean) + 1 for grade in range(1, amount + 1)]
    largest = bound if full else min(bound, max(-(-total // amount), total * loads[0] // sum(loads)))
    least = 1 if total - largest >= amount - 1 else 0
    given, rest = [largest] + [least] * (amount - 1), total - largest - least * (amount - 1)
    while rest > 0:
        movable = [i for i in range(1, amount) if given[i] < largest] or [i for i in range(1, amount) if given[i] < bound]
        mass, budget = sum([loads[i] for i in movable]), rest
        for i in movable:
            addition = min(bound - given[i], max(1, budget * loads[i] // mass), rest)
            given[i] = given[i] + addition
            rest = rest - addition
    return np.array(given)


def gaussian(rng, extent, deviation, bound, cuts=(), kind=jnp.bfloat16):
    loudness = block_levels(rng, extent, cuts, -0.22, 0.18) if cuts else 1.0
    drawn = jax.random.normal(rng, extent, jnp.float32) * deviation * loudness
    return jnp.minimum(jnp.maximum(drawn, -bound), bound).astype(kind)


def setup_inputs(seed: int = 0) -> dict:
    arg_keys = jax.random.split(jax.random.key(seed), 21)
    hidden_in = gaussian(arg_keys[0], (REQUESTS, STEPS, D), 1.0, 6.0, ((0, 16),), jnp.float32)
    cache_lens = draw_cache_lens(jax.random.fold_in(arg_keys[20], 71), 0)
    slot_request = draw_slot_request(jax.random.fold_in(arg_keys[20], 71), 0)
    slot_block = draw_slot_block(jax.random.fold_in(arg_keys[20], 71), 0)
    key_cache = draw_key_cache(jax.random.fold_in(arg_keys[20], 71), 0)
    value_cache = gaussian(arg_keys[5], (N_SEQ * POOL, BLK, H * HD), 1.0, 6.0, ((0, 16), (2, 8)))
    attn_gain = jnp.clip(1.0 + 0.1 * jax.random.normal(arg_keys[6], (D,), jnp.float32), 0.5, 1.5)
    query_weight = gaussian(arg_keys[7], (D, H * HD), D ** -0.5, 0.125, ((1, 8),))
    key_weight = gaussian(arg_keys[8], (D, H * HD), D ** -0.5, 0.125, ((1, 8),))
    value_weight = gaussian(arg_keys[9], (D, H * HD), D ** -0.5, 0.125, ((1, 8),))
    out_weight = gaussian(arg_keys[10], (H * HD, D), (H * HD) ** -0.5, 0.125, ((0, 8),))
    ffn_gain = jnp.clip(1.0 + 0.1 * jax.random.normal(arg_keys[11], (D,), jnp.float32), 0.5, 1.5)
    expert_ids_keys = jax.random.split(jax.random.fold_in(arg_keys[12], 1), REQUESTS * STEPS // (REQ_DEV * STEPS))
    expert_ids_turns = jax.random.permutation(jax.random.fold_in(arg_keys[12], 3), REQUESTS * STEPS // (REQ_DEV * STEPS))
    expert_ids = jax.vmap(lambda own, number: routed_block(jax.random.fold_in(arg_keys[12], 2), own, number, REQ_DEV * STEPS, EXPERTS, TOP, CAP, 2))(expert_ids_keys, expert_ids_turns).reshape((REQUESTS, STEPS, TOP))
    expert_weights = jnp.clip(0.05 + 0.55 * jax.random.uniform(arg_keys[13], (REQUESTS, STEPS, TOP), jnp.float32) ** block_levels(arg_keys[13], (REQUESTS, STEPS, TOP), ((0, 16),), -0.2, 0.2), 0.05, 0.6)
    gate_experts = gaussian(arg_keys[14], (EXPERTS, D, FE), D ** -0.5, 0.125, ((0, 16), (2, 8)))
    up_experts = gaussian(arg_keys[15], (EXPERTS, D, FE), D ** -0.5, 0.125, ((0, 16), (2, 8)))
    down_experts = gaussian(arg_keys[16], (EXPERTS, FE, D), FE ** -0.5, 0.15625, ((0, 16), (1, 8)))
    gate_shared = gaussian(arg_keys[17], (D, SHARED_FF), D ** -0.5, 0.125, ((1, 8),))
    up_shared = gaussian(arg_keys[18], (D, SHARED_FF), D ** -0.5, 0.125, ((1, 8),))
    down_shared = gaussian(arg_keys[19], (SHARED_FF, D), SHARED_FF ** -0.5, 0.109375, ((0, 8),))
    return dict(hidden_in=hidden_in, cache_lens=cache_lens, slot_request=slot_request, slot_block=slot_block, key_cache=key_cache, value_cache=value_cache, attn_gain=attn_gain, query_weight=query_weight, key_weight=key_weight, value_weight=value_weight, out_weight=out_weight, ffn_gain=ffn_gain, expert_ids=expert_ids, expert_weights=expert_weights, gate_experts=gate_experts, up_experts=up_experts, down_experts=down_experts, gate_shared=gate_shared, up_shared=up_shared, down_shared=down_shared)


def rms_scale(values, gain):
    mean_square = lax.optimization_barrier(jnp.mean(values * values, axis=-1, keepdims=True))
    return values * lax.rsqrt(mean_square + 1e-06) * gain

def rotate(vectors, positions):
    half_size = vectors.shape[-1] // 2
    exponent = jnp.arange(half_size, dtype=jnp.float32) * (2.0 / vectors.shape[-1])
    frequency = jnp.power(jnp.float32(10000.0), -exponent)
    angles = positions.astype(jnp.float32)[..., None] * frequency
    cosine = jnp.cos(angles)[..., None, :]
    sine = jnp.sin(angles)[..., None, :]
    first_half = vectors[..., :half_size]
    second_half = vectors[..., half_size:]
    return jnp.concatenate([first_half * cosine - second_half * sine, second_half * cosine + first_half * sine], axis=-1)

def append_rows(cache, new_rows, slot_valid, slot_req, rel_pos):
    updated = cache
    for step_index in range(new_rows.shape[1]):
        hit_mask = slot_valid[:, None] & (rel_pos == step_index)
        updated = jnp.where(hit_mask[..., None], new_rows[slot_req, step_index][:, None, :], updated)
    return updated

def slot_partials(queries, keys, values, slot_valid, slot_req, slot_block, lengths):
    pool_count, block_size, full_width = keys.shape
    steps, heads, head_size = (queries.shape[1], queries.shape[2], queries.shape[3])
    slot_queries = queries[slot_req]
    key_heads = keys.reshape(pool_count, block_size, heads, head_size)
    value_heads = values.reshape(pool_count, block_size, heads, head_size)
    scores = jnp.einsum('pthd,pkhd->pthk', slot_queries.astype(jnp.float32), key_heads.astype(jnp.float32)) / math.sqrt(head_size)
    positions = slot_block[:, None] * block_size + jnp.arange(block_size, dtype=jnp.int32)[None, :]
    limits = lengths[slot_req][:, None] + jnp.arange(steps, dtype=jnp.int32)[None, :] + 1
    allowed = slot_valid[:, None, None] & (positions[:, None, :] < limits[:, :, None])
    allowed = allowed[:, :, None, :]
    block_max = lax.optimization_barrier(jnp.max(jnp.where(allowed, scores, -1e+30), axis=-1))
    safe_max = jnp.where(block_max > -1e+29, block_max, 0.0)
    weights = jnp.where(allowed, jnp.exp(scores - safe_max[..., None]), 0.0)
    totals = lax.optimization_barrier(jnp.sum(weights, axis=-1))
    rounded = weights.astype(jnp.bfloat16)
    outputs = jnp.einsum('pthk,pkhd->pthd', rounded.astype(jnp.float32), value_heads.astype(jnp.float32))
    return (block_max, totals, outputs)

def request_partials(block_max, totals, outputs, slot_valid, slot_req, requests):
    owner = slot_valid[:, None] & (slot_req[:, None] == jnp.arange(requests, dtype=jnp.int32)[None, :])
    request_max = lax.optimization_barrier(jnp.max(jnp.where(owner[:, :, None, None], block_max[:, None], -1e+30), axis=0))
    factor = jnp.where(slot_valid[:, None, None], jnp.exp(block_max - request_max[slot_req]), 0.0)
    owner_float = owner.astype(jnp.float32)
    request_total = jnp.einsum('pb,pth->bth', owner_float, totals * factor, precision=lax.Precision.HIGHEST)
    request_output = jnp.einsum('pb,pthd->bthd', owner_float, outputs * factor[..., None], precision=lax.Precision.HIGHEST)
    return (request_max, request_total, request_output)

def reference(hidden_in, cache_lens, slot_request, slot_block, key_cache, value_cache, attn_gain, query_weight, key_weight, value_weight, out_weight, ffn_gain, expert_ids, expert_weights, gate_experts, up_experts, down_experts, gate_shared, up_shared, down_shared):
    requests, steps, width = hidden_in.shape
    flat = hidden_in.reshape(requests * steps, width)
    normed = rms_scale(flat, attn_gain).astype(jnp.bfloat16)
    positions = cache_lens[:, None] + jnp.arange(steps, dtype=jnp.int32)[None, :]
    query_full = jnp.dot(normed, query_weight, preferred_element_type=jnp.float32).reshape(requests, steps, H, HD)
    queries = rotate(query_full, positions).astype(jnp.bfloat16)
    key_full = jnp.dot(normed, key_weight, preferred_element_type=jnp.float32).reshape(requests, steps, H, HD)
    new_keys = rotate(key_full, positions).astype(jnp.bfloat16).reshape(requests, steps, H * HD)
    new_values = jnp.dot(normed, value_weight, preferred_element_type=jnp.float32).astype(jnp.bfloat16).reshape(requests, steps, H * HD)
    slot_valid = slot_request >= 0
    slot_req = jnp.where(slot_valid, slot_request, 0).astype(jnp.int32)
    rel_pos = slot_block[:, None] * BLK + jnp.arange(BLK, dtype=jnp.int32)[None, :] - cache_lens[slot_req][:, None]
    key_out = append_rows(key_cache, new_keys, slot_valid, slot_req, rel_pos)
    value_out = append_rows(value_cache, new_values, slot_valid, slot_req, rel_pos)
    block_max, totals, outputs = slot_partials(queries, key_out, value_out, slot_valid, slot_req, slot_block, cache_lens)
    request_max, request_total, request_output = request_partials(block_max, totals, outputs, slot_valid, slot_req, requests)
    attended = (request_output / request_total[..., None]).astype(jnp.bfloat16).reshape(requests * steps, H * HD)
    residual = flat + jnp.dot(attended, out_weight, preferred_element_type=jnp.float32)
    ffn_in = rms_scale(residual, ffn_gain).astype(jnp.bfloat16)
    shared_inner = (jax.nn.silu(jnp.dot(ffn_in, gate_shared, preferred_element_type=jnp.float32)) * jnp.dot(ffn_in, up_shared, preferred_element_type=jnp.float32)).astype(jnp.bfloat16)
    shared_out = jnp.dot(shared_inner, down_shared, preferred_element_type=jnp.float32)
    flat_ids = expert_ids.reshape(requests * steps, TOP)
    flat_gates = expert_weights.reshape(requests * steps, TOP)
    coefficient = lax.optimization_barrier(jnp.sum(jnp.where(flat_ids[:, :, None] == jnp.arange(EXPERTS, dtype=jnp.int32)[None, None, :], flat_gates[:, :, None], 0.0), axis=1))

    def expert_step(total, inputs):
        gate_matrix, up_matrix, down_matrix, column = inputs
        inner = (jax.nn.silu(jnp.dot(ffn_in, gate_matrix, preferred_element_type=jnp.float32)) * jnp.dot(ffn_in, up_matrix, preferred_element_type=jnp.float32)).astype(jnp.bfloat16)
        return (total + column[:, None] * jnp.dot(inner, down_matrix, preferred_element_type=jnp.float32), None)
    start_total = jnp.zeros((requests * steps, width), jnp.float32)
    scanned = lax.scan(expert_step, start_total, (gate_experts, up_experts, down_experts, coefficient.T))
    result = residual + scanned[0] + shared_out
    return (result.reshape(requests, steps, width), key_out, value_out)
```

```python
import functools
import math

import jax
import jax.numpy as jnp
import numpy as np
from jax import lax
from jax.experimental import pallas as pl
from jax.experimental.pallas import tpu as pltpu
from jax.sharding import PartitionSpec as P

HD = 128
MESH = pl.DeviceIdType.MESH
F32 = jnp.float32
BF16 = jnp.bfloat16
ROWS = 16


def peer(seq, exp):
    return {"seq": seq, "exp": exp}


def rows_of(ref, scratch):
    count, steps, _ = ref.shape
    for b in range(count):
        scratch[pl.ds(b * steps, steps), :] = ref[b]
    used = count * steps
    scratch[pl.ds(used, ROWS - used), :] = jnp.zeros((ROWS - used, ref.shape[2]), F32)


def split_two(values):
    high = values.astype(BF16)
    low = (values - high.astype(F32)).astype(BF16)
    return high, low


def project_kernel(
    lens_ref, freq_ref, hidden_ref, gain_ref, ids_ref, ew_ref, wq_ref, wk_ref, wv_ref,
    out_ref, xs, wbuf, coef, wsem, send_sem, recv_sem,
):
    ns = lax.axis_size("seq")
    me = lax.axis_index("seq")
    exp = lax.axis_index("exp")
    requests, steps, width = hidden_ref.shape
    cols = wq_ref.shape[1]
    experts = coef.shape[1] // 2

    barrier = pltpu.get_barrier_semaphore()

    def greet(i, _):
        pl.semaphore_signal(barrier, inc=1, device_id=peer((me + i) % ns, exp), device_id_type=MESH)
        return 0

    lax.fori_loop(1, ns, greet, 0)
    loads = []
    for k, w in enumerate((wq_ref, wk_ref, wv_ref)):
        load = pltpu.make_async_copy(w, wbuf.at[k], wsem.at[k])
        load.start()
        loads.append(load)

    rows_of(hidden_ref, xs)
    x = xs[...]
    mean_square = jnp.mean(x * x, axis=-1, keepdims=True)
    normed = (x * lax.rsqrt(mean_square + 1e-06) * gain_ref[...]).astype(BF16)

    row = lax.broadcasted_iota(jnp.int32, (ROWS, HD), 0)
    lane = lax.broadcasted_iota(jnp.int32, (ROWS, HD), 1)
    length = jnp.zeros((ROWS, HD), jnp.int32)
    for b in range(requests):
        length = jnp.where(row // steps == b, lens_ref[me * requests + b], length)
    position = (length + row % steps).astype(F32)
    angles = position * freq_ref[...]
    cosine = jnp.cos(angles)
    sine = jnp.where(lane < HD // 2, -jnp.sin(angles), jnp.sin(angles))

    def rotate(v):
        parts = []
        for h in range(cols // HD):
            head = v[:, h * HD : (h + 1) * HD]
            parts.append(head * cosine + pltpu.roll(head, HD // 2, 1) * sine)
        return jnp.concatenate(parts, axis=1)

    coef[...] = jnp.zeros(coef.shape, F32)
    expert = lax.broadcasted_iota(jnp.int32, (steps, experts), 1)
    for b in range(requests):
        total = jnp.zeros((steps, experts), F32)
        for j in range(ids_ref.shape[2]):
            total += jnp.where(ids_ref[b][:, j : j + 1] == expert, ew_ref[b][:, j : j + 1], 0.0)
        coef[pl.ds(b * steps, steps), pl.ds(0, experts)] = total
    high, low = split_two(coef[:, 0:experts])

    for k in range(3):
        loads[k].wait()
        product = jnp.dot(normed, wbuf[k], preferred_element_type=F32)
        if k < 2:
            product = rotate(product)
        out_ref[me, :, k * cols : (k + 1) * cols] = product.astype(BF16)
    out_ref[me, :, 3 * cols : 3 * cols + 2 * experts] = jnp.concatenate([high, low], axis=1)

    pl.semaphore_wait(barrier, ns - 1)

    def push(i, _):
        pltpu.make_async_remote_copy(
            src_ref=out_ref.at[me],
            dst_ref=out_ref.at[me],
            send_sem=send_sem,
            recv_sem=recv_sem,
            device_id=peer((me + i) % ns, exp),
            device_id_type=MESH,
        ).start()
        return 0

    lax.fori_loop(1, ns, push, 0)
    everything = pltpu.make_async_remote_copy(
        src_ref=out_ref.at[pl.ds(0, ns - 1)],
        dst_ref=out_ref.at[pl.ds(0, ns - 1)],
        send_sem=send_sem,
        recv_sem=recv_sem,
        device_id=peer((me + 1) % ns, exp),
        device_id_type=MESH,
    )
    everything.wait_recv()
    everything.wait_send()


def attend_kernel(
    req_ref, blk_ref, lens_ref, gath_ref, key_ref, value_ref,
    key_out, value_out, part_ref, kbuf, vbuf, qbd, newkv, acc_m, acc_l, in_sem, out_sem,
    *, requests, steps, group,
):
    pool, block, cols = key_ref.shape
    ns = gath_ref.shape[0]
    heads = cols // HD
    hr = heads * steps
    starts = list(range(0, pool, group))
    sizes = [min(group, pool - s) for s in starts]

    def copies(g, into):
        span = pl.ds(starts[g], sizes[g])
        pairs = ((key_ref, kbuf, key_out), (value_ref, vbuf, value_out))
        result = []
        for n, (source, buf, target) in enumerate(pairs):
            if into:
                result.append(pltpu.make_async_copy(source.at[span], buf.at[span], in_sem.at[n, g]))
            else:
                result.append(pltpu.make_async_copy(buf.at[span], target.at[span], out_sem.at[n, g]))
        return result

    for g in range(len(starts)):
        for c in copies(g, True):
            c.start()

    qlane = lax.broadcasted_iota(jnp.int32, (hr, cols), 1) // HD
    qrow = lax.broadcasted_iota(jnp.int32, (hr, cols), 0) // steps
    for s in range(ns):
        q = gath_ref[s, :, 0:cols].astype(F32)
        kv = gath_ref[s, :, cols : 3 * cols].astype(F32)
        for b in range(requests):
            part = q[b * steps : (b + 1) * steps, :]
            both = jnp.concatenate([part] * heads, axis=0)
            qbd[s * requests + b] = jnp.where(qlane == qrow, both, 0.0).astype(BF16)
            newkv[s * requests + b] = kv[b * steps : (b + 1) * steps, :]

    acc_m[...] = jnp.full(acc_m.shape, -1e30, F32)
    acc_l[...] = jnp.zeros(acc_l.shape, F32)
    part_ref[...] = jnp.zeros(part_ref.shape, F32)

    scale = 1.0 / math.sqrt(HD)
    lane = lax.broadcasted_iota(jnp.int32, (hr, block), 1)
    step = lax.broadcasted_iota(jnp.int32, (hr, block), 0) % steps
    upper = lax.broadcasted_iota(jnp.int32, (hr, HD), 0) // steps
    window = 2 * ROWS
    wrow = lax.broadcasted_iota(jnp.int32, (window, cols), 0)

    for g in range(len(starts)):
        for c in copies(g, True):
            c.wait()

        def patch(i, _):
            s = starts[g] + i
            request = jnp.maximum(req_ref[s], 0)
            offset = lens_ref[request] - blk_ref[s] * block

            @pl.when((req_ref[s] >= 0) & (offset > -steps) & (offset < block))
            def _():
                first = jnp.clip(offset // ROWS * ROWS, 0, block - window)
                first = pl.multiple_of(first, ROWS)
                rel = wrow + first - offset
                for n, buf in enumerate((kbuf, vbuf)):
                    tile = buf[s, pl.ds(first, window), :].astype(F32)
                    for t in range(steps):
                        fresh = newkv[request, t : t + 1, n * cols : (n + 1) * cols]
                        tile = jnp.where(rel == t, fresh, tile)
                    buf[s, pl.ds(first, window), :] = tile.astype(BF16)

            return 0

        lax.fori_loop(0, sizes[g], patch, 0)
        for c in copies(g, False):
            c.start()

        for i in range(sizes[g]):
            s = starts[g] + i
            request = jnp.maximum(req_ref[s], 0)
            offset = lens_ref[request] - blk_ref[s] * block
            limit = jnp.where(req_ref[s] >= 0, offset, -(2 * block))
            allowed = lane - step <= limit
            scores = (
                lax.dot_general(
                    qbd[request], kbuf[s], (((1,), (1,)), ((), ())), preferred_element_type=F32
                )
                * scale
            )
            top = jnp.max(jnp.where(allowed, scores, -1e30), axis=-1, keepdims=True)
            safe = jnp.where(top > -1e29, top, 0.0)
            weights = jnp.where(allowed, jnp.exp(scores - safe), 0.0)
            total = jnp.sum(weights, axis=-1, keepdims=True)
            full = jnp.dot(weights.astype(BF16), vbuf[s], preferred_element_type=F32)
            out = full[:, 0:HD]
            for h in range(1, heads):
                out = jnp.where(upper == h, full[:, h * HD : (h + 1) * HD], out)
            owner, which = request // requests, request % requests
            old_m = acc_m[request]
            joint = jnp.maximum(old_m, top)
            old_scale = jnp.exp(old_m - joint)
            new_scale = jnp.exp(top - joint)
            acc_m[request] = joint
            acc_l[request] = acc_l[request] * old_scale + total * new_scale
            part_ref[owner, which] = part_ref[owner, which] * old_scale + out * new_scale

    slane = lax.broadcasted_iota(jnp.int32, (hr, HD), 1)
    for s in range(ns):
        stats = jnp.full((hr, HD), 0.0, F32)
        for b in range(requests):
            stats = jnp.where(slane == b, acc_m[s * requests + b], stats)
            stats = jnp.where(slane == HD // 2 + b, acc_l[s * requests + b], stats)
        part_ref[s, requests] = stats

    for g in range(len(starts)):
        for c in copies(g, False):
            c.wait()


def layer_kernel(
    part_ref, gath_ref, hidden_ref, fgain_ref, wo_ref, ge_ref, ue_ref, de_ref, gs_ref, us_ref, ds_ref,
    out_ref,
    wo, wg, wu, wd, sg, su, sd, rbuf, xs, terms, r3, xbuf, acc, ybuf, ypair, sums, r5, shared,
    wsem, send2, recv2, send3, recv3, send4, recv4, fsend, frecv, psend, precv, send5, recv5,
):
    ns = lax.axis_size("seq")
    ne = lax.axis_size("exp")
    nz = ne // 2
    me = lax.axis_index("seq")
    exp = lax.axis_index("exp")
    z, core = exp // 2, exp % 2
    other = 1 - core
    twin = z * 2 + other
    requests, steps, width = hidden_ref.shape
    hr = part_ref.shape[2]
    cols = out_ref.shape[2]
    own_experts = ge_ref.shape[0]
    count = requests * steps
    total_rows = ns * ROWS

    barrier = pltpu.get_barrier_semaphore()

    def greet_seq(i, _):
        pl.semaphore_signal(barrier, inc=1, device_id=peer((me + i) % ns, exp), device_id_type=MESH)
        return 0

    def greet_exp(i, _):
        pl.semaphore_signal(barrier, inc=1, device_id=peer(me, (exp + i) % ne), device_id_type=MESH)
        return 0

    lax.fori_loop(1, ns, greet_seq, 0)
    lax.fori_loop(1, ne, greet_exp, 0)

    load_wo = pltpu.make_async_copy(wo_ref, wo, wsem.at[0])
    load_wo.start()
    gate_up, shared_in = [], []
    for n, (source, buf) in enumerate(((ge_ref, wg), (ue_ref, wu))):
        for c in range(2):
            for k in range(nz):
                load = pltpu.make_async_copy(
                    source.at[:, pl.ds((k * 2 + c) * cols, cols), :],
                    buf.at[c, :, pl.ds(k * cols, cols), :],
                    wsem.at[1 + (n * 2 + c) * nz + k],
                )
                load.start()
                gate_up.append(load)
    base = 1 + 4 * nz
    load_wd = pltpu.make_async_copy(de_ref, wd, wsem.at[base])
    load_wd.start()
    for n, (source, buf) in enumerate(((gs_ref, sg), (us_ref, su))):
        for c in range(2):
            for k in range(nz):
                load = pltpu.make_async_copy(
                    source.at[pl.ds((k * 2 + c) * cols, cols), :],
                    buf.at[c, pl.ds(k * cols, cols), :],
                    wsem.at[base + 1 + (n * 2 + c) * nz + k],
                )
                load.start()
                shared_in.append(load)
    load_sd = pltpu.make_async_copy(ds_ref, sd, wsem.at[base + 1 + 4 * nz])
    load_sd.start()

    rows_of(hidden_ref, xs)
    rbuf[me] = part_ref[me]
    pl.semaphore_wait(barrier, ns - 1 + ne - 1)

    def push2(i, _):
        to = (me + i) % ns
        pltpu.make_async_remote_copy(
            src_ref=part_ref.at[to], dst_ref=rbuf.at[me], send_sem=send2, recv_sem=recv2,
            device_id=peer(to, exp), device_id_type=MESH,
        ).start()
        return 0

    lax.fori_loop(1, ns, push2, 0)
    all2 = pltpu.make_async_remote_copy(
        src_ref=part_ref.at[pl.ds(0, ns - 1)], dst_ref=rbuf.at[pl.ds(0, ns - 1)],
        send_sem=send2, recv_sem=recv2, device_id=peer((me + 1) % ns, exp), device_id_type=MESH,
    )
    all2.wait_recv()

    top = rbuf[0, requests]
    for s in range(1, ns):
        top = jnp.maximum(top, rbuf[s, requests])
    slane = lax.broadcasted_iota(jnp.int32, (hr, HD), 1)
    factors, total = [], jnp.zeros((hr, HD), F32)
    for s in range(ns):
        stats = rbuf[s, requests]
        factor = jnp.exp(jnp.where(slane < requests, stats - top, 0.0))
        factors.append(factor)
        total += pltpu.roll(stats, HD // 2, 1) * factor
    attended = []
    for b in range(requests):
        summed = jnp.zeros((hr, HD), F32)
        for s in range(ns):
            summed += rbuf[s, b] * factors[s][:, b : b + 1]
        attended.append(summed / total[:, b : b + 1])
    stacked = jnp.concatenate(attended, axis=0).astype(BF16)
    prow = lax.broadcasted_iota(jnp.int32, (ROWS, requests * hr), 0)
    pcol = lax.broadcasted_iota(jnp.int32, (ROWS, requests * hr), 1)
    by_head = []
    for h in range(cols // HD):
        pick = (pcol == prow // steps * hr + h * steps + prow % steps) & (prow < count)
        by_head.append(
            jnp.dot(
                jnp.where(pick, 1.0, 0.0).astype(BF16), stacked, preferred_element_type=F32
            ).astype(BF16)
        )
    own = jnp.concatenate(by_head, axis=1)
    load_wo.wait()
    for e in range(ne):
        terms[e] = jnp.dot(own, wo[:, e * cols : (e + 1) * cols], preferred_element_type=F32)

    def push3(i, _):
        to = (exp + i) % ne
        pltpu.make_async_remote_copy(
            src_ref=terms.at[to], dst_ref=r3.at[exp], send_sem=send3, recv_sem=recv3,
            device_id=peer(me, to), device_id_type=MESH,
        ).start()
        return 0

    lax.fori_loop(1, ne, push3, 0)
    r3[exp] = terms[exp]
    all3 = pltpu.make_async_remote_copy(
        src_ref=terms.at[pl.ds(0, ne - 1)], dst_ref=r3.at[pl.ds(0, ne - 1)],
        send_sem=send3, recv_sem=recv3, device_id=peer(me, (exp + 1) % ne), device_id_type=MESH,
    )
    all3.wait_recv()
    residual = xs[:, pl.ds(pl.multiple_of(exp * cols, cols), cols)]
    for e in range(ne):
        residual += r3[e]

    scaled = residual * fgain_ref[:, pl.ds(pl.multiple_of(exp * cols, cols), cols)]
    square = jnp.sum(residual * residual, axis=-1, keepdims=True)
    brow = lax.broadcasted_iota(jnp.int32, (ROWS, cols), 0)
    blane = lax.broadcasted_iota(jnp.int32, (ROWS, cols), 1)
    line = jnp.sum(jnp.where(brow == blane, square, 0.0), axis=0, keepdims=True)
    high, low = split_two(line)
    scaled = jnp.where(brow == count, high.astype(F32), scaled)
    scaled = jnp.where(brow == count + 1, low.astype(F32), scaled)
    my_rows = pl.ds(pl.multiple_of(me * ROWS, ROWS), ROWS)
    my_cols = pl.ds(pl.multiple_of(z * cols, cols), cols)
    back = pl.ds(pl.multiple_of((z * ns + me) * ROWS, ROWS), ROWS)
    xbuf[core, my_rows, my_cols] = scaled.astype(BF16)

    def push4(i, _):
        to = (z * ns + me + i) % (nz * ns)
        pltpu.make_async_remote_copy(
            src_ref=xbuf.at[core, my_rows, my_cols], dst_ref=xbuf.at[core, my_rows, my_cols],
            send_sem=send4, recv_sem=recv4.at[z],
            device_id=peer(to % ns, to // ns * 2 + core), device_id_type=MESH,
        ).start()
        return 0

    lax.fori_loop(1, nz * ns, push4, 0)
    forwards = []
    for i in range(nz):
        k = (z + i) % nz
        span = pl.ds(0, total_rows - (ROWS if i == 0 else 0))
        kcols = pl.ds(pl.multiple_of(k * cols, cols), cols)
        pltpu.make_async_remote_copy(
            src_ref=xbuf.at[core, span, kcols], dst_ref=xbuf.at[core, span, kcols],
            send_sem=send4, recv_sem=recv4.at[k], device_id=peer(me, twin), device_id_type=MESH,
        ).wait_recv()
        forward = pltpu.make_async_remote_copy(
            src_ref=xbuf.at[core, :, kcols], dst_ref=xbuf.at[core, :, kcols],
            send_sem=fsend.at[k], recv_sem=frecv.at[k], device_id=peer(me, twin), device_id_type=MESH,
        )
        forward.start()
        forwards.append(forward)

    for load in gate_up:
        load.wait()
    for j in range(own_experts):
        acc[0, j] = jnp.dot(xbuf[core], wg[core, j], preferred_element_type=F32)
        acc[1, j] = jnp.dot(xbuf[core], wu[core, j], preferred_element_type=F32)
    for i in range(nz):
        k = (z + i) % nz
        kcols = pl.ds(pl.multiple_of(k * cols, cols), cols)
        pltpu.make_async_remote_copy(
            src_ref=xbuf.at[other, :, kcols], dst_ref=xbuf.at[other, :, kcols],
            send_sem=fsend.at[k], recv_sem=frecv.at[k], device_id=peer(me, twin), device_id_type=MESH,
        ).wait_recv()

    trow = lax.broadcasted_iota(jnp.int32, (total_rows, total_rows), 0)
    tcol = lax.broadcasted_iota(jnp.int32, (total_rows, total_rows), 1)
    spread = (trow // ROWS == tcol // ROWS) & ((tcol % ROWS == count) | (tcol % ROWS == count + 1))
    spread = jnp.where(spread, 1.0, 0.0).astype(BF16)
    square = jnp.zeros((total_rows, HD), F32)
    for c in range(2):
        for k in range(nz):
            square += jnp.dot(
                spread, xbuf[c, :, k * cols : k * cols + HD], preferred_element_type=F32
            )
    lrow = lax.broadcasted_iota(jnp.int32, (total_rows, HD), 0)
    llane = lax.broadcasted_iota(jnp.int32, (total_rows, HD), 1)
    square = jnp.sum(
        jnp.where(lrow % ROWS == llane, square, 0.0), axis=-1, keepdims=True
    )
    scale = lax.rsqrt(square / width + 1e-06)

    experts = (gath_ref.shape[2] - 3 * cols) // 2
    coefs = gath_ref[:, :, 3 * cols : 3 * cols + 2 * experts].reshape(total_rows, 2 * experts)
    coefs = coefs.astype(F32)
    clane = lax.broadcasted_iota(jnp.int32, (total_rows, 2 * experts), 1)
    inners = []
    for j in range(own_experts):
        mine = me * own_experts + j
        weight = jnp.sum(
            jnp.where((clane == mine) | (clane == mine + experts), coefs, 0.0), axis=-1, keepdims=True
        )
        gate = acc[0, j] + jnp.dot(xbuf[other], wg[other, j], preferred_element_type=F32)
        up = acc[1, j] + jnp.dot(xbuf[other], wu[other, j], preferred_element_type=F32)
        gate, up = gate * scale, up * scale
        inners.append((jax.nn.silu(gate) * up * weight).astype(BF16))

    for load in shared_in:
        load.wait()
    load_sd.wait()
    load_wd.wait()

    square = jnp.zeros((ROWS, HD), F32)
    srow = lax.broadcasted_iota(jnp.int32, (ROWS, ROWS), 1)
    spread = jnp.where((srow == count) | (srow == count + 1), 1.0, 0.0).astype(BF16)
    gate = jnp.zeros((ROWS, sg.shape[2]), F32)
    up = jnp.zeros((ROWS, sg.shape[2]), F32)
    for c in range(2):
        rows = xbuf[c, my_rows, :]
        gate += jnp.dot(rows, sg[c], preferred_element_type=F32)
        up += jnp.dot(rows, su[c], preferred_element_type=F32)
        for k in range(nz):
            square += jnp.dot(
                spread, rows[:, k * cols : k * cols + HD], preferred_element_type=F32
            )
    srow = lax.broadcasted_iota(jnp.int32, (ROWS, HD), 0)
    sl = lax.broadcasted_iota(jnp.int32, (ROWS, HD), 1)
    square = jnp.sum(jnp.where(srow == sl, square, 0.0), axis=-1, keepdims=True)
    sscale = lax.rsqrt(square / width + 1e-06)
    gate, up = gate * sscale, up * sscale
    inner = jnp.where(
        lax.broadcasted_iota(jnp.int32, gate.shape, 0) < count, jax.nn.silu(gate) * up, 0.0
    ).astype(BF16)
    for e in range(ne):
        shared[e] = jnp.dot(inner, sd[:, e * cols : (e + 1) * cols], preferred_element_type=F32)

    def down(e):
        where = pl.ds(pl.multiple_of(e * cols, cols), cols)
        value = jnp.zeros((total_rows, cols), F32)
        for j in range(own_experts):
            value += jnp.dot(inners[j], wd[j, :, where], preferred_element_type=F32)
        sums[...] = value
        sums[my_rows, :] += shared[e]

    pairs = []
    for k in range(nz):
        down(k * 2 + other)
        ybuf[other, k] = sums[...].astype(BF16)
        pair = pltpu.make_async_remote_copy(
            src_ref=ybuf.at[other, k], dst_ref=ypair.at[k],
            send_sem=psend.at[k], recv_sem=precv.at[k], device_id=peer(me, twin), device_id_type=MESH,
        )
        pair.start()
        pairs.append(pair)
    for i in range(nz):
        k = (z + 1 + i) % nz
        down(k * 2 + core)
        pltpu.make_async_remote_copy(
            src_ref=ybuf.at[other, k], dst_ref=ypair.at[k],
            send_sem=psend.at[k], recv_sem=precv.at[k], device_id=peer(me, twin), device_id_type=MESH,
        ).wait_recv()
        ybuf[core, k] = (sums[...] + ypair[k].astype(F32)).astype(BF16)

        def push5(n, _):
            to = (me + n) % ns
            there = pl.ds(pl.multiple_of(to * ROWS, ROWS), ROWS)
            pltpu.make_async_remote_copy(
                src_ref=ybuf.at[core, k, there, :], dst_ref=r5.at[back, :],
                send_sem=send5, recv_sem=recv5,
                device_id=peer(to, k * 2 + core), device_id_type=MESH,
            ).start()
            return 0

        lax.fori_loop(1 if i == nz - 1 else 0, ns, push5, 0)
    r5[back, :] = ybuf[core, z, my_rows, :]
    rest = pl.ds(0, (nz * ns - 1) * ROWS)
    all5 = pltpu.make_async_remote_copy(
        src_ref=r5.at[rest, :], dst_ref=r5.at[rest, :],
        send_sem=send5, recv_sem=recv5, device_id=peer(me, twin), device_id_type=MESH,
    )
    all5.wait_recv()
    result = residual
    for k in range(nz * ns):
        result += r5[k * ROWS : (k + 1) * ROWS, :].astype(F32)
    for b in range(requests):
        out_ref[b] = result[b * steps : (b + 1) * steps, :]

    all2.wait_send()
    all3.wait_send()
    all5.wait_send()
    pltpu.make_async_remote_copy(
        src_ref=r5.at[rest, :], dst_ref=r5.at[rest, :],
        send_sem=send4, recv_sem=recv4.at[0], device_id=peer(me, twin), device_id_type=MESH,
    ).wait_send()
    for i in range(nz):
        forwards[i].wait_send()
        pairs[i].wait_send()


def body(
    hidden_in, cache_lens, slot_request, slot_block, key_cache, value_cache, attn_gain,
    query_weight, key_weight, value_weight, out_weight, ffn_gain, expert_ids, expert_weights,
    gate_experts, up_experts, down_experts, gate_shared, up_shared, down_shared,
):
    requests, steps, width = hidden_in.shape
    ns = lax.axis_size("seq")
    ne = lax.axis_size("exp")
    nz = ne // 2
    cols = query_weight.shape[1]
    own_experts, _, fe = gate_experts.shape
    sf = gate_shared.shape[1]
    experts = own_experts * ns
    pool, block, _ = key_cache.shape
    heads = cols // HD
    hr = heads * steps
    total_rows = ns * ROWS

    exponent = jnp.arange(HD // 2, dtype=F32) * (2.0 / HD)
    frequency = jnp.power(F32(10000.0), -exponent)
    frequency = jnp.concatenate([frequency, frequency])[None, :]

    vmem = pl.BlockSpec(memory_space=pltpu.VMEM)
    smem = pl.BlockSpec(memory_space=pltpu.SMEM)
    anys = pl.BlockSpec(memory_space=pl.ANY)
    dma = pltpu.SemaphoreType.DMA

    gathered = pl.pallas_call(
        project_kernel,
        out_shape=jax.ShapeDtypeStruct((ns, ROWS, 3 * cols + 2 * experts), BF16),
        in_specs=[smem, vmem, vmem, vmem, vmem, vmem, anys, anys, anys],
        out_specs=vmem,
        scratch_shapes=[
            pltpu.VMEM((ROWS, width), F32),
            pltpu.VMEM((3, width, cols), BF16),
            pltpu.VMEM((ROWS, 2 * experts), F32),
            dma((3,)),
            dma,
            dma,
        ],
        compiler_params=pltpu.CompilerParams(collective_id=0, has_side_effects=True),
        name="project",
    )(
        cache_lens, frequency, hidden_in, attn_gain[None, :], expert_ids, expert_weights,
        query_weight, key_weight, value_weight,
    )

    group = 8
    groups = -(-pool // group)
    key_out, value_out, part = pl.pallas_call(
        functools.partial(attend_kernel, requests=requests, steps=steps, group=group),
        out_shape=(
            jax.ShapeDtypeStruct(key_cache.shape, BF16),
            jax.ShapeDtypeStruct(value_cache.shape, BF16),
            jax.ShapeDtypeStruct((ns, requests + 1, hr, HD), F32),
        ),
        in_specs=[smem, smem, smem, vmem, anys, anys],
        out_specs=(anys, anys, vmem),
        scratch_shapes=[
            pltpu.VMEM(key_cache.shape, BF16),
            pltpu.VMEM(key_cache.shape, BF16),
            pltpu.VMEM((ns * requests, hr, cols), BF16),
            pltpu.VMEM((ns * requests, steps, 2 * cols), F32),
            pltpu.VMEM((ns * requests, hr, HD), F32),
            pltpu.VMEM((ns * requests, hr, HD), F32),
            dma((2, groups)),
            dma((2, groups)),
        ],
        name="attend",
    )(slot_request, slot_block, cache_lens, gathered, key_cache, value_cache)

    hidden_out = pl.pallas_call(
        layer_kernel,
        out_shape=jax.ShapeDtypeStruct((requests, steps, cols), F32),
        in_specs=[vmem, vmem, vmem, vmem] + [anys] * 7,
        out_specs=vmem,
        scratch_shapes=[
            pltpu.VMEM((cols, width), BF16),
            pltpu.VMEM((2, own_experts, width // 2, fe), BF16),
            pltpu.VMEM((2, own_experts, width // 2, fe), BF16),
            pltpu.VMEM((own_experts, fe, width), BF16),
            pltpu.VMEM((2, width // 2, sf), BF16),
            pltpu.VMEM((2, width // 2, sf), BF16),
            pltpu.VMEM((sf, width), BF16),
            pltpu.VMEM((ns, requests + 1, hr, HD), F32),
            pltpu.VMEM((ROWS, width), F32),
            pltpu.VMEM((ne, ROWS, cols), F32),
            pltpu.VMEM((ne, ROWS, cols), F32),
            pltpu.VMEM((2, total_rows, nz * cols), BF16),
            pltpu.VMEM((2, own_experts, total_rows, fe), F32),
            pltpu.VMEM((2, nz, total_rows, cols), BF16),
            pltpu.VMEM((nz, total_rows, cols), BF16),
            pltpu.VMEM((total_rows, cols), F32),
            pltpu.VMEM((nz * total_rows, cols), BF16),
            pltpu.VMEM((ne, ROWS, cols), F32),
            dma((3 + 8 * nz,)),
            dma, dma, dma, dma, dma,
            dma((nz,)), dma((nz,)), dma((nz,)), dma((nz,)), dma((nz,)),
            dma, dma,
        ],
        compiler_params=pltpu.CompilerParams(collective_id=1, has_side_effects=True),
        name="layer",
    )(
        part, gathered, hidden_in, ffn_gain[None, :], out_weight, gate_experts, up_experts,
        down_experts, gate_shared, up_shared, down_shared,
    )
    return (hidden_out, key_out, value_out)


def solution(mesh):
    in_specs = (
        P("seq", None, None),
        P(),
        P("seq"),
        P("seq"),
        P("seq", None, "exp"),
        P("seq", None, "exp"),
        P(),
        P(None, "exp"),
        P(None, "exp"),
        P(None, "exp"),
        P("exp", None),
        P(),
        P("seq", None, None),
        P("seq", None, None),
        P("seq", None, "exp"),
        P("seq", None, "exp"),
        P("seq", "exp", None),
        P(None, "exp"),
        P(None, "exp"),
        P("exp", None),
    )
    out_specs = (P("seq", None, "exp"), P("seq", None, "exp"), P("seq", None, "exp"))
    return jax.shard_map(body, mesh=mesh, in_specs=in_specs, out_specs=out_specs, check_vma=False)
```

```python
import functools
import math

import jax
import jax.numpy as jnp
import numpy as np
from jax import lax
from jax.experimental import pallas as pl
from jax.experimental.pallas import tpu as pltpu
from jax.sharding import PartitionSpec as P

HD = 128
MESH = pl.DeviceIdType.MESH
F32 = jnp.float32
BF16 = jnp.bfloat16
ROWS = 16


def peer(seq, exp):
    return {"seq": seq, "exp": exp}


def rows_of(ref, scratch):
    count, steps, _ = ref.shape
    for b in range(count):
        scratch[pl.ds(b * steps, steps), :] = ref[b]
    used = count * steps
    scratch[pl.ds(used, ROWS - used), :] = jnp.zeros((ROWS - used, ref.shape[2]), F32)


def dot_t(a, b):
    return lax.dot_general(a, b, (((1,), (1,)), ((), ())), preferred_element_type=F32)


def split_two(values):
    high = values.astype(BF16)
    low = (values - high.astype(F32)).astype(BF16)
    return high, low


def project_kernel(
    lens_ref, freq_ref, hidden_ref, gain_ref, ids_ref, ew_ref, wq_ref, wk_ref, wv_ref,
    out_ref, xs, wbuf, coef, wsem, send_sem, recv_sem,
):
    ns = lax.axis_size("seq")
    me = lax.axis_index("seq")
    exp = lax.axis_index("exp")
    requests, steps, width = hidden_ref.shape
    cols = wq_ref.shape[1]
    experts = coef.shape[1] // 2

    barrier = pltpu.get_barrier_semaphore()

    def greet(i, _):
        pl.semaphore_signal(barrier, inc=1, device_id=peer((me + i) % ns, exp), device_id_type=MESH)
        return 0

    lax.fori_loop(1, ns, greet, 0)
    loads = []
    for k, w in enumerate((wq_ref, wk_ref, wv_ref)):
        load = pltpu.make_async_copy(w, wbuf.at[k], wsem.at[k])
        load.start()
        loads.append(load)

    rows_of(hidden_ref, xs)
    x = xs[...]
    mean_square = jnp.mean(x * x, axis=-1, keepdims=True)
    normed = (x * lax.rsqrt(mean_square + 1e-06) * gain_ref[...]).astype(BF16)

    row = lax.broadcasted_iota(jnp.int32, (ROWS, HD), 0)
    lane = lax.broadcasted_iota(jnp.int32, (ROWS, HD), 1)
    length = jnp.zeros((ROWS, HD), jnp.int32)
    for b in range(requests):
        length = jnp.where(row // steps == b, lens_ref[me * requests + b], length)
    position = (length + row % steps).astype(F32)
    angles = position * freq_ref[...]
    cosine = jnp.cos(angles)
    sine = jnp.where(lane < HD // 2, -jnp.sin(angles), jnp.sin(angles))

    def rotate(v):
        parts = []
        for h in range(cols // HD):
            head = v[:, h * HD : (h + 1) * HD]
            parts.append(head * cosine + pltpu.roll(head, HD // 2, 1) * sine)
        return jnp.concatenate(parts, axis=1)

    coef[...] = jnp.zeros(coef.shape, F32)
    expert = lax.broadcasted_iota(jnp.int32, (steps, experts), 1)
    for b in range(requests):
        total = jnp.zeros((steps, experts), F32)
        for j in range(ids_ref.shape[2]):
            total += jnp.where(ids_ref[b][:, j : j + 1] == expert, ew_ref[b][:, j : j + 1], 0.0)
        coef[pl.ds(b * steps, steps), pl.ds(0, experts)] = total
    high, low = split_two(coef[:, 0:experts])

    for k in range(3):
        loads[k].wait()
        product = jnp.dot(normed, wbuf[k], preferred_element_type=F32)
        if k < 2:
            product = rotate(product)
        out_ref[me, :, k * cols : (k + 1) * cols] = product.astype(BF16)
    out_ref[me, :, 3 * cols : 3 * cols + 2 * experts] = jnp.concatenate([high, low], axis=1)

    pl.semaphore_wait(barrier, ns - 1)

    def push(i, _):
        pltpu.make_async_remote_copy(
            src_ref=out_ref.at[me],
            dst_ref=out_ref.at[me],
            send_sem=send_sem,
            recv_sem=recv_sem,
            device_id=peer((me + i) % ns, exp),
            device_id_type=MESH,
        ).start()
        return 0

    lax.fori_loop(1, ns, push, 0)
    everything = pltpu.make_async_remote_copy(
        src_ref=out_ref.at[pl.ds(0, ns - 1)],
        dst_ref=out_ref.at[pl.ds(0, ns - 1)],
        send_sem=send_sem,
        recv_sem=recv_sem,
        device_id=peer((me + 1) % ns, exp),
        device_id_type=MESH,
    )
    everything.wait_recv()
    everything.wait_send()


def attend_kernel(
    req_ref, blk_ref, lens_ref, gath_ref, key_ref, value_ref,
    key_out, value_out, part_ref, kbuf, vbuf, qbd, newkv, acc_m, acc_l, in_sem, out_sem,
    *, requests, steps, group,
):
    pool, block, cols = key_ref.shape
    ns = gath_ref.shape[0]
    heads = cols // HD
    hr = heads * steps
    starts = list(range(0, pool, group))
    sizes = [min(group, pool - s) for s in starts]

    def copies(g, into):
        span = pl.ds(starts[g], sizes[g])
        pairs = ((key_ref, kbuf, key_out), (value_ref, vbuf, value_out))
        result = []
        for n, (source, buf, target) in enumerate(pairs):
            if into:
                result.append(pltpu.make_async_copy(source.at[span], buf.at[span], in_sem.at[n, g]))
            else:
                result.append(pltpu.make_async_copy(buf.at[span], target.at[span], out_sem.at[n, g]))
        return result

    for g in range(len(starts)):
        for c in copies(g, True):
            c.start()

    qlane = lax.broadcasted_iota(jnp.int32, (hr, cols), 1) // HD
    qrow = lax.broadcasted_iota(jnp.int32, (hr, cols), 0) // steps
    for s in range(ns):
        q = gath_ref[s, :, 0:cols].astype(F32)
        kv = gath_ref[s, :, cols : 3 * cols].astype(F32)
        for b in range(requests):
            part = q[b * steps : (b + 1) * steps, :]
            both = jnp.concatenate([part] * heads, axis=0)
            qbd[s * requests + b] = jnp.where(qlane == qrow, both, 0.0).astype(BF16)
            newkv[s * requests + b] = kv[b * steps : (b + 1) * steps, :]

    acc_m[...] = jnp.full(acc_m.shape, -1e30, F32)
    acc_l[...] = jnp.zeros(acc_l.shape, F32)
    part_ref[...] = jnp.zeros(part_ref.shape, F32)

    scale = 1.0 / math.sqrt(HD)
    lane = lax.broadcasted_iota(jnp.int32, (hr, block), 1)
    step = lax.broadcasted_iota(jnp.int32, (hr, block), 0) % steps
    upper = lax.broadcasted_iota(jnp.int32, (hr, HD), 0) // steps
    window = 2 * ROWS
    wrow = lax.broadcasted_iota(jnp.int32, (window, cols), 0)

    for g in range(len(starts)):
        for c in copies(g, True):
            c.wait()

        def patch(i, _):
            s = starts[g] + i
            request = jnp.maximum(req_ref[s], 0)
            offset = lens_ref[request] - blk_ref[s] * block

            @pl.when((req_ref[s] >= 0) & (offset > -steps) & (offset < block))
            def _():
                first = jnp.clip(offset // ROWS * ROWS, 0, block - window)
                first = pl.multiple_of(first, ROWS)
                rel = wrow + first - offset
                for n, buf in enumerate((kbuf, vbuf)):
                    tile = buf[s, pl.ds(first, window), :].astype(F32)
                    for t in range(steps):
                        fresh = newkv[request, t : t + 1, n * cols : (n + 1) * cols]
                        tile = jnp.where(rel == t, fresh, tile)
                    buf[s, pl.ds(first, window), :] = tile.astype(BF16)

            return 0

        lax.fori_loop(0, sizes[g], patch, 0)
        for c in copies(g, False):
            c.start()

        for i in range(sizes[g]):
            s = starts[g] + i
            request = jnp.maximum(req_ref[s], 0)
            offset = lens_ref[request] - blk_ref[s] * block
            limit = jnp.where(req_ref[s] >= 0, offset, -(2 * block))
            allowed = lane - step <= limit
            scores = (
                lax.dot_general(
                    qbd[request], kbuf[s], (((1,), (1,)), ((), ())), preferred_element_type=F32
                )
                * scale
            )
            top = jnp.max(jnp.where(allowed, scores, -1e30), axis=-1, keepdims=True)
            safe = jnp.where(top > -1e29, top, 0.0)
            weights = jnp.where(allowed, jnp.exp(scores - safe), 0.0)
            total = jnp.sum(weights, axis=-1, keepdims=True)
            full = jnp.dot(weights.astype(BF16), vbuf[s], preferred_element_type=F32)
            out = full[:, 0:HD]
            for h in range(1, heads):
                out = jnp.where(upper == h, full[:, h * HD : (h + 1) * HD], out)
            owner, which = request // requests, request % requests
            old_m = acc_m[request]
            joint = jnp.maximum(old_m, top)
            old_scale = jnp.exp(old_m - joint)
            new_scale = jnp.exp(top - joint)
            acc_m[request] = joint
            acc_l[request] = acc_l[request] * old_scale + total * new_scale
            part_ref[owner, which] = part_ref[owner, which] * old_scale + out * new_scale

    slane = lax.broadcasted_iota(jnp.int32, (hr, HD), 1)
    for s in range(ns):
        stats = jnp.full((hr, HD), 0.0, F32)
        for b in range(requests):
            stats = jnp.where(slane == b, acc_m[s * requests + b], stats)
            stats = jnp.where(slane == HD // 2 + b, acc_l[s * requests + b], stats)
        part_ref[s, requests] = stats

    for g in range(len(starts)):
        for c in copies(g, False):
            c.wait()


def layer_kernel(
    part_ref, gath_ref, hidden_ref, fgain_ref, wo_ref, ge_ref, ue_ref, de_ref, gs_ref, us_ref, ds_ref,
    out_ref,
    wo, wg, wu, wd, sg, su, sd, rbuf, xs, terms, r3, xbuf, acc, ybuf, ypair, sums, r5, shared,
    wsem, send2, recv2, send3, recv3, send4, recv4, fsend, frecv, psend, precv, send5, recv5,
):
    ns = lax.axis_size("seq")
    ne = lax.axis_size("exp")
    nz = ne // 2
    me = lax.axis_index("seq")
    exp = lax.axis_index("exp")
    z, core = exp // 2, exp % 2
    other = 1 - core
    twin = z * 2 + other
    requests, steps, width = hidden_ref.shape
    hr = part_ref.shape[2]
    cols = out_ref.shape[2]
    own_experts = ge_ref.shape[0]
    count = requests * steps
    total_rows = ns * ROWS

    barrier = pltpu.get_barrier_semaphore()

    def greet_seq(i, _):
        pl.semaphore_signal(barrier, inc=1, device_id=peer((me + i) % ns, exp), device_id_type=MESH)
        return 0

    def greet_exp(i, _):
        pl.semaphore_signal(barrier, inc=1, device_id=peer(me, (exp + i) % ne), device_id_type=MESH)
        return 0

    lax.fori_loop(1, ns, greet_seq, 0)
    lax.fori_loop(1, ne, greet_exp, 0)

    load_wo = pltpu.make_async_copy(wo_ref, wo, wsem.at[0])
    load_wo.start()
    gate_up, shared_in = [], []
    for n, (source, buf) in enumerate(((ge_ref, wg), (ue_ref, wu))):
        for c in range(2):
            for k in range(nz):
                load = pltpu.make_async_copy(
                    source.at[:, :, pl.ds((k * 2 + c) * cols, cols)],
                    buf.at[c, :, :, pl.ds(k * cols, cols)],
                    wsem.at[1 + (n * 2 + c) * nz + k],
                )
                load.start()
                gate_up.append(load)
    base = 1 + 4 * nz
    load_wd = pltpu.make_async_copy(de_ref, wd, wsem.at[base])
    load_wd.start()
    for n, (source, buf) in enumerate(((gs_ref, sg), (us_ref, su))):
        for c in range(2):
            for k in range(nz):
                load = pltpu.make_async_copy(
                    source.at[:, pl.ds((k * 2 + c) * cols, cols)],
                    buf.at[c, :, pl.ds(k * cols, cols)],
                    wsem.at[base + 1 + (n * 2 + c) * nz + k],
                )
                load.start()
                shared_in.append(load)
    load_sd = pltpu.make_async_copy(ds_ref, sd, wsem.at[base + 1 + 4 * nz])
    load_sd.start()

    rows_of(hidden_ref, xs)
    rbuf[me] = part_ref[me]
    pl.semaphore_wait(barrier, ns - 1 + ne - 1)

    def push2(i, _):
        to = (me + i) % ns
        pltpu.make_async_remote_copy(
            src_ref=part_ref.at[to], dst_ref=rbuf.at[me], send_sem=send2, recv_sem=recv2,
            device_id=peer(to, exp), device_id_type=MESH,
        ).start()
        return 0

    lax.fori_loop(1, ns, push2, 0)
    all2 = pltpu.make_async_remote_copy(
        src_ref=part_ref.at[pl.ds(0, ns - 1)], dst_ref=rbuf.at[pl.ds(0, ns - 1)],
        send_sem=send2, recv_sem=recv2, device_id=peer((me + 1) % ns, exp), device_id_type=MESH,
    )
    all2.wait_recv()

    top = rbuf[0, requests]
    for s in range(1, ns):
        top = jnp.maximum(top, rbuf[s, requests])
    slane = lax.broadcasted_iota(jnp.int32, (hr, HD), 1)
    factors, total = [], jnp.zeros((hr, HD), F32)
    for s in range(ns):
        stats = rbuf[s, requests]
        factor = jnp.exp(jnp.where(slane < requests, stats - top, 0.0))
        factors.append(factor)
        total += pltpu.roll(stats, HD // 2, 1) * factor
    attended = []
    for b in range(requests):
        summed = jnp.zeros((hr, HD), F32)
        for s in range(ns):
            summed += rbuf[s, b] * factors[s][:, b : b + 1]
        attended.append(summed / total[:, b : b + 1])
    stacked = jnp.concatenate(attended, axis=0).astype(BF16)
    prow = lax.broadcasted_iota(jnp.int32, (ROWS, requests * hr), 0)
    pcol = lax.broadcasted_iota(jnp.int32, (ROWS, requests * hr), 1)
    by_head = []
    for h in range(cols // HD):
        pick = (pcol == prow // steps * hr + h * steps + prow % steps) & (prow < count)
        by_head.append(
            jnp.dot(
                jnp.where(pick, 1.0, 0.0).astype(BF16), stacked, preferred_element_type=F32
            ).astype(BF16)
        )
    own = jnp.concatenate(by_head, axis=1)
    load_wo.wait()
    for e in range(ne):
        terms[e] = jnp.dot(own, wo[:, e * cols : (e + 1) * cols], preferred_element_type=F32)

    def push3(i, _):
        to = (exp + i) % ne
        pltpu.make_async_remote_copy(
            src_ref=terms.at[to], dst_ref=r3.at[exp], send_sem=send3, recv_sem=recv3,
            device_id=peer(me, to), device_id_type=MESH,
        ).start()
        return 0

    lax.fori_loop(1, ne, push3, 0)
    r3[exp] = terms[exp]
    all3 = pltpu.make_async_remote_copy(
        src_ref=terms.at[pl.ds(0, ne - 1)], dst_ref=r3.at[pl.ds(0, ne - 1)],
        send_sem=send3, recv_sem=recv3, device_id=peer(me, (exp + 1) % ne), device_id_type=MESH,
    )
    all3.wait_recv()
    residual = xs[:, pl.ds(pl.multiple_of(exp * cols, cols), cols)]
    for e in range(ne):
        residual += r3[e]

    scaled = residual * fgain_ref[:, pl.ds(pl.multiple_of(exp * cols, cols), cols)]
    square = jnp.sum(residual * residual, axis=-1, keepdims=True)
    brow = lax.broadcasted_iota(jnp.int32, (ROWS, cols), 0)
    blane = lax.broadcasted_iota(jnp.int32, (ROWS, cols), 1)
    line = jnp.sum(jnp.where(brow == blane, square, 0.0), axis=0, keepdims=True)
    high, low = split_two(line)
    scaled = jnp.where(brow == count, high.astype(F32), scaled)
    scaled = jnp.where(brow == count + 1, low.astype(F32), scaled)
    my_rows = pl.ds(pl.multiple_of(me * ROWS, ROWS), ROWS)
    my_cols = pl.ds(pl.multiple_of(z * cols, cols), cols)
    back = pl.ds(pl.multiple_of((z * ns + me) * ROWS, ROWS), ROWS)
    xbuf[core, my_rows, my_cols] = scaled.astype(BF16)

    def push4(i, _):
        to = (z * ns + me + i) % (nz * ns)
        pltpu.make_async_remote_copy(
            src_ref=xbuf.at[core, my_rows, my_cols], dst_ref=xbuf.at[core, my_rows, my_cols],
            send_sem=send4, recv_sem=recv4.at[z],
            device_id=peer(to % ns, to // ns * 2 + core), device_id_type=MESH,
        ).start()
        return 0

    lax.fori_loop(1, nz * ns, push4, 0)
    forwards = []
    for i in range(nz):
        k = (z + i) % nz
        span = pl.ds(0, total_rows - (ROWS if i == 0 else 0))
        kcols = pl.ds(pl.multiple_of(k * cols, cols), cols)
        pltpu.make_async_remote_copy(
            src_ref=xbuf.at[core, span, kcols], dst_ref=xbuf.at[core, span, kcols],
            send_sem=send4, recv_sem=recv4.at[k], device_id=peer(me, twin), device_id_type=MESH,
        ).wait_recv()
        forward = pltpu.make_async_remote_copy(
            src_ref=xbuf.at[core, :, kcols], dst_ref=xbuf.at[core, :, kcols],
            send_sem=fsend.at[k], recv_sem=frecv.at[k], device_id=peer(me, twin), device_id_type=MESH,
        )
        forward.start()
        forwards.append(forward)

    for load in gate_up:
        load.wait()
    for j in range(own_experts):
        acc[0, j] = dot_t(xbuf[core], wg[core, j])
        acc[1, j] = dot_t(xbuf[core], wu[core, j])
    for i in range(nz):
        k = (z + i) % nz
        kcols = pl.ds(pl.multiple_of(k * cols, cols), cols)
        pltpu.make_async_remote_copy(
            src_ref=xbuf.at[other, :, kcols], dst_ref=xbuf.at[other, :, kcols],
            send_sem=fsend.at[k], recv_sem=frecv.at[k], device_id=peer(me, twin), device_id_type=MESH,
        ).wait_recv()

    trow = lax.broadcasted_iota(jnp.int32, (total_rows, total_rows), 0)
    tcol = lax.broadcasted_iota(jnp.int32, (total_rows, total_rows), 1)
    spread = (trow // ROWS == tcol // ROWS) & ((tcol % ROWS == count) | (tcol % ROWS == count + 1))
    spread = jnp.where(spread, 1.0, 0.0).astype(BF16)
    square = jnp.zeros((total_rows, HD), F32)
    for c in range(2):
        for k in range(nz):
            square += jnp.dot(
                spread, xbuf[c, :, k * cols : k * cols + HD], preferred_element_type=F32
            )
    lrow = lax.broadcasted_iota(jnp.int32, (total_rows, HD), 0)
    llane = lax.broadcasted_iota(jnp.int32, (total_rows, HD), 1)
    square = jnp.sum(
        jnp.where(lrow % ROWS == llane, square, 0.0), axis=-1, keepdims=True
    )
    scale = lax.rsqrt(square / width + 1e-06)

    experts = (gath_ref.shape[2] - 3 * cols) // 2
    coefs = gath_ref[:, :, 3 * cols : 3 * cols + 2 * experts].reshape(total_rows, 2 * experts)
    coefs = coefs.astype(F32)
    clane = lax.broadcasted_iota(jnp.int32, (total_rows, 2 * experts), 1)
    inners = []
    for j in range(own_experts):
        mine = me * own_experts + j
        weight = jnp.sum(
            jnp.where((clane == mine) | (clane == mine + experts), coefs, 0.0), axis=-1, keepdims=True
        )
        gate = acc[0, j] + dot_t(xbuf[other], wg[other, j])
        up = acc[1, j] + dot_t(xbuf[other], wu[other, j])
        gate, up = gate * scale, up * scale
        inners.append((jax.nn.silu(gate) * up * weight).astype(BF16))

    for load in shared_in:
        load.wait()
    load_sd.wait()
    load_wd.wait()

    square = jnp.zeros((ROWS, HD), F32)
    srow = lax.broadcasted_iota(jnp.int32, (ROWS, ROWS), 1)
    spread = jnp.where((srow == count) | (srow == count + 1), 1.0, 0.0).astype(BF16)
    gate = jnp.zeros((ROWS, sg.shape[1]), F32)
    up = jnp.zeros((ROWS, sg.shape[1]), F32)
    for c in range(2):
        rows = xbuf[c, my_rows, :]
        gate += dot_t(rows, sg[c])
        up += dot_t(rows, su[c])
        for k in range(nz):
            square += jnp.dot(
                spread, rows[:, k * cols : k * cols + HD], preferred_element_type=F32
            )
    srow = lax.broadcasted_iota(jnp.int32, (ROWS, HD), 0)
    sl = lax.broadcasted_iota(jnp.int32, (ROWS, HD), 1)
    square = jnp.sum(jnp.where(srow == sl, square, 0.0), axis=-1, keepdims=True)
    sscale = lax.rsqrt(square / width + 1e-06)
    gate, up = gate * sscale, up * sscale
    inner = jnp.where(
        lax.broadcasted_iota(jnp.int32, gate.shape, 0) < count, jax.nn.silu(gate) * up, 0.0
    ).astype(BF16)
    for e in range(ne):
        shared[e] = jnp.dot(inner, sd[:, e * cols : (e + 1) * cols], preferred_element_type=F32)

    def down(e):
        where = pl.ds(pl.multiple_of(e * cols, cols), cols)
        value = jnp.zeros((total_rows, cols), F32)
        for j in range(own_experts):
            value += jnp.dot(inners[j], wd[j, :, where], preferred_element_type=F32)
        sums[...] = value
        sums[my_rows, :] += shared[e]

    pairs = []
    for k in range(nz):
        down(k * 2 + other)
        ybuf[other, k] = sums[...].astype(BF16)
        pair = pltpu.make_async_remote_copy(
            src_ref=ybuf.at[other, k], dst_ref=ypair.at[k],
            send_sem=psend.at[k], recv_sem=precv.at[k], device_id=peer(me, twin), device_id_type=MESH,
        )
        pair.start()
        pairs.append(pair)
    for i in range(nz):
        k = (z + 1 + i) % nz
        down(k * 2 + core)
        pltpu.make_async_remote_copy(
            src_ref=ybuf.at[other, k], dst_ref=ypair.at[k],
            send_sem=psend.at[k], recv_sem=precv.at[k], device_id=peer(me, twin), device_id_type=MESH,
        ).wait_recv()
        ybuf[core, k] = (sums[...] + ypair[k].astype(F32)).astype(BF16)

        def push5(n, _):
            to = (me + n) % ns
            there = pl.ds(pl.multiple_of(to * ROWS, ROWS), ROWS)
            pltpu.make_async_remote_copy(
                src_ref=ybuf.at[core, k, there, :], dst_ref=r5.at[back, :],
                send_sem=send5, recv_sem=recv5,
                device_id=peer(to, k * 2 + core), device_id_type=MESH,
            ).start()
            return 0

        lax.fori_loop(1 if i == nz - 1 else 0, ns, push5, 0)
    r5[back, :] = ybuf[core, z, my_rows, :]
    rest = pl.ds(0, (nz * ns - 1) * ROWS)
    all5 = pltpu.make_async_remote_copy(
        src_ref=r5.at[rest, :], dst_ref=r5.at[rest, :],
        send_sem=send5, recv_sem=recv5, device_id=peer(me, twin), device_id_type=MESH,
    )
    all5.wait_recv()
    result = residual
    for k in range(nz * ns):
        result += r5[k * ROWS : (k + 1) * ROWS, :].astype(F32)
    for b in range(requests):
        out_ref[b] = result[b * steps : (b + 1) * steps, :]

    all2.wait_send()
    all3.wait_send()
    all5.wait_send()
    pltpu.make_async_remote_copy(
        src_ref=r5.at[rest, :], dst_ref=r5.at[rest, :],
        send_sem=send4, recv_sem=recv4.at[0], device_id=peer(me, twin), device_id_type=MESH,
    ).wait_send()
    for i in range(nz):
        forwards[i].wait_send()
        pairs[i].wait_send()


def body(
    hidden_in, cache_lens, slot_request, slot_block, key_cache, value_cache, attn_gain,
    query_weight, key_weight, value_weight, out_weight, ffn_gain, expert_ids, expert_weights,
    gate_experts, up_experts, down_experts, gate_shared, up_shared, down_shared,
):
    requests, steps, width = hidden_in.shape
    ns = lax.axis_size("seq")
    ne = lax.axis_size("exp")
    nz = ne // 2
    cols = query_weight.shape[1]
    own_experts, _, fe = gate_experts.shape
    sf = gate_shared.shape[1]
    experts = own_experts * ns
    pool, block, _ = key_cache.shape
    heads = cols // HD
    hr = heads * steps
    total_rows = ns * ROWS

    exponent = jnp.arange(HD // 2, dtype=F32) * (2.0 / HD)
    frequency = jnp.power(F32(10000.0), -exponent)
    frequency = jnp.concatenate([frequency, frequency])[None, :]

    vmem = pl.BlockSpec(memory_space=pltpu.VMEM)
    smem = pl.BlockSpec(memory_space=pltpu.SMEM)
    anys = pl.BlockSpec(memory_space=pl.ANY)
    dma = pltpu.SemaphoreType.DMA

    gathered = pl.pallas_call(
        project_kernel,
        out_shape=jax.ShapeDtypeStruct((ns, ROWS, 3 * cols + 2 * experts), BF16),
        in_specs=[smem, vmem, vmem, vmem, vmem, vmem, anys, anys, anys],
        out_specs=vmem,
        scratch_shapes=[
            pltpu.VMEM((ROWS, width), F32),
            pltpu.VMEM((3, width, cols), BF16),
            pltpu.VMEM((ROWS, 2 * experts), F32),
            dma((3,)),
            dma,
            dma,
        ],
        compiler_params=pltpu.CompilerParams(collective_id=0, has_side_effects=True),
        name="project",
    )(
        cache_lens, frequency, hidden_in, attn_gain[None, :], expert_ids, expert_weights,
        query_weight, key_weight, value_weight,
    )

    group = 8
    groups = -(-pool // group)
    key_out, value_out, part = pl.pallas_call(
        functools.partial(attend_kernel, requests=requests, steps=steps, group=group),
        out_shape=(
            jax.ShapeDtypeStruct(key_cache.shape, BF16),
            jax.ShapeDtypeStruct(value_cache.shape, BF16),
            jax.ShapeDtypeStruct((ns, requests + 1, hr, HD), F32),
        ),
        in_specs=[smem, smem, smem, vmem, anys, anys],
        out_specs=(anys, anys, vmem),
        scratch_shapes=[
            pltpu.VMEM(key_cache.shape, BF16),
            pltpu.VMEM(key_cache.shape, BF16),
            pltpu.VMEM((ns * requests, hr, cols), BF16),
            pltpu.VMEM((ns * requests, steps, 2 * cols), F32),
            pltpu.VMEM((ns * requests, hr, HD), F32),
            pltpu.VMEM((ns * requests, hr, HD), F32),
            dma((2, groups)),
            dma((2, groups)),
        ],
        name="attend",
    )(slot_request, slot_block, cache_lens, gathered, key_cache, value_cache)

    hidden_out = pl.pallas_call(
        layer_kernel,
        out_shape=jax.ShapeDtypeStruct((requests, steps, cols), F32),
        in_specs=[vmem, vmem, vmem, vmem] + [anys] * 7,
        out_specs=vmem,
        scratch_shapes=[
            pltpu.VMEM((cols, width), BF16),
            pltpu.VMEM((2, own_experts, fe, width // 2), BF16),
            pltpu.VMEM((2, own_experts, fe, width // 2), BF16),
            pltpu.VMEM((own_experts, fe, width), BF16),
            pltpu.VMEM((2, sf, width // 2), BF16),
            pltpu.VMEM((2, sf, width // 2), BF16),
            pltpu.VMEM((sf, width), BF16),
            pltpu.VMEM((ns, requests + 1, hr, HD), F32),
            pltpu.VMEM((ROWS, width), F32),
            pltpu.VMEM((ne, ROWS, cols), F32),
            pltpu.VMEM((ne, ROWS, cols), F32),
            pltpu.VMEM((2, total_rows, nz * cols), BF16),
            pltpu.VMEM((2, own_experts, total_rows, fe), F32),
            pltpu.VMEM((2, nz, total_rows, cols), BF16),
            pltpu.VMEM((nz, total_rows, cols), BF16),
            pltpu.VMEM((total_rows, cols), F32),
            pltpu.VMEM((nz * total_rows, cols), BF16),
            pltpu.VMEM((ne, ROWS, cols), F32),
            dma((3 + 8 * nz,)),
            dma, dma, dma, dma, dma,
            dma((nz,)), dma((nz,)), dma((nz,)), dma((nz,)), dma((nz,)),
            dma, dma,
        ],
        compiler_params=pltpu.CompilerParams(collective_id=1, has_side_effects=True),
        name="layer",
    )(
        part, gathered, hidden_in, ffn_gain[None, :], out_weight,
        jnp.swapaxes(gate_experts, 1, 2), jnp.swapaxes(up_experts, 1, 2), down_experts,
        gate_shared.T, up_shared.T, down_shared,
    )
    return (hidden_out, key_out, value_out)


def solution(mesh):
    in_specs = (
        P("seq", None, None),
        P(),
        P("seq"),
        P("seq"),
        P("seq", None, "exp"),
        P("seq", None, "exp"),
        P(),
        P(None, "exp"),
        P(None, "exp"),
        P(None, "exp"),
        P("exp", None),
        P(),
        P("seq", None, None),
        P("seq", None, None),
        P("seq", None, "exp"),
        P("seq", None, "exp"),
        P("seq", "exp", None),
        P(None, "exp"),
        P(None, "exp"),
        P("exp", None),
    )
    out_specs = (P("seq", None, "exp"), P("seq", None, "exp"), P("seq", None, "exp"))
    return jax.shard_map(body, mesh=mesh, in_specs=in_specs, out_specs=out_specs, check_vma=False)
```

```python
import functools
import math

import jax
import jax.numpy as jnp
import numpy as np
from jax import lax
from jax.experimental import pallas as pl
from jax.experimental.pallas import tpu as pltpu
from jax.sharding import PartitionSpec as P

HD = 128
MESH = pl.DeviceIdType.MESH
F32 = jnp.float32
BF16 = jnp.bfloat16
ROWS = 16


def peer(seq, exp):
    return {"seq": seq, "exp": exp}


def rows_of(ref, scratch):
    count, steps, _ = ref.shape
    for b in range(count):
        scratch[pl.ds(b * steps, steps), :] = ref[b]
    used = count * steps
    scratch[pl.ds(used, ROWS - used), :] = jnp.zeros((ROWS - used, ref.shape[2]), F32)


def dot_t(a, b):
    return lax.dot_general(a, b, (((1,), (1,)), ((), ())), preferred_element_type=F32)


def split_two(values):
    high = values.astype(BF16)
    low = (values - high.astype(F32)).astype(BF16)
    return high, low


def layer_kernel(
    lens_ref, req_ref, blk_ref, freq_ref, hidden_ref, again_ref, ids_ref, ew_ref, fgain_ref,
    wq_ref, wk_ref, wv_ref, key_ref, value_ref,
    wo_ref, ge_ref, ue_ref, de_ref, gs_ref, us_ref, ds_ref,
    out_ref, kv_ref,
    wbuf, qbuf, cbuf, coef, kbuf, vbuf, pick, gatherer, slots, part, found,
    wo, wg, wu, wd, sg, su, sd, rbuf, xs, terms, r3, xbuf, acc, ybuf, ypair, sums, r5, shared,
    asem, csem, qsend, qrecv, kvsend, kvrecv, cosend, corecv,
    wsem, send2, recv2, send3, recv3, send4, recv4, fsend, frecv, psend, precv, send5, recv5,
):
    ns = lax.axis_size("seq")
    ne = lax.axis_size("exp")
    nz = ne // 2
    me = lax.axis_index("seq")
    exp = lax.axis_index("exp")
    z, core = exp // 2, exp % 2
    other = 1 - core
    twin = z * 2 + other
    requests, steps, width = hidden_ref.shape
    cols = wq_ref.shape[1]
    heads = cols // HD
    hr = heads * steps
    pool, block, _ = key_ref.shape
    own_experts = ge_ref.shape[0]
    experts = coef.shape[1] // 2
    count = requests * steps
    total_rows = ns * ROWS

    barrier = pltpu.get_barrier_semaphore()

    def greet_seq(i, _):
        pl.semaphore_signal(barrier, inc=1, device_id=peer((me + i) % ns, exp), device_id_type=MESH)
        return 0

    def greet_exp(i, _):
        pl.semaphore_signal(barrier, inc=1, device_id=peer(me, (exp + i) % ne), device_id_type=MESH)
        return 0

    lax.fori_loop(1, ns, greet_seq, 0)
    lax.fori_loop(1, ne, greet_exp, 0)
    loads = []
    for k, w in enumerate((wq_ref, wk_ref, wv_ref)):
        load = pltpu.make_async_copy(w, wbuf.at[k], asem.at[k])
        load.start()
        loads.append(load)
    pieces = []
    chunk = -(-pool // 4)
    for g in range(4):
        span = pl.ds(g * chunk, min(chunk, pool - g * chunk))
        for n, (source, buf) in enumerate(((key_ref, kbuf), (value_ref, vbuf))):
            load = pltpu.make_async_copy(source.at[span], buf.at[span], csem.at[n, g])
            load.start()
            pieces.append(load)

    rows_of(hidden_ref, xs)
    x = xs[...]
    mean_square = jnp.mean(x * x, axis=-1, keepdims=True)
    normed = (x * lax.rsqrt(mean_square + 1e-06) * again_ref[...]).astype(BF16)
    row = lax.broadcasted_iota(jnp.int32, (ROWS, HD), 0)
    lane = lax.broadcasted_iota(jnp.int32, (ROWS, HD), 1)
    length = jnp.zeros((ROWS, HD), jnp.int32)
    for b in range(requests):
        length = jnp.where(row // steps == b, lens_ref[me * requests + b], length)
    position = (length + row % steps).astype(F32)
    angles = position * freq_ref[...]
    cosine = jnp.cos(angles)
    sine = jnp.sin(angles)
    sine = jnp.where(lane < HD // 2, -sine, sine)

    def rotate(v):
        parts = []
        for h in range(heads):
            one = v[:, h * HD : (h + 1) * HD]
            parts.append(one * cosine + pltpu.roll(one, HD // 2, 1) * sine)
        return jnp.concatenate(parts, axis=1)

    def push(src, dst, send, recv):
        def one(i, _):
            pltpu.make_async_remote_copy(
                src_ref=src, dst_ref=dst, send_sem=send, recv_sem=recv,
                device_id=peer((me + i) % ns, exp), device_id_type=MESH,
            ).start()
            return 0

        lax.fori_loop(1, ns, one, 0)

    def whole(ref, send, recv):
        return pltpu.make_async_remote_copy(
            src_ref=ref.at[pl.ds(0, ns - 1)], dst_ref=ref.at[pl.ds(0, ns - 1)],
            send_sem=send, recv_sem=recv,
            device_id=peer((me + 1) % ns, exp), device_id_type=MESH,
        )

    my_rows = pl.ds(pl.multiple_of(me * ROWS, ROWS), ROWS)
    loads[0].wait()
    own_q = rotate(jnp.dot(normed, wbuf[0], preferred_element_type=F32)).astype(BF16)
    qbuf[me] = own_q
    pl.semaphore_wait(barrier, ns - 1 + ne - 1)
    push(qbuf.at[me], qbuf.at[me], qsend, qrecv)
    loads[1].wait()
    own_k = rotate(jnp.dot(normed, wbuf[1], preferred_element_type=F32)).astype(BF16)
    kv_ref[me, :, 0:cols] = own_k
    loads[2].wait()
    own_v = jnp.dot(normed, wbuf[2], preferred_element_type=F32).astype(BF16)
    kv_ref[me, :, cols : 2 * cols] = own_v

    load_wo = pltpu.make_async_copy(wo_ref, wo, wsem.at[0])
    load_wo.start()
    gate_up, shared_in = [], []
    for n, (source, buf) in enumerate(((ge_ref, wg), (ue_ref, wu))):
        for c in range(2):
            for k in range(nz):
                load = pltpu.make_async_copy(
                    source.at[:, :, pl.ds((k * 2 + c) * cols, cols)],
                    buf.at[c, :, :, pl.ds(k * cols, cols)],
                    wsem.at[1 + (n * 2 + c) * nz + k],
                )
                load.start()
                gate_up.append(load)
    base = 1 + 4 * nz
    load_wd = pltpu.make_async_copy(de_ref, wd, wsem.at[base])
    load_wd.start()
    for n, (source, buf) in enumerate(((gs_ref, sg), (us_ref, su))):
        for c in range(2):
            for k in range(nz):
                load = pltpu.make_async_copy(
                    source.at[:, pl.ds((k * 2 + c) * cols, cols)],
                    buf.at[c, :, pl.ds(k * cols, cols)],
                    wsem.at[base + 1 + (n * 2 + c) * nz + k],
                )
                load.start()
                shared_in.append(load)
    load_sd = pltpu.make_async_copy(ds_ref, sd, wsem.at[base + 1 + 4 * nz])
    load_sd.start()

    coef[...] = jnp.zeros(coef.shape, F32)
    expert = lax.broadcasted_iota(jnp.int32, (steps, experts), 1)
    for b in range(requests):
        total = jnp.zeros((steps, experts), F32)
        for j in range(ids_ref.shape[2]):
            total += jnp.where(ids_ref[b][:, j : j + 1] == expert, ew_ref[b][:, j : j + 1], 0.0)
        coef[pl.ds(b * steps, steps), pl.ds(0, experts)] = total
    high, low = split_two(coef[:, 0:experts])
    cbuf[me] = jnp.concatenate([high, low], axis=1)
    push(cbuf.at[me], cbuf.at[me], cosend, corecv)
    push(kv_ref.at[me], kv_ref.at[me], kvsend, kvrecv)

    scalars = []
    prow = lax.broadcasted_iota(jnp.int32, (hr, total_rows), 0)
    pcol = lax.broadcasted_iota(jnp.int32, (hr, total_rows), 1)
    padded = pick.shape[0]
    scol = lax.broadcasted_iota(jnp.int32, (1, padded), 1)
    of_slot = jnp.full((1, padded), -1, jnp.int32)
    for s in range(padded // hr):
        if s < pool:
            request = req_ref[s]
            held = jnp.maximum(request, 0)
            edge = jnp.where(request >= 0, lens_ref[held] - blk_ref[s] * block, -1)
            first = held // requests * ROWS + held % requests * steps
            first = jnp.where(request >= 0, first, -steps)
            scalars.append((request, edge))
            chosen = (pcol - first == prow % steps) & (pcol >= first) & (first >= 0)
            of_slot = jnp.where(scol // hr == s, request, of_slot)
            pick[s * hr : (s + 1) * hr, :] = jnp.where(chosen, 1.0, 0.0)
        else:
            pick[s * hr : (s + 1) * hr, :] = jnp.zeros((hr, total_rows), F32)
    grow = lax.broadcasted_iota(jnp.int32, gatherer.shape, 0)
    gcol = lax.broadcasted_iota(jnp.int32, gatherer.shape, 1)
    gatherer[...] = jnp.where(
        (grow // hr == of_slot) & (grow % hr == gcol % hr), 1.0, 0.0
    ).astype(BF16)

    scale = 1.0 / math.sqrt(HD)
    nrow = lax.broadcasted_iota(jnp.int32, (requests * hr, ROWS), 0)
    ncol = lax.broadcasted_iota(jnp.int32, (requests * hr, ROWS), 1)
    b_of, t_of = nrow // hr, nrow % steps
    spread = jnp.where(ncol == b_of * steps + t_of, 1.0, 0.0).astype(BF16)
    hrow = lax.broadcasted_iota(jnp.int32, (requests * hr, cols), 0) % hr // steps
    hcol = lax.broadcasted_iota(jnp.int32, (requests * hr, cols), 1) // HD
    mine = jnp.where(
        hrow == hcol, jnp.dot(spread, own_q, preferred_element_type=F32), 0.0
    ).astype(BF16)
    scores = dot_t(mine, own_k) * scale
    seen = (ncol // steps == b_of) & (ncol % steps <= t_of) & (ncol < count)
    new_top = jnp.max(jnp.where(seen, scores, -1e30), axis=-1, keepdims=True)
    weights = jnp.where(seen, jnp.exp(scores - new_top), 0.0)
    new_total = jnp.sum(weights, axis=-1, keepdims=True)
    new_full = jnp.dot(weights.astype(BF16), own_v, preferred_element_type=F32)
    new_out = new_full[:, 0:HD]
    half = lax.broadcasted_iota(jnp.int32, (requests * hr, HD), 0) % hr // steps
    for h in range(1, heads):
        new_out = jnp.where(half == h, new_full[:, h * HD : (h + 1) * HD], new_out)

    all_q = whole(qbuf, qsend, qrecv)
    all_q.wait_recv()
    frow = lax.broadcasted_iota(jnp.int32, (padded, cols), 0) % hr // steps
    fcol = lax.broadcasted_iota(jnp.int32, (padded, cols), 1) // HD
    everyone = qbuf[...].reshape(total_rows, cols)
    slots[...] = jnp.where(
        frow == fcol, jnp.dot(pick[...].astype(BF16), everyone, preferred_element_type=F32), 0.0
    )
    for piece in pieces:
        piece.wait()
    slane = lax.broadcasted_iota(jnp.int32, (hr, HD), 1)
    klane = lax.broadcasted_iota(jnp.int32, (hr, block), 1)
    upper = lax.broadcasted_iota(jnp.int32, (hr, HD), 0) // steps
    top = jnp.full((hr, HD), -1e30, F32)
    all_scores = []
    for s in range(pool):
        request, edge = scalars[s]
        scores = dot_t(slots[s * hr : (s + 1) * hr, :].astype(BF16), kbuf[s]) * scale
        scores = jnp.where(klane < edge, scores, -1e30)
        all_scores.append(scores)
        best = jnp.max(scores, axis=-1, keepdims=True)
        top = jnp.maximum(top, jnp.where(slane == request, best, -1e30))
    total = jnp.zeros((hr, HD), F32)
    for s in range(pool):
        request, edge = scalars[s]
        best = jnp.max(jnp.where(slane == request, top, -1e30), axis=-1, keepdims=True)
        weights = jnp.where(klane < edge, jnp.exp(all_scores[s] - best), 0.0)
        total += jnp.where(slane == request, jnp.sum(weights, axis=-1, keepdims=True), 0.0)
        full = jnp.dot(weights.astype(BF16), vbuf[s], preferred_element_type=F32)
        out = full[:, 0:HD]
        for h in range(1, heads):
            out = jnp.where(upper == h, full[:, h * HD : (h + 1) * HD], out)
        found[s * hr : (s + 1) * hr, :] = out
    if padded > pool * hr:
        found[pool * hr :, :] = jnp.zeros((padded - pool * hr, HD), F32)
    high, low = split_two(found[...])
    by_request = jnp.dot(gatherer[...], high, preferred_element_type=F32) + jnp.dot(
        gatherer[...], low, preferred_element_type=F32
    )
    stats = jnp.where(slane < HD // 2, top, pltpu.roll(total, HD // 2, 1))
    for d in range(ns):
        part[d, 0 : requests * hr, :] = by_request[d * requests * hr : (d + 1) * requests * hr, :]
        part[d, requests * hr :, :] = stats
    rbuf[me] = part[me]

    def push2(i, _):
        to = (me + i) % ns
        pltpu.make_async_remote_copy(
            src_ref=part.at[to], dst_ref=rbuf.at[me], send_sem=send2, recv_sem=recv2,
            device_id=peer(to, exp), device_id_type=MESH,
        ).start()
        return 0

    lax.fori_loop(1, ns, push2, 0)
    all2 = whole(part, send2, recv2)
    all2.wait_recv()

    shift = (HD - me * requests) % HD
    sums_of, tops = [], []
    for s in range(ns):
        tops.append(pltpu.roll(rbuf[s, requests * hr :, :], shift, 1))
    fresh = jnp.full((hr, HD), -1e30, F32)
    for b in range(requests):
        rows = slice(b * hr, (b + 1) * hr)
        fresh = jnp.where(slane == b, new_top[rows], fresh)
        fresh = jnp.where(slane == HD // 2 + b, new_total[rows], fresh)
    tops.append(fresh)
    best = tops[0]
    for s in range(1, ns + 1):
        best = jnp.maximum(best, tops[s])
    factors, total = [], jnp.zeros((hr, HD), F32)
    for s in range(ns + 1):
        factor = jnp.exp(jnp.where(slane < requests, tops[s] - best, 0.0))
        factors.append(factor)
        total += pltpu.roll(tops[s], HD // 2, 1) * factor
    attended = []
    for b in range(requests):
        rows = slice(b * hr, (b + 1) * hr)
        summed = new_out[rows] * factors[ns][:, b : b + 1]
        for s in range(ns):
            summed += rbuf[s, rows, :] * factors[s][:, b : b + 1]
        attended.append(summed / total[:, b : b + 1])
    stacked = jnp.concatenate(attended, axis=0).astype(BF16)
    prow = lax.broadcasted_iota(jnp.int32, (ROWS, requests * hr), 0)
    pcol = lax.broadcasted_iota(jnp.int32, (ROWS, requests * hr), 1)
    by_head = []
    for h in range(cols // HD):
        pick = (pcol == prow // steps * hr + h * steps + prow % steps) & (prow < count)
        by_head.append(
            jnp.dot(
                jnp.where(pick, 1.0, 0.0).astype(BF16), stacked, preferred_element_type=F32
            ).astype(BF16)
        )
    own = jnp.concatenate(by_head, axis=1)
    load_wo.wait()
    for e in range(ne):
        terms[e] = jnp.dot(own, wo[:, e * cols : (e + 1) * cols], preferred_element_type=F32)

    def push3(i, _):
        to = (exp + i) % ne
        pltpu.make_async_remote_copy(
            src_ref=terms.at[to], dst_ref=r3.at[exp], send_sem=send3, recv_sem=recv3,
            device_id=peer(me, to), device_id_type=MESH,
        ).start()
        return 0

    lax.fori_loop(1, ne, push3, 0)
    r3[exp] = terms[exp]
    all3 = pltpu.make_async_remote_copy(
        src_ref=terms.at[pl.ds(0, ne - 1)], dst_ref=r3.at[pl.ds(0, ne - 1)],
        send_sem=send3, recv_sem=recv3, device_id=peer(me, (exp + 1) % ne), device_id_type=MESH,
    )
    all3.wait_recv()
    residual = xs[:, pl.ds(pl.multiple_of(exp * cols, cols), cols)]
    for e in range(ne):
        residual += r3[e]

    scaled = residual * fgain_ref[:, pl.ds(pl.multiple_of(exp * cols, cols), cols)]
    square = jnp.sum(residual * residual, axis=-1, keepdims=True)
    brow = lax.broadcasted_iota(jnp.int32, (ROWS, cols), 0)
    blane = lax.broadcasted_iota(jnp.int32, (ROWS, cols), 1)
    line = jnp.sum(jnp.where(brow == blane, square, 0.0), axis=0, keepdims=True)
    high, low = split_two(line)
    scaled = jnp.where(brow == count, high.astype(F32), scaled)
    scaled = jnp.where(brow == count + 1, low.astype(F32), scaled)
    my_cols = pl.ds(pl.multiple_of(z * cols, cols), cols)
    back = pl.ds(pl.multiple_of((z * ns + me) * ROWS, ROWS), ROWS)
    xbuf[core, my_rows, my_cols] = scaled.astype(BF16)

    def push4(i, _):
        to = (z * ns + me + i) % (nz * ns)
        pltpu.make_async_remote_copy(
            src_ref=xbuf.at[core, my_rows, my_cols], dst_ref=xbuf.at[core, my_rows, my_cols],
            send_sem=send4, recv_sem=recv4.at[z],
            device_id=peer(to % ns, to // ns * 2 + core), device_id_type=MESH,
        ).start()
        return 0

    lax.fori_loop(1, nz * ns, push4, 0)
    forwards = []
    for i in range(nz):
        k = (z + i) % nz
        span = pl.ds(0, total_rows - (ROWS if i == 0 else 0))
        kcols = pl.ds(pl.multiple_of(k * cols, cols), cols)
        pltpu.make_async_remote_copy(
            src_ref=xbuf.at[core, span, kcols], dst_ref=xbuf.at[core, span, kcols],
            send_sem=send4, recv_sem=recv4.at[k], device_id=peer(me, twin), device_id_type=MESH,
        ).wait_recv()
        forward = pltpu.make_async_remote_copy(
            src_ref=xbuf.at[core, :, kcols], dst_ref=xbuf.at[core, :, kcols],
            send_sem=fsend.at[k], recv_sem=frecv.at[k], device_id=peer(me, twin), device_id_type=MESH,
        )
        forward.start()
        forwards.append(forward)

    for load in gate_up:
        load.wait()
    for j in range(own_experts):
        acc[0, j] = dot_t(xbuf[core], wg[core, j])
        acc[1, j] = dot_t(xbuf[core], wu[core, j])
    for i in range(nz):
        k = (z + i) % nz
        kcols = pl.ds(pl.multiple_of(k * cols, cols), cols)
        pltpu.make_async_remote_copy(
            src_ref=xbuf.at[other, :, kcols], dst_ref=xbuf.at[other, :, kcols],
            send_sem=fsend.at[k], recv_sem=frecv.at[k], device_id=peer(me, twin), device_id_type=MESH,
        ).wait_recv()

    trow = lax.broadcasted_iota(jnp.int32, (total_rows, total_rows), 0)
    tcol = lax.broadcasted_iota(jnp.int32, (total_rows, total_rows), 1)
    spread = (trow // ROWS == tcol // ROWS) & ((tcol % ROWS == count) | (tcol % ROWS == count + 1))
    spread = jnp.where(spread, 1.0, 0.0).astype(BF16)
    square = jnp.zeros((total_rows, HD), F32)
    for c in range(2):
        for k in range(nz):
            square += jnp.dot(
                spread, xbuf[c, :, k * cols : k * cols + HD], preferred_element_type=F32
            )
    lrow = lax.broadcasted_iota(jnp.int32, (total_rows, HD), 0)
    llane = lax.broadcasted_iota(jnp.int32, (total_rows, HD), 1)
    square = jnp.sum(
        jnp.where(lrow % ROWS == llane, square, 0.0), axis=-1, keepdims=True
    )
    row_scale = lax.rsqrt(square / width + 1e-06)

    all_c = whole(cbuf, cosend, corecv)
    all_c.wait_recv()
    coefs = cbuf[...].reshape(total_rows, 2 * experts).astype(F32)
    clane = lax.broadcasted_iota(jnp.int32, (total_rows, 2 * experts), 1)
    inners = []
    for j in range(own_experts):
        mine = me * own_experts + j
        weight = jnp.sum(
            jnp.where((clane == mine) | (clane == mine + experts), coefs, 0.0), axis=-1, keepdims=True
        )
        gate = acc[0, j] + dot_t(xbuf[other], wg[other, j])
        up = acc[1, j] + dot_t(xbuf[other], wu[other, j])
        gate, up = gate * row_scale, up * row_scale
        inners.append((jax.nn.silu(gate) * up * weight).astype(BF16))

    for load in shared_in:
        load.wait()
    load_sd.wait()
    load_wd.wait()

    square = jnp.zeros((ROWS, HD), F32)
    srow = lax.broadcasted_iota(jnp.int32, (ROWS, ROWS), 1)
    spread = jnp.where((srow == count) | (srow == count + 1), 1.0, 0.0).astype(BF16)
    gate = jnp.zeros((ROWS, sg.shape[1]), F32)
    up = jnp.zeros((ROWS, sg.shape[1]), F32)
    for c in range(2):
        rows = xbuf[c, my_rows, :]
        gate += dot_t(rows, sg[c])
        up += dot_t(rows, su[c])
        for k in range(nz):
            square += jnp.dot(
                spread, rows[:, k * cols : k * cols + HD], preferred_element_type=F32
            )
    srow = lax.broadcasted_iota(jnp.int32, (ROWS, HD), 0)
    sl = lax.broadcasted_iota(jnp.int32, (ROWS, HD), 1)
    square = jnp.sum(jnp.where(srow == sl, square, 0.0), axis=-1, keepdims=True)
    sscale = lax.rsqrt(square / width + 1e-06)
    gate, up = gate * sscale, up * sscale
    inner = jnp.where(
        lax.broadcasted_iota(jnp.int32, gate.shape, 0) < count, jax.nn.silu(gate) * up, 0.0
    ).astype(BF16)
    for e in range(ne):
        shared[e] = jnp.dot(inner, sd[:, e * cols : (e + 1) * cols], preferred_element_type=F32)

    def down(e):
        where = pl.ds(pl.multiple_of(e * cols, cols), cols)
        value = jnp.zeros((total_rows, cols), F32)
        for j in range(own_experts):
            value += jnp.dot(inners[j], wd[j, :, where], preferred_element_type=F32)
        sums[...] = value
        sums[my_rows, :] += shared[e]

    pairs = []
    for k in range(nz):
        down(k * 2 + other)
        ybuf[other, k] = sums[...].astype(BF16)
        pair = pltpu.make_async_remote_copy(
            src_ref=ybuf.at[other, k], dst_ref=ypair.at[k],
            send_sem=psend.at[k], recv_sem=precv.at[k], device_id=peer(me, twin), device_id_type=MESH,
        )
        pair.start()
        pairs.append(pair)
    for i in range(nz):
        k = (z + 1 + i) % nz
        down(k * 2 + core)
        pltpu.make_async_remote_copy(
            src_ref=ybuf.at[other, k], dst_ref=ypair.at[k],
            send_sem=psend.at[k], recv_sem=precv.at[k], device_id=peer(me, twin), device_id_type=MESH,
        ).wait_recv()
        ybuf[core, k] = (sums[...] + ypair[k].astype(F32)).astype(BF16)

        def push5(n, _):
            to = (me + n) % ns
            there = pl.ds(pl.multiple_of(to * ROWS, ROWS), ROWS)
            pltpu.make_async_remote_copy(
                src_ref=ybuf.at[core, k, there, :], dst_ref=r5.at[back, :],
                send_sem=send5, recv_sem=recv5,
                device_id=peer(to, k * 2 + core), device_id_type=MESH,
            ).start()
            return 0

        lax.fori_loop(1 if i == nz - 1 else 0, ns, push5, 0)
    r5[back, :] = ybuf[core, z, my_rows, :]
    rest = pl.ds(0, (nz * ns - 1) * ROWS)
    all5 = pltpu.make_async_remote_copy(
        src_ref=r5.at[rest, :], dst_ref=r5.at[rest, :],
        send_sem=send5, recv_sem=recv5, device_id=peer(me, twin), device_id_type=MESH,
    )
    all5.wait_recv()
    result = residual
    for k in range(nz * ns):
        result += r5[k * ROWS : (k + 1) * ROWS, :].astype(F32)
    for b in range(requests):
        out_ref[b] = result[b * steps : (b + 1) * steps, :]

    all_kv = whole(kv_ref, kvsend, kvrecv)
    all_kv.wait_recv()
    all_kv.wait_send()
    all_q.wait_send()
    all_c.wait_send()
    all2.wait_send()
    all3.wait_send()
    all5.wait_send()
    pltpu.make_async_remote_copy(
        src_ref=r5.at[rest, :], dst_ref=r5.at[rest, :],
        send_sem=send4, recv_sem=recv4.at[0], device_id=peer(me, twin), device_id_type=MESH,
    ).wait_send()
    for i in range(nz):
        forwards[i].wait_send()
        pairs[i].wait_send()


def patch_kernel(
    req_ref, blk_ref, lens_ref, kv_ref, key_ref, value_ref,
    key_out, value_out, kbuf, vbuf, fresh_rows, in_sem, out_sem,
    *, requests, steps, group,
):
    pool, block, cols = key_ref.shape
    ns = kv_ref.shape[0]
    starts = list(range(0, pool, group))
    sizes = [min(group, pool - s) for s in starts]

    def copies(g, into):
        span = pl.ds(starts[g], sizes[g])
        pairs = ((key_ref, kbuf, key_out), (value_ref, vbuf, value_out))
        result = []
        for n, (source, buf, target) in enumerate(pairs):
            if into:
                result.append(pltpu.make_async_copy(source.at[span], buf.at[span], in_sem.at[n, g]))
            else:
                result.append(pltpu.make_async_copy(buf.at[span], target.at[span], out_sem.at[n, g]))
        return result

    for g in range(len(starts)):
        for c in copies(g, True):
            c.start()
    for s in range(ns):
        kv = kv_ref[s].astype(F32)
        for b in range(requests):
            fresh_rows[s * requests + b] = kv[b * steps : (b + 1) * steps, :]
    window = 2 * ROWS
    wrow = lax.broadcasted_iota(jnp.int32, (window, cols), 0)
    for g in range(len(starts)):
        for c in copies(g, True):
            c.wait()

        def patch(i, _):
            s = starts[g] + i
            request = jnp.maximum(req_ref[s], 0)
            offset = lens_ref[request] - blk_ref[s] * block

            @pl.when((req_ref[s] >= 0) & (offset > -steps) & (offset < block))
            def _():
                first = jnp.clip(offset // ROWS * ROWS, 0, block - window)
                first = pl.multiple_of(first, ROWS)
                rel = wrow + first - offset
                for n, buf in enumerate((kbuf, vbuf)):
                    tile = buf[s, pl.ds(first, window), :].astype(F32)
                    for t in range(steps):
                        one = fresh_rows[request, t : t + 1, n * cols : (n + 1) * cols]
                        tile = jnp.where(rel == t, one, tile)
                    buf[s, pl.ds(first, window), :] = tile.astype(BF16)

            return 0

        lax.fori_loop(0, sizes[g], patch, 0)
        for c in copies(g, False):
            c.start()
    for g in range(len(starts)):
        for c in copies(g, False):
            c.wait()


def body(
    hidden_in, cache_lens, slot_request, slot_block, key_cache, value_cache, attn_gain,
    query_weight, key_weight, value_weight, out_weight, ffn_gain, expert_ids, expert_weights,
    gate_experts, up_experts, down_experts, gate_shared, up_shared, down_shared,
):
    requests, steps, width = hidden_in.shape
    ns = lax.axis_size("seq")
    ne = lax.axis_size("exp")
    nz = ne // 2
    cols = query_weight.shape[1]
    own_experts, _, fe = gate_experts.shape
    sf = gate_shared.shape[1]
    experts = own_experts * ns
    pool, block, _ = key_cache.shape
    hr = cols // HD * steps
    total_rows = ns * ROWS
    padded = -(-pool * hr // 128) * 128

    exponent = jnp.arange(HD // 2, dtype=F32) * (2.0 / HD)
    frequency = jnp.power(F32(10000.0), -exponent)
    frequency = jnp.concatenate([frequency, frequency])[None, :]

    vmem = pl.BlockSpec(memory_space=pltpu.VMEM)
    smem = pl.BlockSpec(memory_space=pltpu.SMEM)
    anys = pl.BlockSpec(memory_space=pl.ANY)
    dma = pltpu.SemaphoreType.DMA

    hidden_out, new_kv = pl.pallas_call(
        layer_kernel,
        out_shape=(
            jax.ShapeDtypeStruct((requests, steps, cols), F32),
            jax.ShapeDtypeStruct((ns, ROWS, 2 * cols), BF16),
        ),
        in_specs=[smem] * 3 + [vmem] * 6 + [anys] * 12,
        out_specs=(vmem, vmem),
        scratch_shapes=[
            pltpu.VMEM((3, width, cols), BF16),
            pltpu.VMEM((ns, ROWS, cols), BF16),
            pltpu.VMEM((ns, ROWS, 2 * experts), BF16),
            pltpu.VMEM((ROWS, 2 * experts), F32),
            pltpu.VMEM(key_cache.shape, BF16),
            pltpu.VMEM(key_cache.shape, BF16),
            pltpu.VMEM((padded, total_rows), F32),
            pltpu.VMEM((ns * requests * hr, padded), BF16),
            pltpu.VMEM((padded, cols), F32),
            pltpu.VMEM((ns, (requests + 1) * hr, HD), F32),
            pltpu.VMEM((padded, HD), F32),
            pltpu.VMEM((cols, width), BF16),
            pltpu.VMEM((2, own_experts, fe, width // 2), BF16),
            pltpu.VMEM((2, own_experts, fe, width // 2), BF16),
            pltpu.VMEM((own_experts, fe, width), BF16),
            pltpu.VMEM((2, sf, width // 2), BF16),
            pltpu.VMEM((2, sf, width // 2), BF16),
            pltpu.VMEM((sf, width), BF16),
            pltpu.VMEM((ns, (requests + 1) * hr, HD), F32),
            pltpu.VMEM((ROWS, width), F32),
            pltpu.VMEM((ne, ROWS, cols), F32),
            pltpu.VMEM((ne, ROWS, cols), F32),
            pltpu.VMEM((2, total_rows, nz * cols), BF16),
            pltpu.VMEM((2, own_experts, total_rows, fe), F32),
            pltpu.VMEM((2, nz, total_rows, cols), BF16),
            pltpu.VMEM((nz, total_rows, cols), BF16),
            pltpu.VMEM((total_rows, cols), F32),
            pltpu.VMEM((nz * total_rows, cols), BF16),
            pltpu.VMEM((ne, ROWS, cols), F32),
            dma((3,)), dma((2, 4)),
            dma, dma, dma, dma, dma, dma,
            dma((3 + 8 * nz,)),
            dma, dma, dma, dma, dma,
            dma((nz,)), dma((nz,)), dma((nz,)), dma((nz,)), dma((nz,)),
            dma, dma,
        ],
        compiler_params=pltpu.CompilerParams(collective_id=0, has_side_effects=True),
        name="layer",
    )(
        cache_lens, slot_request, slot_block, frequency, hidden_in, attn_gain[None, :],
        expert_ids, expert_weights, ffn_gain[None, :],
        query_weight, key_weight, value_weight, key_cache, value_cache, out_weight,
        jnp.swapaxes(gate_experts, 1, 2), jnp.swapaxes(up_experts, 1, 2), down_experts,
        gate_shared.T, up_shared.T, down_shared,
    )

    group = 8
    groups = -(-pool // group)
    key_out, value_out = pl.pallas_call(
        functools.partial(patch_kernel, requests=requests, steps=steps, group=group),
        out_shape=(
            jax.ShapeDtypeStruct(key_cache.shape, BF16),
            jax.ShapeDtypeStruct(value_cache.shape, BF16),
        ),
        in_specs=[smem, smem, smem, vmem, anys, anys],
        out_specs=(anys, anys),
        scratch_shapes=[
            pltpu.VMEM(key_cache.shape, BF16),
            pltpu.VMEM(key_cache.shape, BF16),
            pltpu.VMEM((ns * requests, steps, 2 * cols), F32),
            dma((2, groups)),
            dma((2, groups)),
        ],
        name="patch",
    )(slot_request, slot_block, cache_lens, new_kv, key_cache, value_cache)
    return (hidden_out, key_out, value_out)


def solution(mesh):
    in_specs = (
        P("seq", None, None),
        P(),
        P("seq"),
        P("seq"),
        P("seq", None, "exp"),
        P("seq", None, "exp"),
        P(),
        P(None, "exp"),
        P(None, "exp"),
        P(None, "exp"),
        P("exp", None),
        P(),
        P("seq", None, None),
        P("seq", None, None),
        P("seq", None, "exp"),
        P("seq", None, "exp"),
        P("seq", "exp", None),
        P(None, "exp"),
        P(None, "exp"),
        P("exp", None),
    )
    out_specs = (P("seq", None, "exp"), P("seq", None, "exp"), P("seq", None, "exp"))
    return jax.shard_map(body, mesh=mesh, in_specs=in_specs, out_specs=out_specs, check_vma=False)
```

```python
import functools
import math

import jax
import jax.numpy as jnp
import numpy as np
from jax import lax
from jax.experimental import pallas as pl
from jax.experimental.pallas import tpu as pltpu
from jax.sharding import PartitionSpec as P

HD = 128
MESH = pl.DeviceIdType.MESH
F32 = jnp.float32
BF16 = jnp.bfloat16
ROWS = 16


def peer(seq, exp):
    return {"seq": seq, "exp": exp}


def rows_of(ref, scratch):
    count, steps, _ = ref.shape
    for b in range(count):
        scratch[pl.ds(b * steps, steps), :] = ref[b]
    used = count * steps
    scratch[pl.ds(used, ROWS - used), :] = jnp.zeros((ROWS - used, ref.shape[2]), F32)


def dot_t(a, b):
    return lax.dot_general(a, b, (((1,), (1,)), ((), ())), preferred_element_type=F32)


def split_two(values):
    high = values.astype(BF16)
    low = (values - high.astype(F32)).astype(BF16)
    return high, low


def layer_kernel(
    lens_any, req_any, blk_any, freq_any, hidden_any, again_any, ids_any, ew_any, fgain_any,
    wq_ref, wk_ref, wv_ref, key_ref, value_ref,
    wo_ref, ge_ref, ue_ref, de_ref, gs_ref, us_ref, ds_ref,
    out_ref, kv_ref,
    lens_ref, req_ref, blk_ref, freq_ref, hidden_ref, again_ref, ids_ref, ew_ref, fgain_ref,
    wbuf, qbuf, kvbuf, cbuf, coef, kbuf, vbuf, pick, gatherer, slots, part, found,
    wo, wg, wu, wd, sg, su, sd, rbuf, xs, terms, r3, xbuf, acc, routing, scales, ybuf, ypair, sums, r5, shared, r6,
    isem, asem, csem, ksem, qsend, qrecv, kvsend, kvrecv, cosend, corecv,
    wsem, send2, recv2, send3, recv3, send4, recv4, fsend, frecv, psend, precv, send5, recv5, send6, recv6,
):
    ns = lax.axis_size("seq")
    ne = lax.axis_size("exp")
    nz = ne // 2
    me = lax.axis_index("seq")
    exp = lax.axis_index("exp")
    z, core = exp // 2, exp % 2
    other = 1 - core
    twin = z * 2 + other
    requests, steps, width = hidden_ref.shape
    cols = wq_ref.shape[1]
    heads = cols // HD
    hr = heads * steps
    pool, block, _ = key_ref.shape
    experts = coef.shape[1] // 2
    own_experts = experts // ns
    fe = ge_ref.shape[0] // own_experts
    count = requests * steps
    total_rows = ns * ROWS

    barrier = pltpu.get_barrier_semaphore()

    def greet_seq(i, _):
        pl.semaphore_signal(barrier, inc=1, device_id=peer((me + i) % ns, exp), device_id_type=MESH)
        return 0

    def greet_exp(i, _):
        pl.semaphore_signal(barrier, inc=1, device_id=peer(me, (exp + i) % ne), device_id_type=MESH)
        return 0

    lax.fori_loop(1, ns, greet_seq, 0)
    lax.fori_loop(1, ne, greet_exp, 0)
    small = []
    pairs = (
        (hidden_any, hidden_ref), (again_any, again_ref), (lens_any, lens_ref),
        (freq_any, freq_ref), (ids_any, ids_ref), (ew_any, ew_ref), (req_any, req_ref),
        (blk_any, blk_ref), (fgain_any, fgain_ref),
    )
    for n, (source, buf) in enumerate(pairs):
        load = pltpu.make_async_copy(source, buf, isem.at[n])
        load.start()
        small.append(load)
    loads = []
    for k, w in enumerate((wq_ref, wk_ref, wv_ref)):
        load = pltpu.make_async_copy(w, wbuf.at[k], asem.at[k])
        load.start()
        loads.append(load)
    pieces = []
    chunk = -(-pool // 4)
    for g in range(4):
        span = pl.ds(g * chunk, min(chunk, pool - g * chunk))
        for n, (source, buf) in enumerate(((key_ref, kbuf), (value_ref, vbuf))):
            load = pltpu.make_async_copy(source.at[span], buf.at[span], csem.at[n, g])
            load.start()
            pieces.append(load)

    for load in small[:4]:
        load.wait()
    rows_of(hidden_ref, xs)
    x = xs[...]
    mean_square = jnp.mean(x * x, axis=-1, keepdims=True)
    normed = (x * lax.rsqrt(mean_square + 1e-06) * again_ref[...]).astype(BF16)
    row = lax.broadcasted_iota(jnp.int32, (ROWS, HD), 0)
    lane = lax.broadcasted_iota(jnp.int32, (ROWS, HD), 1)
    length = jnp.zeros((ROWS, HD), jnp.int32)
    for b in range(requests):
        length = jnp.where(row // steps == b, lens_ref[me * requests + b], length)
    position = (length + row % steps).astype(F32)
    angles = position * freq_ref[...]
    cosine = jnp.cos(angles)
    sine = jnp.sin(angles)
    sine = jnp.where(lane < HD // 2, -sine, sine)

    def rotate(v):
        parts = []
        for h in range(heads):
            one = v[:, h * HD : (h + 1) * HD]
            parts.append(one * cosine + pltpu.roll(one, HD // 2, 1) * sine)
        return jnp.concatenate(parts, axis=1)

    def push(src, dst, send, recv):
        def one(i, _):
            pltpu.make_async_remote_copy(
                src_ref=src, dst_ref=dst, send_sem=send, recv_sem=recv,
                device_id=peer((me + i) % ns, exp), device_id_type=MESH,
            ).start()
            return 0

        lax.fori_loop(1, ns, one, 0)

    def whole(ref, send, recv):
        return pltpu.make_async_remote_copy(
            src_ref=ref.at[pl.ds(0, ns - 1)], dst_ref=ref.at[pl.ds(0, ns - 1)],
            send_sem=send, recv_sem=recv,
            device_id=peer((me + 1) % ns, exp), device_id_type=MESH,
        )

    my_rows = pl.ds(pl.multiple_of(me * ROWS, ROWS), ROWS)
    loads[0].wait()
    own_q = rotate(jnp.dot(normed, wbuf[0], preferred_element_type=F32)).astype(BF16)
    qbuf[me] = own_q
    pl.semaphore_wait(barrier, ns - 1 + ne - 1)
    push(qbuf.at[me], qbuf.at[me], qsend, qrecv)
    loads[1].wait()
    own_k = rotate(jnp.dot(normed, wbuf[1], preferred_element_type=F32)).astype(BF16)
    kvbuf[:, 0:cols] = own_k
    loads[2].wait()
    own_v = jnp.dot(normed, wbuf[2], preferred_element_type=F32).astype(BF16)
    kvbuf[:, cols : 2 * cols] = own_v
    keep_kv = pltpu.make_async_copy(kvbuf, kv_ref.at[me], ksem)
    keep_kv.start()

    load_wo = pltpu.make_async_copy(wo_ref, wo, wsem.at[0])
    load_wo.start()
    gate_up, shared_in = [], []
    for n, (source, buf) in enumerate(((ge_ref, wg), (ue_ref, wu))):
        for c in range(2):
            for k in range(nz):
                load = pltpu.make_async_copy(
                    source.at[:, pl.ds((k * 2 + c) * cols, cols)],
                    buf.at[c, :, pl.ds(k * cols, cols)],
                    wsem.at[1 + (n * 2 + c) * nz + k],
                )
                load.start()
                gate_up.append(load)
    base = 1 + 4 * nz
    load_wd = pltpu.make_async_copy(de_ref, wd, wsem.at[base])
    load_wd.start()
    for n, (source, buf) in enumerate(((gs_ref, sg), (us_ref, su))):
        for c in range(2):
            for k in range(nz):
                load = pltpu.make_async_copy(
                    source.at[:, pl.ds((k * 2 + c) * cols, cols)],
                    buf.at[c, :, pl.ds(k * cols, cols)],
                    wsem.at[base + 1 + (n * 2 + c) * nz + k],
                )
                load.start()
                shared_in.append(load)
    load_sd = pltpu.make_async_copy(ds_ref, sd, wsem.at[base + 1 + 4 * nz])
    load_sd.start()

    for load in small[4:]:
        load.wait()
    coef[...] = jnp.zeros(coef.shape, F32)
    expert = lax.broadcasted_iota(jnp.int32, (steps, experts), 1)
    for b in range(requests):
        total = jnp.zeros((steps, experts), F32)
        for j in range(ids_ref.shape[2]):
            total += jnp.where(ids_ref[b][:, j : j + 1] == expert, ew_ref[b][:, j : j + 1], 0.0)
        coef[pl.ds(b * steps, steps), pl.ds(0, experts)] = total
    high, low = split_two(coef[:, 0:experts])
    cbuf[me] = jnp.concatenate([high, low], axis=1)

    scalars = []
    prow = lax.broadcasted_iota(jnp.int32, (hr, total_rows), 0)
    pcol = lax.broadcasted_iota(jnp.int32, (hr, total_rows), 1)
    padded = pick.shape[0]
    scol = lax.broadcasted_iota(jnp.int32, (1, padded), 1)
    of_slot = jnp.full((1, padded), -1, jnp.int32)
    for s in range(padded // hr):
        if s < pool:
            request = req_ref[s]
            held = jnp.maximum(request, 0)
            edge = jnp.where(request >= 0, lens_ref[held] - blk_ref[s] * block, -1)
            first = held // requests * ROWS + held % requests * steps
            first = jnp.where(request >= 0, first, -steps)
            scalars.append((request, edge))
            chosen = (pcol - first == prow % steps) & (pcol >= first) & (first >= 0)
            of_slot = jnp.where(scol // hr == s, request, of_slot)
            pick[s * hr : (s + 1) * hr, :] = jnp.where(chosen, 1.0, 0.0)
        else:
            pick[s * hr : (s + 1) * hr, :] = jnp.zeros((hr, total_rows), F32)
    grow = lax.broadcasted_iota(jnp.int32, gatherer.shape, 0)
    gcol = lax.broadcasted_iota(jnp.int32, gatherer.shape, 1)
    gatherer[...] = jnp.where(
        (grow // hr == of_slot) & (grow % hr == gcol % hr), 1.0, 0.0
    ).astype(BF16)

    scale = 1.0 / math.sqrt(HD)
    nrow = lax.broadcasted_iota(jnp.int32, (requests * hr, ROWS), 0)
    ncol = lax.broadcasted_iota(jnp.int32, (requests * hr, ROWS), 1)
    b_of, t_of = nrow // hr, nrow % steps
    spread = jnp.where(ncol == b_of * steps + t_of, 1.0, 0.0).astype(BF16)
    hrow = lax.broadcasted_iota(jnp.int32, (requests * hr, cols), 0) % hr // steps
    hcol = lax.broadcasted_iota(jnp.int32, (requests * hr, cols), 1) // HD
    mine = jnp.where(
        hrow == hcol, jnp.dot(spread, own_q, preferred_element_type=F32), 0.0
    ).astype(BF16)
    scores = dot_t(mine, own_k) * scale
    seen = (ncol // steps == b_of) & (ncol % steps <= t_of) & (ncol < count)
    new_top = jnp.max(jnp.where(seen, scores, -1e30), axis=-1, keepdims=True)
    weights = jnp.where(seen, jnp.exp(scores - new_top), 0.0)
    new_total = jnp.sum(weights, axis=-1, keepdims=True)
    new_full = jnp.dot(weights.astype(BF16), own_v, preferred_element_type=F32)
    new_out = new_full[:, 0:HD]
    half = lax.broadcasted_iota(jnp.int32, (requests * hr, HD), 0) % hr // steps
    for h in range(1, heads):
        new_out = jnp.where(half == h, new_full[:, h * HD : (h + 1) * HD], new_out)

    all_q = whole(qbuf, qsend, qrecv)
    all_q.wait_recv()
    frow = lax.broadcasted_iota(jnp.int32, (padded, cols), 0) % hr // steps
    fcol = lax.broadcasted_iota(jnp.int32, (padded, cols), 1) // HD
    everyone = qbuf[...].reshape(total_rows, cols)
    slots[...] = jnp.where(
        frow == fcol, jnp.dot(pick[...].astype(BF16), everyone, preferred_element_type=F32), 0.0
    )
    for piece in pieces:
        piece.wait()
    slane = lax.broadcasted_iota(jnp.int32, (hr, HD), 1)
    klane = lax.broadcasted_iota(jnp.int32, (hr, block), 1)
    upper = lax.broadcasted_iota(jnp.int32, (hr, HD), 0) // steps
    top = jnp.full((hr, HD), -1e30, F32)
    all_scores = []
    for s in range(pool):
        request, edge = scalars[s]
        scores = dot_t(slots[s * hr : (s + 1) * hr, :].astype(BF16), kbuf[s]) * scale
        scores = jnp.where(klane < edge, scores, -1e30)
        all_scores.append(scores)
        best = jnp.max(scores, axis=-1, keepdims=True)
        top = jnp.maximum(top, jnp.where(slane == request, best, -1e30))
    top = top.astype(BF16).astype(F32)
    total = jnp.zeros((hr, HD), F32)
    for s in range(pool):
        request, edge = scalars[s]
        best = jnp.max(jnp.where(slane == request, top, -1e30), axis=-1, keepdims=True)
        weights = jnp.where(klane < edge, jnp.exp(all_scores[s] - best), 0.0)
        total += jnp.where(slane == request, jnp.sum(weights, axis=-1, keepdims=True), 0.0)
        full = jnp.dot(weights.astype(BF16), vbuf[s], preferred_element_type=F32)
        out = full[:, 0:HD]
        for h in range(1, heads):
            out = jnp.where(upper == h, full[:, h * HD : (h + 1) * HD], out)
        found[s * hr : (s + 1) * hr, :] = out
    if padded > pool * hr:
        found[pool * hr :, :] = jnp.zeros((padded - pool * hr, HD), F32)
    high, low = split_two(found[...])
    by_request = jnp.dot(gatherer[...], high, preferred_element_type=F32) + jnp.dot(
        gatherer[...], low, preferred_element_type=F32
    )
    high, low = split_two(pltpu.roll(total, HD // 2, 1))
    stats = jnp.concatenate(
        [jnp.where(slane < HD // 2, top, high.astype(F32)), low.astype(F32)], axis=0
    ).astype(BF16)
    by_request = by_request.astype(BF16)
    for d in range(ns):
        part[d, 0 : requests * hr, :] = by_request[d * requests * hr : (d + 1) * requests * hr, :]
        part[d, requests * hr :, :] = stats
    rbuf[me] = part[me]

    def push2(i, _):
        to = (me + i) % ns
        pltpu.make_async_remote_copy(
            src_ref=part.at[to], dst_ref=rbuf.at[me], send_sem=send2, recv_sem=recv2,
            device_id=peer(to, exp), device_id_type=MESH,
        ).start()
        return 0

    lax.fori_loop(1, ns, push2, 0)
    all2 = whole(part, send2, recv2)
    all2.wait_recv()

    shift = (HD - me * requests) % HD
    sums_of, tops = [], []
    for s in range(ns):
        stats = rbuf[s, requests * hr :, :].astype(F32)
        low = jnp.where(slane < HD // 2, 0.0, stats[hr:])
        tops.append(pltpu.roll(stats[0:hr] + low, shift, 1))
    fresh = jnp.full((hr, HD), -1e30, F32)
    for b in range(requests):
        rows = slice(b * hr, (b + 1) * hr)
        fresh = jnp.where(slane == b, new_top[rows], fresh)
        fresh = jnp.where(slane == HD // 2 + b, new_total[rows], fresh)
    tops.append(fresh)
    best = tops[0]
    for s in range(1, ns + 1):
        best = jnp.maximum(best, tops[s])
    factors, total = [], jnp.zeros((hr, HD), F32)
    for s in range(ns + 1):
        factor = jnp.exp(jnp.where(slane < requests, tops[s] - best, 0.0))
        factors.append(factor)
        total += pltpu.roll(tops[s], HD // 2, 1) * factor
    held = [rbuf[s, 0 : requests * hr, :].astype(F32) for s in range(ns)]
    attended = []
    for b in range(requests):
        rows = slice(b * hr, (b + 1) * hr)
        summed = new_out[rows] * factors[ns][:, b : b + 1]
        for s in range(ns):
            summed += held[s][rows] * factors[s][:, b : b + 1]
        attended.append(summed / total[:, b : b + 1])
    stacked = jnp.concatenate(attended, axis=0).astype(BF16)
    prow = lax.broadcasted_iota(jnp.int32, (ROWS, requests * hr), 0)
    pcol = lax.broadcasted_iota(jnp.int32, (ROWS, requests * hr), 1)
    by_head = []
    for h in range(cols // HD):
        pick = (pcol == prow // steps * hr + h * steps + prow % steps) & (prow < count)
        by_head.append(
            jnp.dot(
                jnp.where(pick, 1.0, 0.0).astype(BF16), stacked, preferred_element_type=F32
            ).astype(BF16)
        )
    own = jnp.concatenate(by_head, axis=1)
    load_wo.wait()
    for e in range(ne):
        terms[e] = jnp.dot(
            own, wo[:, e * cols : (e + 1) * cols], preferred_element_type=F32
        ).astype(BF16)

    def push3(i, _):
        to = (exp + i) % ne
        pltpu.make_async_remote_copy(
            src_ref=terms.at[to], dst_ref=r3.at[exp], send_sem=send3, recv_sem=recv3,
            device_id=peer(me, to), device_id_type=MESH,
        ).start()
        return 0

    lax.fori_loop(1, ne, push3, 0)
    push(cbuf.at[me], cbuf.at[me], cosend, corecv)
    push(kvbuf, kv_ref.at[me], kvsend, kvrecv)
    r3[exp] = terms[exp]
    all3 = pltpu.make_async_remote_copy(
        src_ref=terms.at[pl.ds(0, ne - 1)], dst_ref=r3.at[pl.ds(0, ne - 1)],
        send_sem=send3, recv_sem=recv3, device_id=peer(me, (exp + 1) % ne), device_id_type=MESH,
    )
    all3.wait_recv()
    residual = xs[:, pl.ds(pl.multiple_of(exp * cols, cols), cols)]
    for e in range(ne):
        residual += r3[e].astype(F32)

    scaled = residual * fgain_ref[:, pl.ds(pl.multiple_of(exp * cols, cols), cols)]
    square = jnp.sum(residual * residual, axis=-1, keepdims=True)
    brow = lax.broadcasted_iota(jnp.int32, (ROWS, cols), 0)
    blane = lax.broadcasted_iota(jnp.int32, (ROWS, cols), 1)
    line = jnp.sum(jnp.where(brow == blane, square, 0.0), axis=0, keepdims=True)
    high, low = split_two(line)
    scaled = jnp.where(brow == count, high.astype(F32), scaled)
    scaled = jnp.where(brow == count + 1, low.astype(F32), scaled)
    my_cols = pl.ds(pl.multiple_of(z * cols, cols), cols)
    back = pl.ds(pl.multiple_of((z * ns + me) * ROWS, ROWS), ROWS)
    xbuf[core, my_rows, my_cols] = scaled.astype(BF16)

    def push4(i, _):
        to = (z * ns + me + i) % (nz * ns)
        pltpu.make_async_remote_copy(
            src_ref=xbuf.at[core, my_rows, my_cols], dst_ref=xbuf.at[core, my_rows, my_cols],
            send_sem=send4, recv_sem=recv4.at[z],
            device_id=peer(to % ns, to // ns * 2 + core), device_id_type=MESH,
        ).start()
        return 0

    lax.fori_loop(1, nz * ns, push4, 0)

    all_c = whole(cbuf, cosend, corecv)
    all_c.wait_recv()
    coefs = cbuf[...].reshape(total_rows, 2 * experts).astype(F32)
    clane = lax.broadcasted_iota(jnp.int32, (total_rows, 2 * experts), 1)
    ucol = lax.broadcasted_iota(jnp.int32, (total_rows, wd.shape[0]), 1)
    routing[...] = jnp.zeros(routing.shape, F32)
    for j in range(own_experts):
        mine = me * own_experts + j
        weight = jnp.sum(
            jnp.where((clane == mine) | (clane == mine + experts), coefs, 0.0), axis=-1, keepdims=True
        )
        routing[...] += jnp.where((ucol >= j * fe) & (ucol < (j + 1) * fe), weight, 0.0)

    forwards = []
    for i in range(nz):
        k = (z + i) % nz
        span = pl.ds(0, total_rows - (ROWS if i == 0 else 0))
        kcols = pl.ds(pl.multiple_of(k * cols, cols), cols)
        pltpu.make_async_remote_copy(
            src_ref=xbuf.at[core, span, kcols], dst_ref=xbuf.at[core, span, kcols],
            send_sem=send4, recv_sem=recv4.at[k], device_id=peer(me, twin), device_id_type=MESH,
        ).wait_recv()
        forward = pltpu.make_async_remote_copy(
            src_ref=xbuf.at[core, :, kcols], dst_ref=xbuf.at[core, :, kcols],
            send_sem=fsend.at[k], recv_sem=frecv.at[k], device_id=peer(me, twin), device_id_type=MESH,
        )
        forward.start()
        forwards.append(forward)

    for load in gate_up:
        load.wait()
    acc[0] = dot_t(xbuf[core], wg[core])
    acc[1] = dot_t(xbuf[core], wu[core])

    trow = lax.broadcasted_iota(jnp.int32, (total_rows, total_rows), 0)
    tcol = lax.broadcasted_iota(jnp.int32, (total_rows, total_rows), 1)
    spread = (trow // ROWS == tcol // ROWS) & ((tcol % ROWS == count) | (tcol % ROWS == count + 1))
    spread = jnp.where(spread, 1.0, 0.0).astype(BF16)

    def squares(c):
        value = xbuf[c, :, 0:HD].astype(F32)
        for k in range(1, nz):
            value += xbuf[c, :, k * cols : k * cols + HD].astype(F32)
        return value

    first = squares(core)
    for i in range(nz):
        k = (z + i) % nz
        kcols = pl.ds(pl.multiple_of(k * cols, cols), cols)
        pltpu.make_async_remote_copy(
            src_ref=xbuf.at[other, :, kcols], dst_ref=xbuf.at[other, :, kcols],
            send_sem=fsend.at[k], recv_sem=frecv.at[k], device_id=peer(me, twin), device_id_type=MESH,
        ).wait_recv()
    high, low = split_two(first + squares(other))
    square = jnp.dot(spread, high, preferred_element_type=F32) + jnp.dot(
        spread, low, preferred_element_type=F32
    )
    lrow = lax.broadcasted_iota(jnp.int32, (total_rows, HD), 0)
    llane = lax.broadcasted_iota(jnp.int32, (total_rows, HD), 1)
    square = jnp.sum(jnp.where(lrow % ROWS == llane, square, 0.0), axis=-1, keepdims=True)
    row_scale = lax.rsqrt(square / width + 1e-06)
    scales[...] = jnp.broadcast_to(row_scale, scales.shape)
    gate = (acc[0] + dot_t(xbuf[other], wg[other])) * row_scale
    up = (acc[1] + dot_t(xbuf[other], wu[other])) * row_scale
    inner = (jax.nn.silu(gate) * up * routing[...]).astype(BF16)
    load_wd.wait()

    def down(e):
        where = pl.ds(pl.multiple_of(e * cols, cols), cols)
        return jnp.dot(inner, wd[:, where], preferred_element_type=F32)

    pairs = []

    def give(i):
        k = (z + 1 + i) % nz
        ybuf[other, k] = down(k * 2 + other).astype(BF16)
        pair = pltpu.make_async_remote_copy(
            src_ref=ybuf.at[other, k], dst_ref=ypair.at[k],
            send_sem=psend.at[k], recv_sem=precv.at[k], device_id=peer(me, twin), device_id_type=MESH,
        )
        pair.start()
        pairs.append(pair)

    give(0)
    give(1)
    for i in range(nz):
        k = (z + 1 + i) % nz
        if i + 2 < nz:
            give(i + 2)
        sums[...] = down(k * 2 + core)
        pairs[i].wait_recv()
        ybuf[core, k] = (sums[...] + ypair[k].astype(F32)).astype(BF16)

        def push5(n, _):
            to = (me + n) % ns
            there = pl.ds(pl.multiple_of(to * ROWS, ROWS), ROWS)
            pltpu.make_async_remote_copy(
                src_ref=ybuf.at[core, k, there, :], dst_ref=r5.at[back, :],
                send_sem=send5, recv_sem=recv5,
                device_id=peer(to, k * 2 + core), device_id_type=MESH,
            ).start()
            return 0

        lax.fori_loop(1 if i == nz - 1 else 0, ns, push5, 0)
    r5[back, :] = ybuf[core, z, my_rows, :]

    for load in shared_in:
        load.wait()
    load_sd.wait()
    gate = jnp.zeros((ROWS, sg.shape[1]), F32)
    up = jnp.zeros((ROWS, sg.shape[1]), F32)
    for c in range(2):
        rows = xbuf[c, my_rows, :]
        gate += dot_t(rows, sg[c])
        up += dot_t(rows, su[c])
    own_scale = scales[my_rows, 0:1]
    gate, up = gate * own_scale, up * own_scale
    inner = jnp.where(
        lax.broadcasted_iota(jnp.int32, gate.shape, 0) < count, jax.nn.silu(gate) * up, 0.0
    ).astype(BF16)
    for e in range(ne):
        shared[e] = jnp.dot(
            inner, sd[:, e * cols : (e + 1) * cols], preferred_element_type=F32
        ).astype(BF16)

    def push6(i, _):
        to = (exp + i) % ne
        pltpu.make_async_remote_copy(
            src_ref=shared.at[to], dst_ref=r6.at[exp], send_sem=send6, recv_sem=recv6,
            device_id=peer(me, to), device_id_type=MESH,
        ).start()
        return 0

    lax.fori_loop(1, ne, push6, 0)
    r6[exp] = shared[exp]
    all6 = pltpu.make_async_remote_copy(
        src_ref=shared.at[pl.ds(0, ne - 1)], dst_ref=r6.at[pl.ds(0, ne - 1)],
        send_sem=send6, recv_sem=recv6, device_id=peer(me, (exp + 1) % ne), device_id_type=MESH,
    )
    all6.wait_recv()
    result = residual
    for e in range(ne):
        result += r6[e].astype(F32)

    rest = pl.ds(0, (nz * ns - 1) * ROWS)
    all5 = pltpu.make_async_remote_copy(
        src_ref=r5.at[rest, :], dst_ref=r5.at[rest, :],
        send_sem=send5, recv_sem=recv5, device_id=peer(me, twin), device_id_type=MESH,
    )
    all5.wait_recv()
    for k in range(nz * ns):
        result += r5[k * ROWS : (k + 1) * ROWS, :].astype(F32)
    for b in range(requests):
        out_ref[b] = result[b * steps : (b + 1) * steps, :]

    all_kv = whole(kv_ref, kvsend, kvrecv)
    all_kv.wait_recv()
    all_kv.wait_send()
    keep_kv.wait()
    all_q.wait_send()
    all_c.wait_send()
    all2.wait_send()
    all3.wait_send()
    all5.wait_send()
    all6.wait_send()
    pltpu.make_async_remote_copy(
        src_ref=r5.at[rest, :], dst_ref=r5.at[rest, :],
        send_sem=send4, recv_sem=recv4.at[0], device_id=peer(me, twin), device_id_type=MESH,
    ).wait_send()
    for i in range(nz):
        forwards[i].wait_send()
        pairs[i].wait_send()


def patch_kernel(
    req_ref, blk_ref, lens_ref, kv_any, key_ref, value_ref,
    key_out, value_out, kv_ref, kbuf, vbuf, fresh_rows, kv_sem, in_sem, out_sem,
    *, requests, steps, group,
):
    pool, block, cols = key_ref.shape
    ns = kv_any.shape[0]
    starts = list(range(0, pool, group))
    sizes = [min(group, pool - s) for s in starts]

    def copies(g, into):
        span = pl.ds(starts[g], sizes[g])
        pairs = ((key_ref, kbuf, key_out), (value_ref, vbuf, value_out))
        result = []
        for n, (source, buf, target) in enumerate(pairs):
            if into:
                result.append(pltpu.make_async_copy(source.at[span], buf.at[span], in_sem.at[n, g]))
            else:
                result.append(pltpu.make_async_copy(buf.at[span], target.at[span], out_sem.at[n, g]))
        return result

    load_kv = pltpu.make_async_copy(kv_any, kv_ref, kv_sem)
    load_kv.start()
    for g in range(len(starts)):
        for c in copies(g, True):
            c.start()
    load_kv.wait()
    for s in range(ns):
        kv = kv_ref[s].astype(F32)
        for b in range(requests):
            fresh_rows[s * requests + b] = kv[b * steps : (b + 1) * steps, :]
    window = 2 * ROWS
    wrow = lax.broadcasted_iota(jnp.int32, (window, cols), 0)
    for g in range(len(starts)):
        for c in copies(g, True):
            c.wait()

        def patch(i, _):
            s = starts[g] + i
            request = jnp.maximum(req_ref[s], 0)
            offset = lens_ref[request] - blk_ref[s] * block

            @pl.when((req_ref[s] >= 0) & (offset > -steps) & (offset < block))
            def _():
                first = jnp.clip(offset // ROWS * ROWS, 0, block - window)
                first = pl.multiple_of(first, ROWS)
                rel = wrow + first - offset
                for n, buf in enumerate((kbuf, vbuf)):
                    tile = buf[s, pl.ds(first, window), :].astype(F32)
                    for t in range(steps):
                        one = fresh_rows[request, t : t + 1, n * cols : (n + 1) * cols]
                        tile = jnp.where(rel == t, one, tile)
                    buf[s, pl.ds(first, window), :] = tile.astype(BF16)

            return 0

        lax.fori_loop(0, sizes[g], patch, 0)
        for c in copies(g, False):
            c.start()
    for g in range(len(starts)):
        for c in copies(g, False):
            c.wait()


def body(
    hidden_in, cache_lens, slot_request, slot_block, key_cache, value_cache, attn_gain,
    query_weight, key_weight, value_weight, out_weight, ffn_gain, expert_ids, expert_weights,
    gate_experts, up_experts, down_experts, gate_shared, up_shared, down_shared,
):
    requests, steps, width = hidden_in.shape
    ns = lax.axis_size("seq")
    ne = lax.axis_size("exp")
    nz = ne // 2
    cols = query_weight.shape[1]
    own_experts, _, fe = gate_experts.shape
    sf = gate_shared.shape[1]
    experts = own_experts * ns
    pool, block, _ = key_cache.shape
    hr = cols // HD * steps
    total_rows = ns * ROWS
    padded = -(-pool * hr // 128) * 128

    exponent = np.arange(HD // 2) * (2.0 / HD)
    frequency = np.power(10000.0, -exponent).astype(np.float32)
    frequency = jnp.asarray(np.concatenate([frequency, frequency])[None, :])

    vmem = pl.BlockSpec(memory_space=pltpu.VMEM)
    smem = pl.BlockSpec(memory_space=pltpu.SMEM)
    anys = pl.BlockSpec(memory_space=pl.ANY)
    dma = pltpu.SemaphoreType.DMA

    hidden_out, new_kv = pl.pallas_call(
        layer_kernel,
        out_shape=(
            jax.ShapeDtypeStruct((requests, steps, cols), F32),
            jax.ShapeDtypeStruct((ns, ROWS, 2 * cols), BF16),
        ),
        in_specs=[anys] * 21,
        out_specs=(vmem, anys),
        scratch_shapes=[
            pltpu.SMEM(cache_lens.shape, jnp.int32),
            pltpu.SMEM(slot_request.shape, jnp.int32),
            pltpu.SMEM(slot_block.shape, jnp.int32),
            pltpu.VMEM((1, HD), F32),
            pltpu.VMEM(hidden_in.shape, F32),
            pltpu.VMEM((1, width), F32),
            pltpu.VMEM(expert_ids.shape, jnp.int32),
            pltpu.VMEM(expert_weights.shape, F32),
            pltpu.VMEM((1, width), F32),
            pltpu.VMEM((3, width, cols), BF16),
            pltpu.VMEM((ns, ROWS, cols), BF16),
            pltpu.VMEM((ROWS, 2 * cols), BF16),
            pltpu.VMEM((ns, ROWS, 2 * experts), BF16),
            pltpu.VMEM((ROWS, 2 * experts), F32),
            pltpu.VMEM(key_cache.shape, BF16),
            pltpu.VMEM(key_cache.shape, BF16),
            pltpu.VMEM((padded, total_rows), F32),
            pltpu.VMEM((ns * requests * hr, padded), BF16),
            pltpu.VMEM((padded, cols), F32),
            pltpu.VMEM((ns, (requests + 2) * hr, HD), BF16),
            pltpu.VMEM((padded, HD), F32),
            pltpu.VMEM((cols, width), BF16),
            pltpu.VMEM((2, own_experts * fe, width // 2), BF16),
            pltpu.VMEM((2, own_experts * fe, width // 2), BF16),
            pltpu.VMEM((own_experts * fe, width), BF16),
            pltpu.VMEM((2, sf, width // 2), BF16),
            pltpu.VMEM((2, sf, width // 2), BF16),
            pltpu.VMEM((sf, width), BF16),
            pltpu.VMEM((ns, (requests + 2) * hr, HD), BF16),
            pltpu.VMEM((ROWS, width), F32),
            pltpu.VMEM((ne, ROWS, cols), BF16),
            pltpu.VMEM((ne, ROWS, cols), BF16),
            pltpu.VMEM((2, total_rows, nz * cols), BF16),
            pltpu.VMEM((2, total_rows, own_experts * fe), F32),
            pltpu.VMEM((total_rows, own_experts * fe), F32),
            pltpu.VMEM((total_rows, HD), F32),
            pltpu.VMEM((2, nz, total_rows, cols), BF16),
            pltpu.VMEM((nz, total_rows, cols), BF16),
            pltpu.VMEM((total_rows, cols), F32),
            pltpu.VMEM((nz * total_rows, cols), BF16),
            pltpu.VMEM((ne, ROWS, cols), BF16),
            pltpu.VMEM((ne, ROWS, cols), BF16),
            dma((9,)), dma((3,)), dma((2, 4)), dma,
            dma, dma, dma, dma, dma, dma,
            dma((3 + 8 * nz,)),
            dma, dma, dma, dma, dma,
            dma((nz,)), dma((nz,)), dma((nz,)), dma((nz,)), dma((nz,)),
            dma, dma, dma, dma,
        ],
        compiler_params=pltpu.CompilerParams(collective_id=0, has_side_effects=True),
        name="layer",
    )(
        cache_lens, slot_request, slot_block, frequency, hidden_in, attn_gain[None, :],
        expert_ids, expert_weights, ffn_gain[None, :],
        query_weight, key_weight, value_weight, key_cache, value_cache, out_weight,
        jnp.swapaxes(gate_experts, 1, 2).reshape(own_experts * fe, width),
        jnp.swapaxes(up_experts, 1, 2).reshape(own_experts * fe, width),
        down_experts.reshape(own_experts * fe, width),
        gate_shared.T, up_shared.T, down_shared,
    )

    group = 8
    groups = -(-pool // group)
    key_out, value_out = pl.pallas_call(
        functools.partial(patch_kernel, requests=requests, steps=steps, group=group),
        out_shape=(
            jax.ShapeDtypeStruct(key_cache.shape, BF16),
            jax.ShapeDtypeStruct(value_cache.shape, BF16),
        ),
        in_specs=[smem, smem, smem, anys, anys, anys],
        out_specs=(anys, anys),
        scratch_shapes=[
            pltpu.VMEM(new_kv.shape, BF16),
            pltpu.VMEM(key_cache.shape, BF16),
            pltpu.VMEM(key_cache.shape, BF16),
            pltpu.VMEM((ns * requests, steps, 2 * cols), F32),
            dma,
            dma((2, groups)),
            dma((2, groups)),
        ],
        name="patch",
    )(slot_request, slot_block, cache_lens, new_kv, key_cache, value_cache)
    return (hidden_out, key_out, value_out)


def solution(mesh):
    in_specs = (
        P("seq", None, None),
        P(),
        P("seq"),
        P("seq"),
        P("seq", None, "exp"),
        P("seq", None, "exp"),
        P(),
        P(None, "exp"),
        P(None, "exp"),
        P(None, "exp"),
        P("exp", None),
        P(),
        P("seq", None, None),
        P("seq", None, None),
        P("seq", None, "exp"),
        P("seq", None, "exp"),
        P("seq", "exp", None),
        P(None, "exp"),
        P(None, "exp"),
        P("exp", None),
    )
    out_specs = (P("seq", None, "exp"), P("seq", None, "exp"), P("seq", None, "exp"))
    return jax.shard_map(body, mesh=mesh, in_specs=in_specs, out_specs=out_specs, check_vma=False)
```

```python
import functools
import math

import jax
import jax.numpy as jnp
import numpy as np
from jax import lax
from jax.experimental import pallas as pl
from jax.experimental.pallas import tpu as pltpu
from jax.sharding import PartitionSpec as P

HD = 128
MESH = pl.DeviceIdType.MESH
F32 = jnp.float32
BF16 = jnp.bfloat16
ROWS = 16


def peer(seq, exp):
    return {"seq": seq, "exp": exp}


def rows_of(ref, scratch):
    count, steps, _ = ref.shape
    for b in range(count):
        scratch[pl.ds(b * steps, steps), :] = ref[b]
    used = count * steps
    scratch[pl.ds(used, ROWS - used), :] = jnp.zeros((ROWS - used, ref.shape[2]), F32)


def far_first(i, side):
    if side == 4:
        return jnp.where(i == 0, 2, jnp.where(i == 1, 1, jnp.where(i == 2, 3, 0)))
    return side - 1 - i


def dot_t(a, b):
    return lax.dot_general(a, b, (((1,), (1,)), ((), ())), preferred_element_type=F32)


def split_two(values):
    high = values.astype(BF16)
    low = (values - high.astype(F32)).astype(BF16)
    return high, low


def layer_kernel(
    lens_any, req_any, blk_any, freq_any, hidden_any, again_any, ids_any, ew_any, fgain_any,
    wq_ref, wk_ref, wv_ref, key_ref, value_ref,
    wo_ref, ge_ref, ue_ref, de_ref, gs_ref, us_ref, ds_ref,
    out_ref, kv_ref,
    lens_ref, req_ref, blk_ref, freq_ref, hidden_ref, again_ref, ids_ref, ew_ref, fgain_ref,
    wbuf, qbuf, kvbuf, cbuf, coef, kbuf, vbuf, pick, gatherer, slots, part, found,
    wo, wg, wu, wd, sg, su, sd, rbuf, xs, terms, r3, xbuf, acc, routing, scales, ybuf, ypair, sums, r5, shared, r6,
    isem, asem, csem, ksem, qsend, qrecv, kvsend, kvrecv, cosend, corecv,
    wsem, send2, recv2, send3, recv3, send4, recv4, fsend, frecv, psend, precv, send5, recv5, send6, recv6,
):
    ns = lax.axis_size("seq")
    ne = lax.axis_size("exp")
    nz = ne // 2
    me = lax.axis_index("seq")
    exp = lax.axis_index("exp")
    z, core = exp // 2, exp % 2
    other = 1 - core
    twin = z * 2 + other
    requests, steps, width = hidden_ref.shape
    cols = wq_ref.shape[1]
    heads = cols // HD
    hr = heads * steps
    pool, block, _ = key_ref.shape
    experts = coef.shape[1] // 2
    own_experts = experts // ns
    fe = ge_ref.shape[0] // own_experts
    count = requests * steps
    total_rows = ns * ROWS

    side = math.isqrt(ns)

    def seq_far(i):
        x = (me // side + far_first(i // side % side, side)) % side
        y = (me % side + far_first(i % side, side)) % side
        return x * side + y

    def exp_far(i):
        return (z + far_first(i // 2, nz)) % nz * 2 + (core + 1 - i % 2) % 2

    barrier = pltpu.get_barrier_semaphore()

    def greet_seq(i, _):
        pl.semaphore_signal(barrier, inc=1, device_id=peer((me + i) % ns, exp), device_id_type=MESH)
        return 0

    def greet_exp(i, _):
        pl.semaphore_signal(barrier, inc=1, device_id=peer(me, (exp + i) % ne), device_id_type=MESH)
        return 0

    lax.fori_loop(1, ns, greet_seq, 0)
    lax.fori_loop(1, ne, greet_exp, 0)
    small = []
    pairs = (
        (hidden_any, hidden_ref), (again_any, again_ref), (lens_any, lens_ref),
        (freq_any, freq_ref), (ids_any, ids_ref), (ew_any, ew_ref), (req_any, req_ref),
        (blk_any, blk_ref), (fgain_any, fgain_ref),
    )
    for n, (source, buf) in enumerate(pairs):
        load = pltpu.make_async_copy(source, buf, isem.at[n])
        load.start()
        small.append(load)
    loads = []
    for k, w in enumerate((wq_ref, wk_ref, wv_ref)):
        load = pltpu.make_async_copy(w, wbuf.at[k], asem.at[k])
        load.start()
        loads.append(load)
    pieces = []
    chunk = -(-pool // 4)
    for g in range(4):
        span = pl.ds(g * chunk, min(chunk, pool - g * chunk))
        for n, (source, buf) in enumerate(((key_ref, kbuf), (value_ref, vbuf))):
            load = pltpu.make_async_copy(source.at[span], buf.at[span], csem.at[n, g])
            load.start()
            pieces.append(load)

    for load in small[:4]:
        load.wait()
    rows_of(hidden_ref, xs)
    x = xs[...]
    mean_square = jnp.mean(x * x, axis=-1, keepdims=True)
    normed = (x * lax.rsqrt(mean_square + 1e-06) * again_ref[...]).astype(BF16)
    row = lax.broadcasted_iota(jnp.int32, (ROWS, HD), 0)
    lane = lax.broadcasted_iota(jnp.int32, (ROWS, HD), 1)
    length = jnp.zeros((ROWS, HD), jnp.int32)
    for b in range(requests):
        length = jnp.where(row // steps == b, lens_ref[me * requests + b], length)
    position = (length + row % steps).astype(F32)
    angles = position * freq_ref[...]
    cosine = jnp.cos(angles)
    sine = jnp.sin(angles)
    sine = jnp.where(lane < HD // 2, -sine, sine)

    def rotate(v):
        parts = []
        for h in range(heads):
            one = v[:, h * HD : (h + 1) * HD]
            parts.append(one * cosine + pltpu.roll(one, HD // 2, 1) * sine)
        return jnp.concatenate(parts, axis=1)

    def push(src, dst, send, recv):
        def one(i, _):
            pltpu.make_async_remote_copy(
                src_ref=src, dst_ref=dst, send_sem=send, recv_sem=recv,
                device_id=peer(seq_far(i), exp), device_id_type=MESH,
            ).start()
            return 0

        lax.fori_loop(0, ns - 1, one, 0)

    def whole(ref, send, recv):
        return pltpu.make_async_remote_copy(
            src_ref=ref.at[pl.ds(0, ns - 1)], dst_ref=ref.at[pl.ds(0, ns - 1)],
            send_sem=send, recv_sem=recv,
            device_id=peer((me + 1) % ns, exp), device_id_type=MESH,
        )

    my_rows = pl.ds(pl.multiple_of(me * ROWS, ROWS), ROWS)
    loads[0].wait()
    own_q = rotate(jnp.dot(normed, wbuf[0], preferred_element_type=F32)).astype(BF16)
    qbuf[me] = own_q
    pl.semaphore_wait(barrier, ns - 1 + ne - 1)
    push(qbuf.at[me], qbuf.at[me], qsend, qrecv)
    loads[1].wait()
    own_k = rotate(jnp.dot(normed, wbuf[1], preferred_element_type=F32)).astype(BF16)
    kvbuf[:, 0:cols] = own_k
    loads[2].wait()
    own_v = jnp.dot(normed, wbuf[2], preferred_element_type=F32).astype(BF16)
    kvbuf[:, cols : 2 * cols] = own_v
    keep_kv = pltpu.make_async_copy(kvbuf, kv_ref.at[me], ksem)
    keep_kv.start()

    load_wo = pltpu.make_async_copy(wo_ref, wo, wsem.at[0])
    load_wo.start()
    gate_up, shared_in = [], []
    for n, (source, buf) in enumerate(((ge_ref, wg), (ue_ref, wu))):
        for c in range(2):
            for k in range(nz):
                load = pltpu.make_async_copy(
                    source.at[:, pl.ds((k * 2 + c) * cols, cols)],
                    buf.at[c, :, pl.ds(k * cols, cols)],
                    wsem.at[1 + (n * 2 + c) * nz + k],
                )
                load.start()
                gate_up.append(load)
    base = 1 + 4 * nz
    load_wd = pltpu.make_async_copy(de_ref, wd, wsem.at[base])
    load_wd.start()
    for n, (source, buf) in enumerate(((gs_ref, sg), (us_ref, su))):
        for c in range(2):
            for k in range(nz):
                load = pltpu.make_async_copy(
                    source.at[:, pl.ds((k * 2 + c) * cols, cols)],
                    buf.at[c, :, pl.ds(k * cols, cols)],
                    wsem.at[base + 1 + (n * 2 + c) * nz + k],
                )
                load.start()
                shared_in.append(load)
    load_sd = pltpu.make_async_copy(ds_ref, sd, wsem.at[base + 1 + 4 * nz])
    load_sd.start()

    for load in small[4:]:
        load.wait()
    coef[...] = jnp.zeros(coef.shape, F32)
    expert = lax.broadcasted_iota(jnp.int32, (steps, experts), 1)
    for b in range(requests):
        total = jnp.zeros((steps, experts), F32)
        for j in range(ids_ref.shape[2]):
            total += jnp.where(ids_ref[b][:, j : j + 1] == expert, ew_ref[b][:, j : j + 1], 0.0)
        coef[pl.ds(b * steps, steps), pl.ds(0, experts)] = total
    high, low = split_two(coef[:, 0:experts])
    cbuf[me] = jnp.concatenate([high, low], axis=1)

    scalars = []
    prow = lax.broadcasted_iota(jnp.int32, (hr, total_rows), 0)
    pcol = lax.broadcasted_iota(jnp.int32, (hr, total_rows), 1)
    padded = pick.shape[0]
    scol = lax.broadcasted_iota(jnp.int32, (1, padded), 1)
    of_slot = jnp.full((1, padded), -1, jnp.int32)
    for s in range(padded // hr):
        if s < pool:
            request = req_ref[s]
            held = jnp.maximum(request, 0)
            edge = jnp.where(request >= 0, lens_ref[held] - blk_ref[s] * block, -1)
            first = held // requests * ROWS + held % requests * steps
            first = jnp.where(request >= 0, first, -steps)
            scalars.append((request, edge))
            chosen = (pcol - first == prow % steps) & (pcol >= first) & (first >= 0)
            of_slot = jnp.where(scol // hr == s, request, of_slot)
            pick[s * hr : (s + 1) * hr, :] = jnp.where(chosen, 1.0, 0.0)
        else:
            pick[s * hr : (s + 1) * hr, :] = jnp.zeros((hr, total_rows), F32)
    grow = lax.broadcasted_iota(jnp.int32, gatherer.shape, 0)
    gcol = lax.broadcasted_iota(jnp.int32, gatherer.shape, 1)
    gatherer[...] = jnp.where(
        (grow // hr == of_slot) & (grow % hr == gcol % hr), 1.0, 0.0
    ).astype(BF16)

    scale = 1.0 / math.sqrt(HD)
    nrow = lax.broadcasted_iota(jnp.int32, (requests * hr, ROWS), 0)
    ncol = lax.broadcasted_iota(jnp.int32, (requests * hr, ROWS), 1)
    b_of, t_of = nrow // hr, nrow % steps
    spread = jnp.where(ncol == b_of * steps + t_of, 1.0, 0.0).astype(BF16)
    hrow = lax.broadcasted_iota(jnp.int32, (requests * hr, cols), 0) % hr // steps
    hcol = lax.broadcasted_iota(jnp.int32, (requests * hr, cols), 1) // HD
    mine = jnp.where(
        hrow == hcol, jnp.dot(spread, own_q, preferred_element_type=F32), 0.0
    ).astype(BF16)
    scores = dot_t(mine, own_k) * scale
    seen = (ncol // steps == b_of) & (ncol % steps <= t_of) & (ncol < count)
    new_top = jnp.max(jnp.where(seen, scores, -1e30), axis=-1, keepdims=True)
    weights = jnp.where(seen, jnp.exp(scores - new_top), 0.0)
    new_total = jnp.sum(weights, axis=-1, keepdims=True)
    new_full = jnp.dot(weights.astype(BF16), own_v, preferred_element_type=F32)
    new_out = new_full[:, 0:HD]
    half = lax.broadcasted_iota(jnp.int32, (requests * hr, HD), 0) % hr // steps
    for h in range(1, heads):
        new_out = jnp.where(half == h, new_full[:, h * HD : (h + 1) * HD], new_out)

    all_q = whole(qbuf, qsend, qrecv)
    all_q.wait_recv()
    frow = lax.broadcasted_iota(jnp.int32, (padded, cols), 0) % hr // steps
    fcol = lax.broadcasted_iota(jnp.int32, (padded, cols), 1) // HD
    everyone = qbuf[...].reshape(total_rows, cols)
    slots[...] = jnp.where(
        frow == fcol, jnp.dot(pick[...].astype(BF16), everyone, preferred_element_type=F32), 0.0
    )
    for piece in pieces:
        piece.wait()
    slane = lax.broadcasted_iota(jnp.int32, (hr, HD), 1)
    klane = lax.broadcasted_iota(jnp.int32, (hr, block), 1)
    upper = lax.broadcasted_iota(jnp.int32, (hr, HD), 0) // steps
    top = jnp.full((hr, HD), -1e30, F32)
    all_scores = []
    for s in range(pool):
        request, edge = scalars[s]
        scores = dot_t(slots[s * hr : (s + 1) * hr, :].astype(BF16), kbuf[s]) * scale
        scores = jnp.where(klane < edge, scores, -1e30)
        all_scores.append(scores)
        best = jnp.max(scores, axis=-1, keepdims=True)
        top = jnp.maximum(top, jnp.where(slane == request, best, -1e30))
    top = top.astype(BF16).astype(F32)
    total = jnp.zeros((hr, HD), F32)
    for s in range(pool):
        request, edge = scalars[s]
        best = jnp.max(jnp.where(slane == request, top, -1e30), axis=-1, keepdims=True)
        weights = jnp.where(klane < edge, jnp.exp(all_scores[s] - best), 0.0)
        total += jnp.where(slane == request, jnp.sum(weights, axis=-1, keepdims=True), 0.0)
        full = jnp.dot(weights.astype(BF16), vbuf[s], preferred_element_type=F32)
        out = full[:, 0:HD]
        for h in range(1, heads):
            out = jnp.where(upper == h, full[:, h * HD : (h + 1) * HD], out)
        found[s * hr : (s + 1) * hr, :] = out
    if padded > pool * hr:
        found[pool * hr :, :] = jnp.zeros((padded - pool * hr, HD), F32)
    high, low = split_two(found[...])
    by_request = jnp.dot(gatherer[...], high, preferred_element_type=F32) + jnp.dot(
        gatherer[...], low, preferred_element_type=F32
    )
    high, low = split_two(pltpu.roll(total, HD // 2, 1))
    stats = jnp.concatenate(
        [jnp.where(slane < HD // 2, top, high.astype(F32)), low.astype(F32)], axis=0
    ).astype(BF16)
    by_request = by_request.astype(BF16)
    for d in range(ns):
        part[d, 0 : requests * hr, :] = by_request[d * requests * hr : (d + 1) * requests * hr, :]
        part[d, requests * hr :, :] = stats
    rbuf[me] = part[me]

    def push2(i, _):
        to = seq_far(i)
        pltpu.make_async_remote_copy(
            src_ref=part.at[to], dst_ref=rbuf.at[me], send_sem=send2, recv_sem=recv2,
            device_id=peer(to, exp), device_id_type=MESH,
        ).start()
        return 0

    lax.fori_loop(0, ns - 1, push2, 0)
    all2 = whole(part, send2, recv2)
    all2.wait_recv()

    shift = (HD - me * requests) % HD
    sums_of, tops = [], []
    for s in range(ns):
        stats = rbuf[s, requests * hr :, :].astype(F32)
        low = jnp.where(slane < HD // 2, 0.0, stats[hr:])
        tops.append(pltpu.roll(stats[0:hr] + low, shift, 1))
    fresh = jnp.full((hr, HD), -1e30, F32)
    for b in range(requests):
        rows = slice(b * hr, (b + 1) * hr)
        fresh = jnp.where(slane == b, new_top[rows], fresh)
        fresh = jnp.where(slane == HD // 2 + b, new_total[rows], fresh)
    tops.append(fresh)
    best = tops[0]
    for s in range(1, ns + 1):
        best = jnp.maximum(best, tops[s])
    factors, total = [], jnp.zeros((hr, HD), F32)
    for s in range(ns + 1):
        factor = jnp.exp(jnp.where(slane < requests, tops[s] - best, 0.0))
        factors.append(factor)
        total += pltpu.roll(tops[s], HD // 2, 1) * factor
    held = [rbuf[s, 0 : requests * hr, :].astype(F32) for s in range(ns)]
    attended = []
    for b in range(requests):
        rows = slice(b * hr, (b + 1) * hr)
        summed = new_out[rows] * factors[ns][:, b : b + 1]
        for s in range(ns):
            summed += held[s][rows] * factors[s][:, b : b + 1]
        attended.append(summed / total[:, b : b + 1])
    stacked = jnp.concatenate(attended, axis=0).astype(BF16)
    prow = lax.broadcasted_iota(jnp.int32, (ROWS, requests * hr), 0)
    pcol = lax.broadcasted_iota(jnp.int32, (ROWS, requests * hr), 1)
    by_head = []
    for h in range(cols // HD):
        pick = (pcol == prow // steps * hr + h * steps + prow % steps) & (prow < count)
        by_head.append(
            jnp.dot(
                jnp.where(pick, 1.0, 0.0).astype(BF16), stacked, preferred_element_type=F32
            ).astype(BF16)
        )
    own = jnp.concatenate(by_head, axis=1)
    load_wo.wait()
    for e in range(ne):
        terms[e] = jnp.dot(
            own, wo[:, e * cols : (e + 1) * cols], preferred_element_type=F32
        ).astype(BF16)

    def push3(i, _):
        to = exp_far(i)
        pltpu.make_async_remote_copy(
            src_ref=terms.at[to], dst_ref=r3.at[exp], send_sem=send3, recv_sem=recv3,
            device_id=peer(me, to), device_id_type=MESH,
        ).start()
        return 0

    lax.fori_loop(0, ne - 1, push3, 0)
    push(cbuf.at[me], cbuf.at[me], cosend, corecv)
    push(kvbuf, kv_ref.at[me], kvsend, kvrecv)
    r3[exp] = terms[exp]
    all3 = pltpu.make_async_remote_copy(
        src_ref=terms.at[pl.ds(0, ne - 1)], dst_ref=r3.at[pl.ds(0, ne - 1)],
        send_sem=send3, recv_sem=recv3, device_id=peer(me, (exp + 1) % ne), device_id_type=MESH,
    )
    all3.wait_recv()
    residual = xs[:, pl.ds(pl.multiple_of(exp * cols, cols), cols)]
    for e in range(ne):
        residual += r3[e].astype(F32)

    scaled = residual * fgain_ref[:, pl.ds(pl.multiple_of(exp * cols, cols), cols)]
    square = jnp.sum(residual * residual, axis=-1, keepdims=True)
    brow = lax.broadcasted_iota(jnp.int32, (ROWS, cols), 0)
    blane = lax.broadcasted_iota(jnp.int32, (ROWS, cols), 1)
    line = jnp.sum(jnp.where(brow == blane, square, 0.0), axis=0, keepdims=True)
    high, low = split_two(line)
    scaled = jnp.where(brow == count, high.astype(F32), scaled)
    scaled = jnp.where(brow == count + 1, low.astype(F32), scaled)
    my_cols = pl.ds(pl.multiple_of(z * cols, cols), cols)
    back = pl.ds(pl.multiple_of((z * ns + me) * ROWS, ROWS), ROWS)
    xbuf[core, my_rows, my_cols] = scaled.astype(BF16)

    def push4(i, _):
        there = (z + far_first(i // ns, nz)) % nz * 2 + core
        pltpu.make_async_remote_copy(
            src_ref=xbuf.at[core, my_rows, my_cols], dst_ref=xbuf.at[core, my_rows, my_cols],
            send_sem=send4, recv_sem=recv4.at[z],
            device_id=peer(seq_far(i), there), device_id_type=MESH,
        ).start()
        return 0

    lax.fori_loop(0, nz * ns - 1, push4, 0)

    all_c = whole(cbuf, cosend, corecv)
    all_c.wait_recv()
    coefs = cbuf[...].reshape(total_rows, 2 * experts).astype(F32)
    clane = lax.broadcasted_iota(jnp.int32, (total_rows, 2 * experts), 1)
    ucol = lax.broadcasted_iota(jnp.int32, (total_rows, wd.shape[0]), 1)
    routing[...] = jnp.zeros(routing.shape, F32)
    for j in range(own_experts):
        mine = me * own_experts + j
        weight = jnp.sum(
            jnp.where((clane == mine) | (clane == mine + experts), coefs, 0.0), axis=-1, keepdims=True
        )
        routing[...] += jnp.where((ucol >= j * fe) & (ucol < (j + 1) * fe), weight, 0.0)

    arrival = [(z + nz - far_first(i, nz)) % nz for i in range(nz)]
    forwards = []
    for i in range(nz):
        k = arrival[i]
        span = pl.ds(0, total_rows - (ROWS if i == nz - 1 else 0))
        kcols = pl.ds(pl.multiple_of(k * cols, cols), cols)
        pltpu.make_async_remote_copy(
            src_ref=xbuf.at[core, span, kcols], dst_ref=xbuf.at[core, span, kcols],
            send_sem=send4, recv_sem=recv4.at[k], device_id=peer(me, twin), device_id_type=MESH,
        ).wait_recv()
        forward = pltpu.make_async_remote_copy(
            src_ref=xbuf.at[core, :, kcols], dst_ref=xbuf.at[core, :, kcols],
            send_sem=fsend.at[k], recv_sem=frecv.at[k], device_id=peer(me, twin), device_id_type=MESH,
        )
        forward.start()
        forwards.append(forward)

    for load in gate_up:
        load.wait()
    acc[0] = dot_t(xbuf[core], wg[core])
    acc[1] = dot_t(xbuf[core], wu[core])

    trow = lax.broadcasted_iota(jnp.int32, (total_rows, total_rows), 0)
    tcol = lax.broadcasted_iota(jnp.int32, (total_rows, total_rows), 1)
    spread = (trow // ROWS == tcol // ROWS) & ((tcol % ROWS == count) | (tcol % ROWS == count + 1))
    spread = jnp.where(spread, 1.0, 0.0).astype(BF16)

    def squares(c):
        value = xbuf[c, :, 0:HD].astype(F32)
        for k in range(1, nz):
            value += xbuf[c, :, k * cols : k * cols + HD].astype(F32)
        return value

    first = squares(core)
    for i in range(nz):
        k = arrival[i]
        kcols = pl.ds(pl.multiple_of(k * cols, cols), cols)
        pltpu.make_async_remote_copy(
            src_ref=xbuf.at[other, :, kcols], dst_ref=xbuf.at[other, :, kcols],
            send_sem=fsend.at[k], recv_sem=frecv.at[k], device_id=peer(me, twin), device_id_type=MESH,
        ).wait_recv()
    high, low = split_two(first + squares(other))
    square = jnp.dot(spread, high, preferred_element_type=F32) + jnp.dot(
        spread, low, preferred_element_type=F32
    )
    lrow = lax.broadcasted_iota(jnp.int32, (total_rows, HD), 0)
    llane = lax.broadcasted_iota(jnp.int32, (total_rows, HD), 1)
    square = jnp.sum(jnp.where(lrow % ROWS == llane, square, 0.0), axis=-1, keepdims=True)
    row_scale = lax.rsqrt(square / width + 1e-06)
    scales[...] = jnp.broadcast_to(row_scale, scales.shape)
    gate = (acc[0] + dot_t(xbuf[other], wg[other])) * row_scale
    up = (acc[1] + dot_t(xbuf[other], wu[other])) * row_scale
    inner = (jax.nn.silu(gate) * up * routing[...]).astype(BF16)
    load_wd.wait()

    def down(e):
        where = pl.ds(pl.multiple_of(e * cols, cols), cols)
        return jnp.dot(inner, wd[:, where], preferred_element_type=F32)

    pairs = []

    def give(i):
        k = (z + far_first(i, nz)) % nz
        ybuf[other, k] = down(k * 2 + other).astype(BF16)
        pair = pltpu.make_async_remote_copy(
            src_ref=ybuf.at[other, k], dst_ref=ypair.at[k],
            send_sem=psend.at[k], recv_sem=precv.at[k], device_id=peer(me, twin), device_id_type=MESH,
        )
        pair.start()
        pairs.append(pair)

    give(0)
    give(1)
    for i in range(nz):
        k = (z + far_first(i, nz)) % nz
        if i + 2 < nz:
            give(i + 2)
        sums[...] = down(k * 2 + core)
        pairs[i].wait_recv()
        ybuf[core, k] = (sums[...] + ypair[k].astype(F32)).astype(BF16)

        def push5(n, _):
            to = seq_far(n)
            there = pl.ds(pl.multiple_of(to * ROWS, ROWS), ROWS)
            pltpu.make_async_remote_copy(
                src_ref=ybuf.at[core, k, there, :], dst_ref=r5.at[back, :],
                send_sem=send5, recv_sem=recv5,
                device_id=peer(to, k * 2 + core), device_id_type=MESH,
            ).start()
            return 0

        lax.fori_loop(0, ns - 1 if i == nz - 1 else ns, push5, 0)
    r5[back, :] = ybuf[core, z, my_rows, :]

    for load in shared_in:
        load.wait()
    load_sd.wait()
    gate = jnp.zeros((ROWS, sg.shape[1]), F32)
    up = jnp.zeros((ROWS, sg.shape[1]), F32)
    for c in range(2):
        rows = xbuf[c, my_rows, :]
        gate += dot_t(rows, sg[c])
        up += dot_t(rows, su[c])
    own_scale = scales[my_rows, 0:1]
    gate, up = gate * own_scale, up * own_scale
    inner = jnp.where(
        lax.broadcasted_iota(jnp.int32, gate.shape, 0) < count, jax.nn.silu(gate) * up, 0.0
    ).astype(BF16)
    for e in range(ne):
        shared[e] = jnp.dot(
            inner, sd[:, e * cols : (e + 1) * cols], preferred_element_type=F32
        ).astype(BF16)

    def push6(i, _):
        to = exp_far(i)
        pltpu.make_async_remote_copy(
            src_ref=shared.at[to], dst_ref=r6.at[exp], send_sem=send6, recv_sem=recv6,
            device_id=peer(me, to), device_id_type=MESH,
        ).start()
        return 0

    lax.fori_loop(0, ne - 1, push6, 0)
    r6[exp] = shared[exp]
    all6 = pltpu.make_async_remote_copy(
        src_ref=shared.at[pl.ds(0, ne - 1)], dst_ref=r6.at[pl.ds(0, ne - 1)],
        send_sem=send6, recv_sem=recv6, device_id=peer(me, (exp + 1) % ne), device_id_type=MESH,
    )
    all6.wait_recv()
    result = residual
    for e in range(ne):
        result += r6[e].astype(F32)

    rest = pl.ds(0, (nz * ns - 1) * ROWS)
    all5 = pltpu.make_async_remote_copy(
        src_ref=r5.at[rest, :], dst_ref=r5.at[rest, :],
        send_sem=send5, recv_sem=recv5, device_id=peer(me, twin), device_id_type=MESH,
    )
    all5.wait_recv()
    for k in range(nz * ns):
        result += r5[k * ROWS : (k + 1) * ROWS, :].astype(F32)
    for b in range(requests):
        out_ref[b] = result[b * steps : (b + 1) * steps, :]

    all_kv = whole(kv_ref, kvsend, kvrecv)
    all_kv.wait_recv()
    all_kv.wait_send()
    keep_kv.wait()
    all_q.wait_send()
    all_c.wait_send()
    all2.wait_send()
    all3.wait_send()
    all5.wait_send()
    all6.wait_send()
    pltpu.make_async_remote_copy(
        src_ref=r5.at[rest, :], dst_ref=r5.at[rest, :],
        send_sem=send4, recv_sem=recv4.at[0], device_id=peer(me, twin), device_id_type=MESH,
    ).wait_send()
    for i in range(nz):
        forwards[i].wait_send()
        pairs[i].wait_send()


def patch_kernel(
    req_ref, blk_ref, lens_ref, kv_ref, hidden_ref, key_ref, value_ref,
    key_out, value_out, hidden_out, kbuf, vbuf, fresh_rows, in_sem, out_sem,
    *, requests, steps, group,
):
    pool, block, cols = key_ref.shape
    ns = kv_ref.shape[0]
    starts = list(range(0, pool, group))
    sizes = [min(group, pool - s) for s in starts]

    def copies(g, into):
        span = pl.ds(starts[g], sizes[g])
        pairs = ((key_ref, kbuf, key_out), (value_ref, vbuf, value_out))
        result = []
        for n, (source, buf, target) in enumerate(pairs):
            if into:
                result.append(pltpu.make_async_copy(source.at[span], buf.at[span], in_sem.at[n, g]))
            else:
                result.append(pltpu.make_async_copy(buf.at[span], target.at[span], out_sem.at[n, g]))
        return result

    for g in range(len(starts)):
        for c in copies(g, True):
            c.start()
    hidden_out[...] = hidden_ref[...]
    for s in range(ns):
        kv = kv_ref[s].astype(F32)
        for b in range(requests):
            fresh_rows[s * requests + b] = kv[b * steps : (b + 1) * steps, :]
    window = 2 * ROWS
    wrow = lax.broadcasted_iota(jnp.int32, (window, cols), 0)
    for g in range(len(starts)):
        for c in copies(g, True):
            c.wait()

        def patch(i, _):
            s = starts[g] + i
            request = jnp.maximum(req_ref[s], 0)
            offset = lens_ref[request] - blk_ref[s] * block

            @pl.when((req_ref[s] >= 0) & (offset > -steps) & (offset < block))
            def _():
                first = jnp.clip(offset // ROWS * ROWS, 0, block - window)
                first = pl.multiple_of(first, ROWS)
                rel = wrow + first - offset
                for n, buf in enumerate((kbuf, vbuf)):
                    tile = buf[s, pl.ds(first, window), :].astype(F32)
                    for t in range(steps):
                        one = fresh_rows[request, t : t + 1, n * cols : (n + 1) * cols]
                        tile = jnp.where(rel == t, one, tile)
                    buf[s, pl.ds(first, window), :] = tile.astype(BF16)

            return 0

        lax.fori_loop(0, sizes[g], patch, 0)
        for c in copies(g, False):
            c.start()
    for g in range(len(starts)):
        for c in copies(g, False):
            c.wait()


def body(
    hidden_in, cache_lens, slot_request, slot_block, key_cache, value_cache, attn_gain,
    query_weight, key_weight, value_weight, out_weight, ffn_gain, expert_ids, expert_weights,
    gate_experts, up_experts, down_experts, gate_shared, up_shared, down_shared,
):
    requests, steps, width = hidden_in.shape
    ns = lax.axis_size("seq")
    ne = lax.axis_size("exp")
    nz = ne // 2
    cols = query_weight.shape[1]
    own_experts, _, fe = gate_experts.shape
    sf = gate_shared.shape[1]
    experts = own_experts * ns
    pool, block, _ = key_cache.shape
    hr = cols // HD * steps
    total_rows = ns * ROWS
    padded = -(-pool * hr // 128) * 128

    exponent = np.arange(HD // 2) * (2.0 / HD)
    frequency = np.power(10000.0, -exponent).astype(np.float32)
    frequency = jnp.asarray(np.concatenate([frequency, frequency])[None, :])

    vmem = pl.BlockSpec(memory_space=pltpu.VMEM)
    smem = pl.BlockSpec(memory_space=pltpu.SMEM)
    anys = pl.BlockSpec(memory_space=pl.ANY)
    dma = pltpu.SemaphoreType.DMA

    hidden, new_kv = pl.pallas_call(
        layer_kernel,
        out_shape=(
            jax.ShapeDtypeStruct((requests, steps, cols), F32),
            jax.ShapeDtypeStruct((ns, ROWS, 2 * cols), BF16),
        ),
        in_specs=[anys] * 21,
        out_specs=(vmem, anys),
        scratch_shapes=[
            pltpu.SMEM(cache_lens.shape, jnp.int32),
            pltpu.SMEM(slot_request.shape, jnp.int32),
            pltpu.SMEM(slot_block.shape, jnp.int32),
            pltpu.VMEM((1, HD), F32),
            pltpu.VMEM(hidden_in.shape, F32),
            pltpu.VMEM((1, width), F32),
            pltpu.VMEM(expert_ids.shape, jnp.int32),
            pltpu.VMEM(expert_weights.shape, F32),
            pltpu.VMEM((1, width), F32),
            pltpu.VMEM((3, width, cols), BF16),
            pltpu.VMEM((ns, ROWS, cols), BF16),
            pltpu.VMEM((ROWS, 2 * cols), BF16),
            pltpu.VMEM((ns, ROWS, 2 * experts), BF16),
            pltpu.VMEM((ROWS, 2 * experts), F32),
            pltpu.VMEM(key_cache.shape, BF16),
            pltpu.VMEM(key_cache.shape, BF16),
            pltpu.VMEM((padded, total_rows), F32),
            pltpu.VMEM((ns * requests * hr, padded), BF16),
            pltpu.VMEM((padded, cols), F32),
            pltpu.VMEM((ns, (requests + 2) * hr, HD), BF16),
            pltpu.VMEM((padded, HD), F32),
            pltpu.VMEM((cols, width), BF16),
            pltpu.VMEM((2, own_experts * fe, width // 2), BF16),
            pltpu.VMEM((2, own_experts * fe, width // 2), BF16),
            pltpu.VMEM((own_experts * fe, width), BF16),
            pltpu.VMEM((2, sf, width // 2), BF16),
            pltpu.VMEM((2, sf, width // 2), BF16),
            pltpu.VMEM((sf, width), BF16),
            pltpu.VMEM((ns, (requests + 2) * hr, HD), BF16),
            pltpu.VMEM((ROWS, width), F32),
            pltpu.VMEM((ne, ROWS, cols), BF16),
            pltpu.VMEM((ne, ROWS, cols), BF16),
            pltpu.VMEM((2, total_rows, nz * cols), BF16),
            pltpu.VMEM((2, total_rows, own_experts * fe), F32),
            pltpu.VMEM((total_rows, own_experts * fe), F32),
            pltpu.VMEM((total_rows, HD), F32),
            pltpu.VMEM((2, nz, total_rows, cols), BF16),
            pltpu.VMEM((nz, total_rows, cols), BF16),
            pltpu.VMEM((total_rows, cols), F32),
            pltpu.VMEM((nz * total_rows, cols), BF16),
            pltpu.VMEM((ne, ROWS, cols), BF16),
            pltpu.VMEM((ne, ROWS, cols), BF16),
            dma((9,)), dma((3,)), dma((2, 4)), dma,
            dma, dma, dma, dma, dma, dma,
            dma((3 + 8 * nz,)),
            dma, dma, dma, dma, dma,
            dma((nz,)), dma((nz,)), dma((nz,)), dma((nz,)), dma((nz,)),
            dma, dma, dma, dma,
        ],
        compiler_params=pltpu.CompilerParams(collective_id=0, has_side_effects=True),
        name="layer",
    )(
        cache_lens, slot_request, slot_block, frequency, hidden_in, attn_gain[None, :],
        expert_ids, expert_weights, ffn_gain[None, :],
        query_weight, key_weight, value_weight, key_cache, value_cache, out_weight,
        jnp.swapaxes(gate_experts, 1, 2).reshape(own_experts * fe, width),
        jnp.swapaxes(up_experts, 1, 2).reshape(own_experts * fe, width),
        down_experts.reshape(own_experts * fe, width),
        gate_shared.T, up_shared.T, down_shared,
    )

    group = 8
    groups = -(-pool // group)
    key_out, value_out, hidden_out = pl.pallas_call(
        functools.partial(patch_kernel, requests=requests, steps=steps, group=group),
        out_shape=(
            jax.ShapeDtypeStruct(key_cache.shape, BF16),
            jax.ShapeDtypeStruct(value_cache.shape, BF16),
            jax.ShapeDtypeStruct(hidden.shape, F32),
        ),
        in_specs=[smem, smem, smem, vmem, vmem, anys, anys],
        out_specs=(anys, anys, vmem),
        scratch_shapes=[
            pltpu.VMEM(key_cache.shape, BF16),
            pltpu.VMEM(key_cache.shape, BF16),
            pltpu.VMEM((ns * requests, steps, 2 * cols), F32),
            dma((2, groups)),
            dma((2, groups)),
        ],
        name="patch",
    )(slot_request, slot_block, cache_lens, new_kv, hidden, key_cache, value_cache)
    return (hidden_out, key_out, value_out)


def solution(mesh):
    in_specs = (
        P("seq", None, None),
        P(),
        P("seq"),
        P("seq"),
        P("seq", None, "exp"),
        P("seq", None, "exp"),
        P(),
        P(None, "exp"),
        P(None, "exp"),
        P(None, "exp"),
        P("exp", None),
        P(),
        P("seq", None, None),
        P("seq", None, None),
        P("seq", None, "exp"),
        P("seq", None, "exp"),
        P("seq", "exp", None),
        P(None, "exp"),
        P(None, "exp"),
        P("exp", None),
    )
    out_specs = (P("seq", None, "exp"), P("seq", None, "exp"), P("seq", None, "exp"))
    return jax.shard_map(body, mesh=mesh, in_specs=in_specs, out_specs=out_specs, check_vma=False)
```

```python
import functools
import math

import jax
import jax.numpy as jnp
import numpy as np
from jax import lax
from jax.experimental import pallas as pl
from jax.experimental.pallas import tpu as pltpu
from jax.sharding import PartitionSpec as P

HD = 128
MESH = pl.DeviceIdType.MESH
F32 = jnp.float32
BF16 = jnp.bfloat16
ROWS = 16


def peer(seq, exp):
    return {"seq": seq, "exp": exp}


def rows_of(ref, scratch):
    count, steps, _ = ref.shape
    for b in range(count):
        scratch[pl.ds(b * steps, steps), :] = ref[b]
    used = count * steps
    scratch[pl.ds(used, ROWS - used), :] = jnp.zeros((ROWS - used, ref.shape[2]), F32)


def far_first(i, side):
    if side == 4:
        return jnp.where(i == 0, 2, jnp.where(i == 1, 1, jnp.where(i == 2, 3, 0)))
    return side - 1 - i


def packed(value, blocks):
    value = value.reshape(blocks, ROWS, value.shape[1])
    half = value.shape[2] // 2
    left, right = value[:, 8:, :half], value[:, 8:, half:]
    row = lax.broadcasted_iota(jnp.int32, left.shape, 1)
    tail = jnp.where(row < 4, left, pltpu.roll(right, 4, 1))
    return jnp.concatenate([value[:, :8, :], tail], axis=2)


def dot_t(a, b):
    return lax.dot_general(a, b, (((1,), (1,)), ((), ())), preferred_element_type=F32)


def split_two(values):
    high = values.astype(BF16)
    low = (values - high.astype(F32)).astype(BF16)
    return high, low


def layer_kernel(
    lens_any, req_any, blk_any, freq_any, hidden_any, again_any, ids_any, ew_any, fgain_any,
    wq_ref, wk_ref, wv_ref, key_ref, value_ref,
    wo_ref, ge_ref, ue_ref, de_ref, gs_ref, us_ref, ds_ref,
    out_ref, kv_ref,
    lens_ref, req_ref, blk_ref, freq_ref, hidden_ref, again_ref, ids_ref, ew_ref, fgain_ref,
    wbuf, qbuf, kvbuf, cbuf, coef, kbuf, vbuf, pick, gatherer, slots, part, found,
    wo, wg, wu, wd, sg, su, sd, rbuf, xs, terms, r3, xbuf, acc, routing, scales, ybuf, ypair, sums, r5, shared, r6,
    isem, asem, csem, ksem, qsend, qrecv, kvsend, kvrecv, cosend, corecv,
    wsem, send2, recv2, send3, recv3, send4, recv4, fsend, frecv, psend, precv, send5, recv5, send6, recv6,
):
    ns = lax.axis_size("seq")
    ne = lax.axis_size("exp")
    nz = ne // 2
    me = lax.axis_index("seq")
    exp = lax.axis_index("exp")
    z, core = exp // 2, exp % 2
    other = 1 - core
    twin = z * 2 + other
    requests, steps, width = hidden_ref.shape
    cols = wq_ref.shape[1]
    heads = cols // HD
    hr = heads * steps
    pool, block, _ = key_ref.shape
    experts = coef.shape[1] // 2
    own_experts = experts // ns
    fe = ge_ref.shape[0] // own_experts
    count = requests * steps
    total_rows = ns * ROWS

    side = math.isqrt(ns)

    def seq_far(i):
        x = (me // side + far_first(i // side % side, side)) % side
        y = (me % side + far_first(i % side, side)) % side
        return x * side + y

    def exp_far(i):
        return (z + far_first(i // 2, nz)) % nz * 2 + (core + 1 - i % 2) % 2

    barrier = pltpu.get_barrier_semaphore()

    def greet_seq(i, _):
        pl.semaphore_signal(barrier, inc=1, device_id=peer((me + i) % ns, exp), device_id_type=MESH)
        return 0

    def greet_exp(i, _):
        pl.semaphore_signal(barrier, inc=1, device_id=peer(me, (exp + i) % ne), device_id_type=MESH)
        return 0

    lax.fori_loop(1, ns, greet_seq, 0)
    lax.fori_loop(1, ne, greet_exp, 0)
    small = []
    pairs = (
        (hidden_any, hidden_ref), (again_any, again_ref), (lens_any, lens_ref),
        (freq_any, freq_ref), (ids_any, ids_ref), (ew_any, ew_ref), (req_any, req_ref),
        (blk_any, blk_ref), (fgain_any, fgain_ref),
    )
    for n, (source, buf) in enumerate(pairs):
        load = pltpu.make_async_copy(source, buf, isem.at[n])
        load.start()
        small.append(load)
    loads = []
    for k, w in enumerate((wq_ref, wk_ref, wv_ref)):
        load = pltpu.make_async_copy(w, wbuf.at[k], asem.at[k])
        load.start()
        loads.append(load)
    pieces = []
    chunk = -(-pool // 4)
    for g in range(4):
        span = pl.ds(g * chunk, min(chunk, pool - g * chunk))
        for n, (source, buf) in enumerate(((key_ref, kbuf), (value_ref, vbuf))):
            load = pltpu.make_async_copy(source.at[span], buf.at[span], csem.at[n, g])
            load.start()
            pieces.append(load)

    for load in small[:4]:
        load.wait()
    rows_of(hidden_ref, xs)
    x = xs[...]
    mean_square = jnp.mean(x * x, axis=-1, keepdims=True)
    normed = (x * lax.rsqrt(mean_square + 1e-06) * again_ref[...]).astype(BF16)
    row = lax.broadcasted_iota(jnp.int32, (ROWS, HD), 0)
    lane = lax.broadcasted_iota(jnp.int32, (ROWS, HD), 1)
    length = jnp.zeros((ROWS, HD), jnp.int32)
    for b in range(requests):
        length = jnp.where(row // steps == b, lens_ref[me * requests + b], length)
    position = (length + row % steps).astype(F32)
    angles = position * freq_ref[...]
    cosine = jnp.cos(angles)
    sine = jnp.sin(angles)
    sine = jnp.where(lane < HD // 2, -sine, sine)

    def rotate(v):
        parts = []
        for h in range(heads):
            one = v[:, h * HD : (h + 1) * HD]
            parts.append(one * cosine + pltpu.roll(one, HD // 2, 1) * sine)
        return jnp.concatenate(parts, axis=1)

    def push(src, dst, send, recv):
        def one(i, _):
            pltpu.make_async_remote_copy(
                src_ref=src, dst_ref=dst, send_sem=send, recv_sem=recv,
                device_id=peer(seq_far(i), exp), device_id_type=MESH,
            ).start()
            return 0

        lax.fori_loop(0, ns - 1, one, 0)

    def whole(ref, send, recv):
        return pltpu.make_async_remote_copy(
            src_ref=ref.at[pl.ds(0, ns - 1)], dst_ref=ref.at[pl.ds(0, ns - 1)],
            send_sem=send, recv_sem=recv,
            device_id=peer((me + 1) % ns, exp), device_id_type=MESH,
        )

    my_rows = pl.ds(pl.multiple_of(me * ROWS, ROWS), ROWS)
    loads[0].wait()
    own_q = rotate(jnp.dot(normed, wbuf[0], preferred_element_type=F32)).astype(BF16)
    qbuf[me] = own_q
    pl.semaphore_wait(barrier, ns - 1 + ne - 1)
    push(qbuf.at[me], qbuf.at[me], qsend, qrecv)
    loads[1].wait()
    own_k = rotate(jnp.dot(normed, wbuf[1], preferred_element_type=F32)).astype(BF16)
    kvbuf[:, 0:cols] = own_k
    loads[2].wait()
    own_v = jnp.dot(normed, wbuf[2], preferred_element_type=F32).astype(BF16)
    kvbuf[:, cols : 2 * cols] = own_v
    keep_kv = pltpu.make_async_copy(kvbuf, kv_ref.at[me], ksem)
    keep_kv.start()

    load_wo = pltpu.make_async_copy(wo_ref, wo, wsem.at[0])
    load_wo.start()
    gate_up, shared_in = [], []
    for n, (source, buf) in enumerate(((ge_ref, wg), (ue_ref, wu))):
        for c in range(2):
            for k in range(nz):
                load = pltpu.make_async_copy(
                    source.at[:, pl.ds((k * 2 + c) * cols, cols)],
                    buf.at[c, :, pl.ds(k * cols, cols)],
                    wsem.at[1 + (n * 2 + c) * nz + k],
                )
                load.start()
                gate_up.append(load)
    base = 1 + 4 * nz
    load_wd = pltpu.make_async_copy(de_ref, wd, wsem.at[base])
    load_wd.start()
    for n, (source, buf) in enumerate(((gs_ref, sg), (us_ref, su))):
        for c in range(2):
            for k in range(nz):
                load = pltpu.make_async_copy(
                    source.at[:, pl.ds((k * 2 + c) * cols, cols)],
                    buf.at[c, :, pl.ds(k * cols, cols)],
                    wsem.at[base + 1 + (n * 2 + c) * nz + k],
                )
                load.start()
                shared_in.append(load)
    load_sd = pltpu.make_async_copy(ds_ref, sd, wsem.at[base + 1 + 4 * nz])
    load_sd.start()

    for load in small[4:]:
        load.wait()
    coef[...] = jnp.zeros(coef.shape, F32)
    expert = lax.broadcasted_iota(jnp.int32, (steps, experts), 1)
    for b in range(requests):
        total = jnp.zeros((steps, experts), F32)
        for j in range(ids_ref.shape[2]):
            total += jnp.where(ids_ref[b][:, j : j + 1] == expert, ew_ref[b][:, j : j + 1], 0.0)
        coef[pl.ds(b * steps, steps), pl.ds(0, experts)] = total
    high, low = split_two(coef[:, 0:experts])
    cbuf[me] = jnp.concatenate([high, low], axis=1)

    scalars = []
    prow = lax.broadcasted_iota(jnp.int32, (hr, total_rows), 0)
    pcol = lax.broadcasted_iota(jnp.int32, (hr, total_rows), 1)
    padded = pick.shape[0]
    scol = lax.broadcasted_iota(jnp.int32, (1, padded), 1)
    of_slot = jnp.full((1, padded), -1, jnp.int32)
    for s in range(padded // hr):
        if s < pool:
            request = req_ref[s]
            held = jnp.maximum(request, 0)
            edge = jnp.where(request >= 0, lens_ref[held] - blk_ref[s] * block, -1)
            first = held // requests * ROWS + held % requests * steps
            first = jnp.where(request >= 0, first, -steps)
            scalars.append((request, edge))
            chosen = (pcol - first == prow % steps) & (pcol >= first) & (first >= 0)
            of_slot = jnp.where(scol // hr == s, request, of_slot)
            pick[s * hr : (s + 1) * hr, :] = jnp.where(chosen, 1.0, 0.0)
        else:
            pick[s * hr : (s + 1) * hr, :] = jnp.zeros((hr, total_rows), F32)
    grow = lax.broadcasted_iota(jnp.int32, gatherer.shape, 0)
    gcol = lax.broadcasted_iota(jnp.int32, gatherer.shape, 1)
    gatherer[...] = jnp.where(
        (grow // hr == of_slot) & (grow % hr == gcol % hr), 1.0, 0.0
    ).astype(BF16)

    scale = 1.0 / math.sqrt(HD)
    nrow = lax.broadcasted_iota(jnp.int32, (requests * hr, ROWS), 0)
    ncol = lax.broadcasted_iota(jnp.int32, (requests * hr, ROWS), 1)
    b_of, t_of = nrow // hr, nrow % steps
    spread = jnp.where(ncol == b_of * steps + t_of, 1.0, 0.0).astype(BF16)
    hrow = lax.broadcasted_iota(jnp.int32, (requests * hr, cols), 0) % hr // steps
    hcol = lax.broadcasted_iota(jnp.int32, (requests * hr, cols), 1) // HD
    mine = jnp.where(
        hrow == hcol, jnp.dot(spread, own_q, preferred_element_type=F32), 0.0
    ).astype(BF16)
    scores = dot_t(mine, own_k) * scale
    seen = (ncol // steps == b_of) & (ncol % steps <= t_of) & (ncol < count)
    new_top = jnp.max(jnp.where(seen, scores, -1e30), axis=-1, keepdims=True)
    weights = jnp.where(seen, jnp.exp(scores - new_top), 0.0)
    new_total = jnp.sum(weights, axis=-1, keepdims=True)
    new_full = jnp.dot(weights.astype(BF16), own_v, preferred_element_type=F32)
    new_out = new_full[:, 0:HD]
    half = lax.broadcasted_iota(jnp.int32, (requests * hr, HD), 0) % hr // steps
    for h in range(1, heads):
        new_out = jnp.where(half == h, new_full[:, h * HD : (h + 1) * HD], new_out)

    all_q = whole(qbuf, qsend, qrecv)
    all_q.wait_recv()
    frow = lax.broadcasted_iota(jnp.int32, (padded, cols), 0) % hr // steps
    fcol = lax.broadcasted_iota(jnp.int32, (padded, cols), 1) // HD
    everyone = qbuf[...].reshape(total_rows, cols)
    slots[...] = jnp.where(
        frow == fcol, jnp.dot(pick[...].astype(BF16), everyone, preferred_element_type=F32), 0.0
    )
    for piece in pieces:
        piece.wait()
    slane = lax.broadcasted_iota(jnp.int32, (hr, HD), 1)
    klane = lax.broadcasted_iota(jnp.int32, (hr, block), 1)
    upper = lax.broadcasted_iota(jnp.int32, (hr, HD), 0) // steps
    top = jnp.full((hr, HD), -1e30, F32)
    all_scores = []
    for s in range(pool):
        request, edge = scalars[s]
        scores = dot_t(slots[s * hr : (s + 1) * hr, :].astype(BF16), kbuf[s]) * scale
        scores = jnp.where(klane < edge, scores, -1e30)
        all_scores.append(scores)
        best = jnp.max(scores, axis=-1, keepdims=True)
        top = jnp.maximum(top, jnp.where(slane == request, best, -1e30))
    top = top.astype(BF16).astype(F32)
    total = jnp.zeros((hr, HD), F32)
    for s in range(pool):
        request, edge = scalars[s]
        best = jnp.max(jnp.where(slane == request, top, -1e30), axis=-1, keepdims=True)
        weights = jnp.where(klane < edge, jnp.exp(all_scores[s] - best), 0.0)
        total += jnp.where(slane == request, jnp.sum(weights, axis=-1, keepdims=True), 0.0)
        full = jnp.dot(weights.astype(BF16), vbuf[s], preferred_element_type=F32)
        out = full[:, 0:HD]
        for h in range(1, heads):
            out = jnp.where(upper == h, full[:, h * HD : (h + 1) * HD], out)
        found[s * hr : (s + 1) * hr, :] = out
    if padded > pool * hr:
        found[pool * hr :, :] = jnp.zeros((padded - pool * hr, HD), F32)
    high, low = split_two(found[...])
    by_request = jnp.dot(gatherer[...], high, preferred_element_type=F32) + jnp.dot(
        gatherer[...], low, preferred_element_type=F32
    )
    high, low = split_two(pltpu.roll(total, HD // 2, 1))
    stats = jnp.concatenate(
        [jnp.where(slane < HD // 2, top, high.astype(F32)), low.astype(F32)], axis=0
    ).astype(BF16)
    by_request = by_request.astype(BF16)
    for d in range(ns):
        part[d, 0 : requests * hr, :] = by_request[d * requests * hr : (d + 1) * requests * hr, :]
        part[d, requests * hr :, :] = stats
    rbuf[me] = part[me]

    def push2(i, _):
        to = seq_far(i)
        pltpu.make_async_remote_copy(
            src_ref=part.at[to], dst_ref=rbuf.at[me], send_sem=send2, recv_sem=recv2,
            device_id=peer(to, exp), device_id_type=MESH,
        ).start()
        return 0

    lax.fori_loop(0, ns - 1, push2, 0)
    all2 = whole(part, send2, recv2)
    all2.wait_recv()

    shift = (HD - me * requests) % HD
    sums_of, tops = [], []
    for s in range(ns):
        stats = rbuf[s, requests * hr :, :].astype(F32)
        low = jnp.where(slane < HD // 2, 0.0, stats[hr:])
        tops.append(pltpu.roll(stats[0:hr] + low, shift, 1))
    fresh = jnp.full((hr, HD), -1e30, F32)
    for b in range(requests):
        rows = slice(b * hr, (b + 1) * hr)
        fresh = jnp.where(slane == b, new_top[rows], fresh)
        fresh = jnp.where(slane == HD // 2 + b, new_total[rows], fresh)
    tops.append(fresh)
    best = tops[0]
    for s in range(1, ns + 1):
        best = jnp.maximum(best, tops[s])
    factors, total = [], jnp.zeros((hr, HD), F32)
    for s in range(ns + 1):
        factor = jnp.exp(jnp.where(slane < requests, tops[s] - best, 0.0))
        factors.append(factor)
        total += pltpu.roll(tops[s], HD // 2, 1) * factor
    held = [rbuf[s, 0 : requests * hr, :].astype(F32) for s in range(ns)]
    attended = []
    for b in range(requests):
        rows = slice(b * hr, (b + 1) * hr)
        summed = new_out[rows] * factors[ns][:, b : b + 1]
        for s in range(ns):
            summed += held[s][rows] * factors[s][:, b : b + 1]
        attended.append(summed / total[:, b : b + 1])
    stacked = jnp.concatenate(attended, axis=0).astype(BF16)
    prow = lax.broadcasted_iota(jnp.int32, (ROWS, requests * hr), 0)
    pcol = lax.broadcasted_iota(jnp.int32, (ROWS, requests * hr), 1)
    by_head = []
    for h in range(cols // HD):
        pick = (pcol == prow // steps * hr + h * steps + prow % steps) & (prow < count)
        by_head.append(
            jnp.dot(
                jnp.where(pick, 1.0, 0.0).astype(BF16), stacked, preferred_element_type=F32
            ).astype(BF16)
        )
    own = jnp.concatenate(by_head, axis=1)
    load_wo.wait()
    for e in range(ne):
        terms[e] = jnp.dot(
            own, wo[:, e * cols : (e + 1) * cols], preferred_element_type=F32
        ).astype(BF16)

    def push3(i, _):
        to = exp_far(i)
        pltpu.make_async_remote_copy(
            src_ref=terms.at[to], dst_ref=r3.at[exp], send_sem=send3, recv_sem=recv3,
            device_id=peer(me, to), device_id_type=MESH,
        ).start()
        return 0

    lax.fori_loop(0, ne - 1, push3, 0)
    push(cbuf.at[me], cbuf.at[me], cosend, corecv)
    push(kvbuf, kv_ref.at[me], kvsend, kvrecv)
    r3[exp] = terms[exp]
    all3 = pltpu.make_async_remote_copy(
        src_ref=terms.at[pl.ds(0, ne - 1)], dst_ref=r3.at[pl.ds(0, ne - 1)],
        send_sem=send3, recv_sem=recv3, device_id=peer(me, (exp + 1) % ne), device_id_type=MESH,
    )
    all3.wait_recv()
    residual = xs[:, pl.ds(pl.multiple_of(exp * cols, cols), cols)]
    for e in range(ne):
        residual += r3[e].astype(F32)

    scaled = residual * fgain_ref[:, pl.ds(pl.multiple_of(exp * cols, cols), cols)]
    square = jnp.sum(residual * residual, axis=-1, keepdims=True)
    brow = lax.broadcasted_iota(jnp.int32, (ROWS, cols), 0)
    blane = lax.broadcasted_iota(jnp.int32, (ROWS, cols), 1)
    line = jnp.sum(jnp.where(brow == blane, square, 0.0), axis=0, keepdims=True)
    high, low = split_two(line)
    scaled = jnp.where(brow == count, high.astype(F32), scaled)
    scaled = jnp.where(brow == count + 1, low.astype(F32), scaled)
    my_cols = pl.ds(pl.multiple_of(z * cols, cols), cols)
    back = z * ns + me
    xbuf[core, my_rows, my_cols] = scaled.astype(BF16)

    def push4(i, _):
        there = (z + far_first(i // ns, nz)) % nz * 2 + core
        pltpu.make_async_remote_copy(
            src_ref=xbuf.at[core, my_rows, my_cols], dst_ref=xbuf.at[core, my_rows, my_cols],
            send_sem=send4.at[i // ns], recv_sem=recv4.at[z],
            device_id=peer(seq_far(i), there), device_id_type=MESH,
        ).start()
        return 0

    lax.fori_loop(0, nz * ns - 1, push4, 0)

    all_c = whole(cbuf, cosend, corecv)
    all_c.wait_recv()
    coefs = cbuf[...].reshape(total_rows, 2 * experts).astype(F32)
    clane = lax.broadcasted_iota(jnp.int32, (total_rows, 2 * experts), 1)
    ucol = lax.broadcasted_iota(jnp.int32, (total_rows, wd.shape[0]), 1)
    routing[...] = jnp.zeros(routing.shape, F32)
    for j in range(own_experts):
        mine = me * own_experts + j
        weight = jnp.sum(
            jnp.where((clane == mine) | (clane == mine + experts), coefs, 0.0), axis=-1, keepdims=True
        )
        routing[...] += jnp.where((ucol >= j * fe) & (ucol < (j + 1) * fe), weight, 0.0)

    arrival = [(z + nz - far_first(i, nz)) % nz for i in range(nz)]
    forwards = []
    for i in range(nz):
        k = arrival[i]
        span = pl.ds(0, total_rows - (ROWS if i == nz - 1 else 0))
        kcols = pl.ds(pl.multiple_of(k * cols, cols), cols)
        pltpu.make_async_remote_copy(
            src_ref=xbuf.at[core, span, kcols], dst_ref=xbuf.at[core, span, kcols],
            send_sem=send4.at[i], recv_sem=recv4.at[k], device_id=peer(me, twin), device_id_type=MESH,
        ).wait_recv()
        forward = pltpu.make_async_remote_copy(
            src_ref=xbuf.at[core, :, kcols], dst_ref=xbuf.at[core, :, kcols],
            send_sem=fsend.at[k], recv_sem=frecv.at[k], device_id=peer(me, twin), device_id_type=MESH,
        )
        forward.start()
        forwards.append(forward)

    for load in gate_up:
        load.wait()
    acc[0] = dot_t(xbuf[core], wg[core])
    acc[1] = dot_t(xbuf[core], wu[core])

    trow = lax.broadcasted_iota(jnp.int32, (total_rows, total_rows), 0)
    tcol = lax.broadcasted_iota(jnp.int32, (total_rows, total_rows), 1)
    spread = (trow // ROWS == tcol // ROWS) & ((tcol % ROWS == count) | (tcol % ROWS == count + 1))
    spread = jnp.where(spread, 1.0, 0.0).astype(BF16)

    def squares(c):
        value = xbuf[c, :, 0:HD].astype(F32)
        for k in range(1, nz):
            value += xbuf[c, :, k * cols : k * cols + HD].astype(F32)
        return value

    first = squares(core)
    for i in range(nz):
        k = arrival[i]
        kcols = pl.ds(pl.multiple_of(k * cols, cols), cols)
        pltpu.make_async_remote_copy(
            src_ref=xbuf.at[other, :, kcols], dst_ref=xbuf.at[other, :, kcols],
            send_sem=fsend.at[k], recv_sem=frecv.at[k], device_id=peer(me, twin), device_id_type=MESH,
        ).wait_recv()
    high, low = split_two(first + squares(other))
    square = jnp.dot(spread, high, preferred_element_type=F32) + jnp.dot(
        spread, low, preferred_element_type=F32
    )
    lrow = lax.broadcasted_iota(jnp.int32, (total_rows, HD), 0)
    llane = lax.broadcasted_iota(jnp.int32, (total_rows, HD), 1)
    square = jnp.sum(jnp.where(lrow % ROWS == llane, square, 0.0), axis=-1, keepdims=True)
    row_scale = lax.rsqrt(square / width + 1e-06)
    scales[...] = jnp.broadcast_to(row_scale, scales.shape)
    gate = (acc[0] + dot_t(xbuf[other], wg[other])) * row_scale
    up = (acc[1] + dot_t(xbuf[other], wu[other])) * row_scale
    inner = (jax.nn.silu(gate) * up * routing[...]).astype(BF16)
    load_wd.wait()

    def down(e):
        where = pl.ds(pl.multiple_of(e * cols, cols), cols)
        return jnp.dot(inner, wd[:, where], preferred_element_type=F32)

    pairs = []

    def give(i):
        k = (z + far_first(i, nz)) % nz
        ybuf[other, k] = packed(down(k * 2 + other), ns).astype(BF16)
        pair = pltpu.make_async_remote_copy(
            src_ref=ybuf.at[other, k], dst_ref=ypair.at[k],
            send_sem=psend.at[k], recv_sem=precv.at[k], device_id=peer(me, twin), device_id_type=MESH,
        )
        pair.start()
        pairs.append(pair)

    give(0)
    give(1)
    for i in range(nz):
        k = (z + far_first(i, nz)) % nz
        if i + 2 < nz:
            give(i + 2)
        sums[...] = packed(down(k * 2 + core), ns)
        pairs[i].wait_recv()
        ybuf[core, k] = (sums[...] + ypair[k].astype(F32)).astype(BF16)

        def push5(n, _):
            to = seq_far(n)
            pltpu.make_async_remote_copy(
                src_ref=ybuf.at[core, k, to], dst_ref=r5.at[back],
                send_sem=send5, recv_sem=recv5,
                device_id=peer(to, k * 2 + core), device_id_type=MESH,
            ).start()
            return 0

        lax.fori_loop(0, ns - 1 if i == nz - 1 else ns, push5, 0)
    r5[back] = ybuf[core, z, me]

    for load in shared_in:
        load.wait()
    load_sd.wait()
    gate = jnp.zeros((ROWS, sg.shape[1]), F32)
    up = jnp.zeros((ROWS, sg.shape[1]), F32)
    for c in range(2):
        rows = xbuf[c, my_rows, :]
        gate += dot_t(rows, sg[c])
        up += dot_t(rows, su[c])
    own_scale = scales[my_rows, 0:1]
    gate, up = gate * own_scale, up * own_scale
    inner = jnp.where(
        lax.broadcasted_iota(jnp.int32, gate.shape, 0) < count, jax.nn.silu(gate) * up, 0.0
    ).astype(BF16)
    for e in range(ne):
        shared[e] = jnp.dot(
            inner, sd[:, e * cols : (e + 1) * cols], preferred_element_type=F32
        ).astype(BF16)

    def push6(i, _):
        to = exp_far(i)
        pltpu.make_async_remote_copy(
            src_ref=shared.at[to], dst_ref=r6.at[exp], send_sem=send6, recv_sem=recv6,
            device_id=peer(me, to), device_id_type=MESH,
        ).start()
        return 0

    lax.fori_loop(0, ne - 1, push6, 0)
    r6[exp] = shared[exp]
    all6 = pltpu.make_async_remote_copy(
        src_ref=shared.at[pl.ds(0, ne - 1)], dst_ref=r6.at[pl.ds(0, ne - 1)],
        send_sem=send6, recv_sem=recv6, device_id=peer(me, (exp + 1) % ne), device_id_type=MESH,
    )
    all6.wait_recv()
    result = residual
    for e in range(ne):
        result += r6[e].astype(F32)

    rest = pl.ds(0, nz * ns - 1)
    all5 = pltpu.make_async_remote_copy(
        src_ref=r5.at[rest], dst_ref=r5.at[rest],
        send_sem=send5, recv_sem=recv5, device_id=peer(me, twin), device_id_type=MESH,
    )
    all5.wait_recv()
    routed = r5[0].astype(F32)
    for k in range(1, nz * ns):
        routed += r5[k].astype(F32)
    tail = jnp.concatenate([routed[0:4, cols:], routed[4:8, cols:]], axis=1)
    result = result[0:count] + jnp.concatenate([routed[:, 0:cols], tail], axis=0)
    for b in range(requests):
        out_ref[b] = result[b * steps : (b + 1) * steps, :]

    all_kv = whole(kv_ref, kvsend, kvrecv)
    all_kv.wait_recv()
    all_kv.wait_send()
    keep_kv.wait()
    all_q.wait_send()
    all_c.wait_send()
    all2.wait_send()
    all3.wait_send()
    all5.wait_send()
    all6.wait_send()
    for i in range(nz):
        span = pl.ds(0, total_rows - (ROWS if i == nz - 1 else 0))
        pltpu.make_async_remote_copy(
            src_ref=xbuf.at[core, span, 0:cols], dst_ref=xbuf.at[core, span, 0:cols],
            send_sem=send4.at[i], recv_sem=recv4.at[i], device_id=peer(me, twin), device_id_type=MESH,
        ).wait_send()
    for i in range(nz):
        forwards[i].wait_send()
        pairs[i].wait_send()


def patch_kernel(
    req_any, blk_any, lens_any, kv_any, hidden_any, key_ref, value_ref,
    key_out, value_out, hidden_out,
    req_ref, blk_ref, lens_ref, kv_ref, hidden_ref, kbuf, vbuf, fresh_rows, small_sem, in_sem, out_sem,
    *, requests, steps, group,
):
    pool, block, cols = key_ref.shape
    ns = kv_any.shape[0]
    starts = list(range(0, pool, group))
    sizes = [min(group, pool - s) for s in starts]

    def copies(g, into):
        span = pl.ds(starts[g], sizes[g])
        pairs = ((key_ref, kbuf, key_out), (value_ref, vbuf, value_out))
        result = []
        for n, (source, buf, target) in enumerate(pairs):
            if into:
                result.append(pltpu.make_async_copy(source.at[span], buf.at[span], in_sem.at[n, g]))
            else:
                result.append(pltpu.make_async_copy(buf.at[span], target.at[span], out_sem.at[n, g]))
        return result

    small = []
    pairs = (
        (kv_any, kv_ref), (req_any, req_ref), (blk_any, blk_ref), (lens_any, lens_ref),
        (hidden_any, hidden_ref),
    )
    for n, (source, buf) in enumerate(pairs):
        load = pltpu.make_async_copy(source, buf, small_sem.at[n])
        load.start()
        small.append(load)
    for g in range(len(starts)):
        for c in copies(g, True):
            c.start()
    for load in small:
        load.wait()
    hidden_out[...] = hidden_ref[...]
    for s in range(ns):
        kv = kv_ref[s].astype(F32)
        for b in range(requests):
            fresh_rows[s * requests + b] = kv[b * steps : (b + 1) * steps, :]
    window = 2 * ROWS
    wrow = lax.broadcasted_iota(jnp.int32, (window, cols), 0)
    for g in range(len(starts)):
        for c in copies(g, True):
            c.wait()

        def patch(i, _):
            s = starts[g] + i
            request = jnp.maximum(req_ref[s], 0)
            offset = lens_ref[request] - blk_ref[s] * block

            @pl.when((req_ref[s] >= 0) & (offset > -steps) & (offset < block))
            def _():
                first = jnp.clip(offset // ROWS * ROWS, 0, block - window)
                first = pl.multiple_of(first, ROWS)
                rel = wrow + first - offset
                for n, buf in enumerate((kbuf, vbuf)):
                    tile = buf[s, pl.ds(first, window), :].astype(F32)
                    for t in range(steps):
                        one = fresh_rows[request, t : t + 1, n * cols : (n + 1) * cols]
                        tile = jnp.where(rel == t, one, tile)
                    buf[s, pl.ds(first, window), :] = tile.astype(BF16)

            return 0

        lax.fori_loop(0, sizes[g], patch, 0)
        for c in copies(g, False):
            c.start()
    for g in range(len(starts)):
        for c in copies(g, False):
            c.wait()


def body(
    hidden_in, cache_lens, slot_request, slot_block, key_cache, value_cache, attn_gain,
    query_weight, key_weight, value_weight, out_weight, ffn_gain, expert_ids, expert_weights,
    gate_experts, up_experts, down_experts, gate_shared, up_shared, down_shared,
):
    requests, steps, width = hidden_in.shape
    ns = lax.axis_size("seq")
    ne = lax.axis_size("exp")
    nz = ne // 2
    cols = query_weight.shape[1]
    own_experts, _, fe = gate_experts.shape
    sf = gate_shared.shape[1]
    experts = own_experts * ns
    pool, block, _ = key_cache.shape
    hr = cols // HD * steps
    total_rows = ns * ROWS
    padded = -(-pool * hr // 128) * 128

    exponent = np.arange(HD // 2) * (2.0 / HD)
    frequency = np.power(10000.0, -exponent).astype(np.float32)
    frequency = jnp.asarray(np.concatenate([frequency, frequency])[None, :])

    vmem = pl.BlockSpec(memory_space=pltpu.VMEM)
    anys = pl.BlockSpec(memory_space=pl.ANY)
    dma = pltpu.SemaphoreType.DMA

    hidden, new_kv = pl.pallas_call(
        layer_kernel,
        out_shape=(
            jax.ShapeDtypeStruct((requests, steps, cols), F32),
            jax.ShapeDtypeStruct((ns, ROWS, 2 * cols), BF16),
        ),
        in_specs=[anys] * 21,
        out_specs=(vmem, anys),
        scratch_shapes=[
            pltpu.SMEM(cache_lens.shape, jnp.int32),
            pltpu.SMEM(slot_request.shape, jnp.int32),
            pltpu.SMEM(slot_block.shape, jnp.int32),
            pltpu.VMEM((1, HD), F32),
            pltpu.VMEM(hidden_in.shape, F32),
            pltpu.VMEM((1, width), F32),
            pltpu.VMEM(expert_ids.shape, jnp.int32),
            pltpu.VMEM(expert_weights.shape, F32),
            pltpu.VMEM((1, width), F32),
            pltpu.VMEM((3, width, cols), BF16),
            pltpu.VMEM((ns, ROWS, cols), BF16),
            pltpu.VMEM((ROWS, 2 * cols), BF16),
            pltpu.VMEM((ns, ROWS, 2 * experts), BF16),
            pltpu.VMEM((ROWS, 2 * experts), F32),
            pltpu.VMEM(key_cache.shape, BF16),
            pltpu.VMEM(key_cache.shape, BF16),
            pltpu.VMEM((padded, total_rows), F32),
            pltpu.VMEM((ns * requests * hr, padded), BF16),
            pltpu.VMEM((padded, cols), F32),
            pltpu.VMEM((ns, (requests + 2) * hr, HD), BF16),
            pltpu.VMEM((padded, HD), F32),
            pltpu.VMEM((cols, width), BF16),
            pltpu.VMEM((2, own_experts * fe, width // 2), BF16),
            pltpu.VMEM((2, own_experts * fe, width // 2), BF16),
            pltpu.VMEM((own_experts * fe, width), BF16),
            pltpu.VMEM((2, sf, width // 2), BF16),
            pltpu.VMEM((2, sf, width // 2), BF16),
            pltpu.VMEM((sf, width), BF16),
            pltpu.VMEM((ns, (requests + 2) * hr, HD), BF16),
            pltpu.VMEM((ROWS, width), F32),
            pltpu.VMEM((ne, ROWS, cols), BF16),
            pltpu.VMEM((ne, ROWS, cols), BF16),
            pltpu.VMEM((2, total_rows, nz * cols), BF16),
            pltpu.VMEM((2, total_rows, own_experts * fe), F32),
            pltpu.VMEM((total_rows, own_experts * fe), F32),
            pltpu.VMEM((total_rows, HD), F32),
            pltpu.VMEM((2, nz, ns, 8, cols + cols // 2), BF16),
            pltpu.VMEM((nz, ns, 8, cols + cols // 2), BF16),
            pltpu.VMEM((ns, 8, cols + cols // 2), F32),
            pltpu.VMEM((nz * ns, 8, cols + cols // 2), BF16),
            pltpu.VMEM((ne, ROWS, cols), BF16),
            pltpu.VMEM((ne, ROWS, cols), BF16),
            dma((9,)), dma((3,)), dma((2, 4)), dma,
            dma, dma, dma, dma, dma, dma,
            dma((3 + 8 * nz,)),
            dma, dma, dma, dma, dma((nz,)),
            dma((nz,)), dma((nz,)), dma((nz,)), dma((nz,)), dma((nz,)),
            dma, dma, dma, dma,
        ],
        compiler_params=pltpu.CompilerParams(collective_id=0, has_side_effects=True),
        name="layer",
    )(
        cache_lens, slot_request, slot_block, frequency, hidden_in, attn_gain[None, :],
        expert_ids, expert_weights, ffn_gain[None, :],
        query_weight, key_weight, value_weight, key_cache, value_cache, out_weight,
        jnp.swapaxes(gate_experts, 1, 2).reshape(own_experts * fe, width),
        jnp.swapaxes(up_experts, 1, 2).reshape(own_experts * fe, width),
        down_experts.reshape(own_experts * fe, width),
        gate_shared.T, up_shared.T, down_shared,
    )

    group = 8
    groups = -(-pool // group)
    key_out, value_out, hidden_out = pl.pallas_call(
        functools.partial(patch_kernel, requests=requests, steps=steps, group=group),
        out_shape=(
            jax.ShapeDtypeStruct(key_cache.shape, BF16),
            jax.ShapeDtypeStruct(value_cache.shape, BF16),
            jax.ShapeDtypeStruct(hidden.shape, F32),
        ),
        in_specs=[anys] * 7,
        out_specs=(anys, anys, vmem),
        scratch_shapes=[
            pltpu.SMEM(slot_request.shape, jnp.int32),
            pltpu.SMEM(slot_block.shape, jnp.int32),
            pltpu.SMEM(cache_lens.shape, jnp.int32),
            pltpu.VMEM(new_kv.shape, BF16),
            pltpu.VMEM(hidden.shape, F32),
            pltpu.VMEM(key_cache.shape, BF16),
            pltpu.VMEM(key_cache.shape, BF16),
            pltpu.VMEM((ns * requests, steps, 2 * cols), F32),
            dma((5,)),
            dma((2, groups)),
            dma((2, groups)),
        ],
        name="patch",
    )(slot_request, slot_block, cache_lens, new_kv, hidden, key_cache, value_cache)
    return (hidden_out, key_out, value_out)


def solution(mesh):
    in_specs = (
        P("seq", None, None),
        P(),
        P("seq"),
        P("seq"),
        P("seq", None, "exp"),
        P("seq", None, "exp"),
        P(),
        P(None, "exp"),
        P(None, "exp"),
        P(None, "exp"),
        P("exp", None),
        P(),
        P("seq", None, None),
        P("seq", None, None),
        P("seq", None, "exp"),
        P("seq", None, "exp"),
        P("seq", "exp", None),
        P(None, "exp"),
        P(None, "exp"),
        P("exp", None),
    )
    out_specs = (P("seq", None, "exp"), P("seq", None, "exp"), P("seq", None, "exp"))
    return jax.shard_map(body, mesh=mesh, in_specs=in_specs, out_specs=out_specs, check_vma=False)
```

```python
import functools
import math

import jax
import jax.numpy as jnp
import numpy as np
from jax import lax
from jax.experimental import pallas as pl
from jax.experimental.pallas import tpu as pltpu
from jax.sharding import PartitionSpec as P

HD = 128
MESH = pl.DeviceIdType.MESH
F32 = jnp.float32
BF16 = jnp.bfloat16
ROWS = 16


def peer(seq, exp):
    return {"seq": seq, "exp": exp}


def rows_of(ref, scratch):
    count, steps, _ = ref.shape
    for b in range(count):
        scratch[pl.ds(b * steps, steps), :] = ref[b]
    used = count * steps
    scratch[pl.ds(used, ROWS - used), :] = jnp.zeros((ROWS - used, ref.shape[2]), F32)


def far_first(i, side):
    if side == 4:
        return jnp.where(i == 0, 2, jnp.where(i == 1, 1, jnp.where(i == 2, 3, 0)))
    return side - 1 - i


def packed(value, blocks):
    value = value.reshape(blocks, ROWS, value.shape[1])
    half = value.shape[2] // 2
    left, right = value[:, 8:, :half], value[:, 8:, half:]
    row = lax.broadcasted_iota(jnp.int32, left.shape, 1)
    tail = jnp.where(row < 4, left, pltpu.roll(right, 4, 1))
    return jnp.concatenate([value[:, :8, :], tail], axis=2)


def silu(x):
    half = 0.5 * x
    return half + half * jnp.tanh(half)


def dot_t(a, b):
    return lax.dot_general(a, b, (((1,), (1,)), ((), ())), preferred_element_type=F32)


def split_two(values):
    high = values.astype(BF16)
    low = (values - high.astype(F32)).astype(BF16)
    return high, low


def layer_kernel(
    lens_any, req_any, blk_any, freq_any, hidden_any, again_any, ids_any, ew_any, fgain_any,
    wq_ref, wk_ref, wv_ref, key_ref, value_ref,
    wo_ref, ge_ref, ue_ref, de_ref, gs_ref, us_ref, ds_ref,
    out_ref, kv_ref,
    lens_ref, req_ref, blk_ref, freq_ref, hidden_ref, again_ref, ids_ref, ew_ref, fgain_ref,
    wbuf, qbuf, kvbuf, cbuf, coef, kbuf, vbuf, pick, gatherer, slots, part, found,
    wo, wg, wu, wd, sg, su, sd, rbuf, xs, terms, r3, xbuf, acc, routing, scales, ybuf, ypair, sums, r5, shared, r6,
    isem, asem, csem, ksem, qsend, qrecv, kvsend, kvrecv, cosend, corecv,
    wsem, send2, recv2, send3, recv3, send4, recv4, fsend, frecv, psend, precv, send5, recv5, send6, recv6,
):
    ns = lax.axis_size("seq")
    ne = lax.axis_size("exp")
    nz = ne // 2
    me = lax.axis_index("seq")
    exp = lax.axis_index("exp")
    z, core = exp // 2, exp % 2
    other = 1 - core
    twin = z * 2 + other
    requests, steps, width = hidden_ref.shape
    cols = wq_ref.shape[1]
    heads = cols // HD
    hr = heads * steps
    pool, block, _ = key_ref.shape
    experts = coef.shape[1] // 2
    own_experts = experts // ns
    fe = ge_ref.shape[0] // own_experts
    count = requests * steps
    total_rows = ns * ROWS

    side = math.isqrt(ns)

    def seq_far(i):
        x = (me // side + far_first(i // side % side, side)) % side
        y = (me % side + far_first(i % side, side)) % side
        return x * side + y

    def exp_far(i):
        return (z + far_first(i // 2, nz)) % nz * 2 + (core + 1 - i % 2) % 2

    barrier = pltpu.get_barrier_semaphore()

    def greet_seq(i, _):
        pl.semaphore_signal(barrier, inc=1, device_id=peer((me + i) % ns, exp), device_id_type=MESH)
        return 0

    def greet_exp(i, _):
        pl.semaphore_signal(barrier, inc=1, device_id=peer(me, (exp + i) % ne), device_id_type=MESH)
        return 0

    lax.fori_loop(1, ns, greet_seq, 0)
    lax.fori_loop(1, ne, greet_exp, 0)
    small = []
    pairs = (
        (hidden_any, hidden_ref), (again_any, again_ref), (lens_any, lens_ref),
        (freq_any, freq_ref), (ids_any, ids_ref), (ew_any, ew_ref), (req_any, req_ref),
        (blk_any, blk_ref), (fgain_any, fgain_ref),
    )
    for n, (source, buf) in enumerate(pairs):
        load = pltpu.make_async_copy(source, buf, isem.at[n])
        load.start()
        small.append(load)
    loads = []
    for k, w in enumerate((wq_ref, wk_ref, wv_ref)):
        load = pltpu.make_async_copy(w, wbuf.at[k], asem.at[k])
        load.start()
        loads.append(load)
    pieces = []
    chunk = -(-pool // 4)
    for g in range(4):
        span = pl.ds(g * chunk, min(chunk, pool - g * chunk))
        for n, (source, buf) in enumerate(((key_ref, kbuf), (value_ref, vbuf))):
            load = pltpu.make_async_copy(source.at[span], buf.at[span], csem.at[n, g])
            load.start()
            pieces.append(load)

    for load in small[:4]:
        load.wait()
    rows_of(hidden_ref, xs)
    x = xs[...]
    mean_square = jnp.mean(x * x, axis=-1, keepdims=True)
    normed = (x * lax.rsqrt(mean_square + 1e-06) * again_ref[...]).astype(BF16)
    row = lax.broadcasted_iota(jnp.int32, (ROWS, HD), 0)
    lane = lax.broadcasted_iota(jnp.int32, (ROWS, HD), 1)
    length = jnp.zeros((ROWS, HD), jnp.int32)
    for b in range(requests):
        length = jnp.where(row // steps == b, lens_ref[me * requests + b], length)
    position = (length + row % steps).astype(F32)
    angles = position * freq_ref[...]
    cosine = jnp.cos(angles)
    sine = jnp.sin(angles)
    sine = jnp.where(lane < HD // 2, -sine, sine)

    def rotate(v):
        parts = []
        for h in range(heads):
            one = v[:, h * HD : (h + 1) * HD]
            parts.append(one * cosine + pltpu.roll(one, HD // 2, 1) * sine)
        return jnp.concatenate(parts, axis=1)

    def push(src, dst, send, recv):
        def one(i, _):
            pltpu.make_async_remote_copy(
                src_ref=src, dst_ref=dst, send_sem=send, recv_sem=recv,
                device_id=peer(seq_far(i), exp), device_id_type=MESH,
            ).start()
            return 0

        lax.fori_loop(0, ns - 1, one, 0)

    def whole(ref, send, recv):
        return pltpu.make_async_remote_copy(
            src_ref=ref.at[pl.ds(0, ns - 1)], dst_ref=ref.at[pl.ds(0, ns - 1)],
            send_sem=send, recv_sem=recv,
            device_id=peer((me + 1) % ns, exp), device_id_type=MESH,
        )

    my_rows = pl.ds(pl.multiple_of(me * ROWS, ROWS), ROWS)
    loads[0].wait()
    own_q = rotate(jnp.dot(normed, wbuf[0], preferred_element_type=F32)).astype(BF16)
    qbuf[me] = own_q
    pl.semaphore_wait(barrier, ns - 1 + ne - 1)
    push(qbuf.at[me], qbuf.at[me], qsend, qrecv)
    loads[1].wait()
    own_k = rotate(jnp.dot(normed, wbuf[1], preferred_element_type=F32)).astype(BF16)
    kvbuf[:, 0:cols] = own_k
    loads[2].wait()
    own_v = jnp.dot(normed, wbuf[2], preferred_element_type=F32).astype(BF16)
    kvbuf[:, cols : 2 * cols] = own_v
    keep_kv = pltpu.make_async_copy(kvbuf, kv_ref.at[me], ksem)
    keep_kv.start()

    load_wo = pltpu.make_async_copy(wo_ref, wo, wsem.at[0])
    load_wo.start()
    gate_up, shared_in = [], []
    for n, (source, buf) in enumerate(((ge_ref, wg), (ue_ref, wu))):
        for c in range(2):
            for k in range(nz):
                load = pltpu.make_async_copy(
                    source.at[:, pl.ds((k * 2 + c) * cols, cols)],
                    buf.at[c, :, pl.ds(k * cols, cols)],
                    wsem.at[1 + (n * 2 + c) * nz + k],
                )
                load.start()
                gate_up.append(load)
    base = 1 + 4 * nz
    load_wd = pltpu.make_async_copy(de_ref, wd, wsem.at[base])
    load_wd.start()
    for n, (source, buf) in enumerate(((gs_ref, sg), (us_ref, su))):
        for c in range(2):
            for k in range(nz):
                load = pltpu.make_async_copy(
                    source.at[:, pl.ds((k * 2 + c) * cols, cols)],
                    buf.at[c, :, pl.ds(k * cols, cols)],
                    wsem.at[base + 1 + (n * 2 + c) * nz + k],
                )
                load.start()
                shared_in.append(load)
    load_sd = pltpu.make_async_copy(ds_ref, sd, wsem.at[base + 1 + 4 * nz])
    load_sd.start()

    for load in small[4:]:
        load.wait()
    coef[...] = jnp.zeros(coef.shape, F32)
    expert = lax.broadcasted_iota(jnp.int32, (steps, experts), 1)
    for b in range(requests):
        total = jnp.zeros((steps, experts), F32)
        for j in range(ids_ref.shape[2]):
            total += jnp.where(ids_ref[b][:, j : j + 1] == expert, ew_ref[b][:, j : j + 1], 0.0)
        coef[pl.ds(b * steps, steps), pl.ds(0, experts)] = total
    high, low = split_two(coef[:, 0:experts])
    cbuf[me] = jnp.concatenate([high, low], axis=1)

    scalars = []
    prow = lax.broadcasted_iota(jnp.int32, (hr, total_rows), 0)
    pcol = lax.broadcasted_iota(jnp.int32, (hr, total_rows), 1)
    padded = pick.shape[0]
    scol = lax.broadcasted_iota(jnp.int32, (1, padded), 1)
    of_slot = jnp.full((1, padded), -1, jnp.int32)
    for s in range(padded // hr):
        if s < pool:
            request = req_ref[s]
            held = jnp.maximum(request, 0)
            edge = jnp.where(request >= 0, lens_ref[held] - blk_ref[s] * block, -1)
            first = held // requests * ROWS + held % requests * steps
            first = jnp.where(request >= 0, first, -steps)
            scalars.append((request, edge))
            chosen = (pcol - first == prow % steps) & (pcol >= first) & (first >= 0)
            of_slot = jnp.where(scol // hr == s, request, of_slot)
            pick[s * hr : (s + 1) * hr, :] = jnp.where(chosen, 1.0, 0.0)
        else:
            pick[s * hr : (s + 1) * hr, :] = jnp.zeros((hr, total_rows), F32)
    grow = lax.broadcasted_iota(jnp.int32, gatherer.shape, 0)
    gcol = lax.broadcasted_iota(jnp.int32, gatherer.shape, 1)
    gatherer[...] = jnp.where(
        (grow // hr == of_slot) & (grow % hr == gcol % hr), 1.0, 0.0
    ).astype(BF16)

    scale = 1.0 / math.sqrt(HD)
    nrow = lax.broadcasted_iota(jnp.int32, (requests * hr, ROWS), 0)
    ncol = lax.broadcasted_iota(jnp.int32, (requests * hr, ROWS), 1)
    b_of, t_of = nrow // hr, nrow % steps
    spread = jnp.where(ncol == b_of * steps + t_of, 1.0, 0.0).astype(BF16)
    hrow = lax.broadcasted_iota(jnp.int32, (requests * hr, cols), 0) % hr // steps
    hcol = lax.broadcasted_iota(jnp.int32, (requests * hr, cols), 1) // HD
    mine = jnp.where(
        hrow == hcol, jnp.dot(spread, own_q, preferred_element_type=F32), 0.0
    ).astype(BF16)
    scores = dot_t(mine, own_k) * scale
    seen = (ncol // steps == b_of) & (ncol % steps <= t_of) & (ncol < count)
    new_top = jnp.max(jnp.where(seen, scores, -1e30), axis=-1, keepdims=True)
    weights = jnp.where(seen, jnp.exp(scores - new_top), 0.0)
    new_total = jnp.sum(weights, axis=-1, keepdims=True)
    new_full = jnp.dot(weights.astype(BF16), own_v, preferred_element_type=F32)
    new_out = new_full[:, 0:HD]
    half = lax.broadcasted_iota(jnp.int32, (requests * hr, HD), 0) % hr // steps
    for h in range(1, heads):
        new_out = jnp.where(half == h, new_full[:, h * HD : (h + 1) * HD], new_out)

    all_q = whole(qbuf, qsend, qrecv)
    all_q.wait_recv()
    frow = lax.broadcasted_iota(jnp.int32, (padded, cols), 0) % hr // steps
    fcol = lax.broadcasted_iota(jnp.int32, (padded, cols), 1) // HD
    everyone = qbuf[...].reshape(total_rows, cols)
    slots[...] = jnp.where(
        frow == fcol, jnp.dot(pick[...].astype(BF16), everyone, preferred_element_type=F32), 0.0
    )
    for piece in pieces:
        piece.wait()
    slane = lax.broadcasted_iota(jnp.int32, (hr, HD), 1)
    klane = lax.broadcasted_iota(jnp.int32, (hr, block), 1)
    upper = lax.broadcasted_iota(jnp.int32, (hr, HD), 0) // steps
    top = jnp.full((hr, HD), -1e30, F32)
    all_scores = []
    for s in range(pool):
        request, edge = scalars[s]
        scores = dot_t(slots[s * hr : (s + 1) * hr, :].astype(BF16), kbuf[s]) * scale
        scores = jnp.where(klane < edge, scores, -1e30)
        all_scores.append(scores)
        best = jnp.max(scores, axis=-1, keepdims=True)
        top = jnp.maximum(top, jnp.where(slane == request, best, -1e30))
    top = top.astype(BF16).astype(F32)
    total = jnp.zeros((hr, HD), F32)
    for s in range(pool):
        request, edge = scalars[s]
        best = jnp.max(jnp.where(slane == request, top, -1e30), axis=-1, keepdims=True)
        weights = jnp.where(klane < edge, jnp.exp(all_scores[s] - best), 0.0)
        total += jnp.where(slane == request, jnp.sum(weights, axis=-1, keepdims=True), 0.0)
        full = jnp.dot(weights.astype(BF16), vbuf[s], preferred_element_type=F32)
        out = full[:, 0:HD]
        for h in range(1, heads):
            out = jnp.where(upper == h, full[:, h * HD : (h + 1) * HD], out)
        found[s * hr : (s + 1) * hr, :] = out
    if padded > pool * hr:
        found[pool * hr :, :] = jnp.zeros((padded - pool * hr, HD), F32)
    high, low = split_two(found[...])
    by_request = jnp.dot(gatherer[...], high, preferred_element_type=F32) + jnp.dot(
        gatherer[...], low, preferred_element_type=F32
    )
    high, low = split_two(pltpu.roll(total, HD // 2, 1))
    stats = jnp.concatenate(
        [jnp.where(slane < HD // 2, top, high.astype(F32)), low.astype(F32)], axis=0
    ).astype(BF16)
    by_request = by_request.astype(BF16)
    for d in range(ns):
        part[d, 0 : requests * hr, :] = by_request[d * requests * hr : (d + 1) * requests * hr, :]
        part[d, requests * hr :, :] = stats
    rbuf[me] = part[me]

    def push2(i, _):
        to = seq_far(i)
        pltpu.make_async_remote_copy(
            src_ref=part.at[to], dst_ref=rbuf.at[me], send_sem=send2, recv_sem=recv2,
            device_id=peer(to, exp), device_id_type=MESH,
        ).start()
        return 0

    lax.fori_loop(0, ns - 1, push2, 0)
    all2 = whole(part, send2, recv2)
    all2.wait_recv()

    shift = (HD - me * requests) % HD
    sums_of, tops = [], []
    for s in range(ns):
        stats = rbuf[s, requests * hr :, :].astype(F32)
        low = jnp.where(slane < HD // 2, 0.0, stats[hr:])
        tops.append(pltpu.roll(stats[0:hr] + low, shift, 1))
    fresh = jnp.full((hr, HD), -1e30, F32)
    for b in range(requests):
        rows = slice(b * hr, (b + 1) * hr)
        fresh = jnp.where(slane == b, new_top[rows], fresh)
        fresh = jnp.where(slane == HD // 2 + b, new_total[rows], fresh)
    tops.append(fresh)
    best = tops[0]
    for s in range(1, ns + 1):
        best = jnp.maximum(best, tops[s])
    factors, total = [], jnp.zeros((hr, HD), F32)
    for s in range(ns + 1):
        factor = jnp.exp(jnp.where(slane < requests, tops[s] - best, 0.0))
        factors.append(factor)
        total += pltpu.roll(tops[s], HD // 2, 1) * factor
    held = [rbuf[s, 0 : requests * hr, :].astype(F32) for s in range(ns)]
    attended = []
    for b in range(requests):
        rows = slice(b * hr, (b + 1) * hr)
        summed = new_out[rows] * factors[ns][:, b : b + 1]
        for s in range(ns):
            summed += held[s][rows] * factors[s][:, b : b + 1]
        attended.append(summed / total[:, b : b + 1])
    stacked = jnp.concatenate(attended, axis=0).astype(BF16)
    prow = lax.broadcasted_iota(jnp.int32, (ROWS, requests * hr), 0)
    pcol = lax.broadcasted_iota(jnp.int32, (ROWS, requests * hr), 1)
    by_head = []
    for h in range(cols // HD):
        pick = (pcol == prow // steps * hr + h * steps + prow % steps) & (prow < count)
        by_head.append(
            jnp.dot(
                jnp.where(pick, 1.0, 0.0).astype(BF16), stacked, preferred_element_type=F32
            ).astype(BF16)
        )
    own = jnp.concatenate(by_head, axis=1)
    load_wo.wait()
    for e in range(ne):
        terms[e] = jnp.dot(
            own, wo[:, e * cols : (e + 1) * cols], preferred_element_type=F32
        ).astype(BF16)

    def push3(i, _):
        to = exp_far(i)
        pltpu.make_async_remote_copy(
            src_ref=terms.at[to], dst_ref=r3.at[exp], send_sem=send3, recv_sem=recv3,
            device_id=peer(me, to), device_id_type=MESH,
        ).start()
        return 0

    lax.fori_loop(0, ne - 1, push3, 0)
    push(cbuf.at[me], cbuf.at[me], cosend, corecv)
    push(kvbuf, kv_ref.at[me], kvsend, kvrecv)
    r3[exp] = terms[exp]
    all3 = pltpu.make_async_remote_copy(
        src_ref=terms.at[pl.ds(0, ne - 1)], dst_ref=r3.at[pl.ds(0, ne - 1)],
        send_sem=send3, recv_sem=recv3, device_id=peer(me, (exp + 1) % ne), device_id_type=MESH,
    )
    all3.wait_recv()
    residual = xs[:, pl.ds(pl.multiple_of(exp * cols, cols), cols)]
    for e in range(ne):
        residual += r3[e].astype(F32)

    scaled = residual * fgain_ref[:, pl.ds(pl.multiple_of(exp * cols, cols), cols)]
    square = jnp.sum(residual * residual, axis=-1, keepdims=True)
    brow = lax.broadcasted_iota(jnp.int32, (ROWS, cols), 0)
    blane = lax.broadcasted_iota(jnp.int32, (ROWS, cols), 1)
    line = jnp.sum(jnp.where(brow == blane, square, 0.0), axis=0, keepdims=True)
    high, low = split_two(line)
    scaled = jnp.where(brow == count, high.astype(F32), scaled)
    scaled = jnp.where(brow == count + 1, low.astype(F32), scaled)
    my_cols = pl.ds(pl.multiple_of(z * cols, cols), cols)
    back = z * ns + me
    xbuf[core, my_rows, my_cols] = scaled.astype(BF16)

    def push4(i, _):
        there = (z + far_first(i // ns, nz)) % nz * 2 + core
        pltpu.make_async_remote_copy(
            src_ref=xbuf.at[core, my_rows, my_cols], dst_ref=xbuf.at[core, my_rows, my_cols],
            send_sem=send4.at[i // ns], recv_sem=recv4.at[z],
            device_id=peer(seq_far(i), there), device_id_type=MESH,
        ).start()
        return 0

    lax.fori_loop(0, nz * ns - 1, push4, 0)

    all_c = whole(cbuf, cosend, corecv)
    all_c.wait_recv()
    coefs = cbuf[...].reshape(total_rows, 2 * experts).astype(F32)
    clane = lax.broadcasted_iota(jnp.int32, (total_rows, 2 * experts), 1)
    ucol = lax.broadcasted_iota(jnp.int32, (total_rows, wd.shape[0]), 1)
    routing[...] = jnp.zeros(routing.shape, F32)
    for j in range(own_experts):
        mine = me * own_experts + j
        weight = jnp.sum(
            jnp.where((clane == mine) | (clane == mine + experts), coefs, 0.0), axis=-1, keepdims=True
        )
        routing[...] += jnp.where((ucol >= j * fe) & (ucol < (j + 1) * fe), weight, 0.0)

    arrival = [(z + nz - far_first(i, nz)) % nz for i in range(nz)]
    forwards = []
    for i in range(nz):
        k = arrival[i]
        span = pl.ds(0, total_rows - (ROWS if i == nz - 1 else 0))
        kcols = pl.ds(pl.multiple_of(k * cols, cols), cols)
        pltpu.make_async_remote_copy(
            src_ref=xbuf.at[core, span, kcols], dst_ref=xbuf.at[core, span, kcols],
            send_sem=send4.at[i], recv_sem=recv4.at[k], device_id=peer(me, twin), device_id_type=MESH,
        ).wait_recv()
        forward = pltpu.make_async_remote_copy(
            src_ref=xbuf.at[core, :, kcols], dst_ref=xbuf.at[core, :, kcols],
            send_sem=fsend.at[k], recv_sem=frecv.at[k], device_id=peer(me, twin), device_id_type=MESH,
        )
        forward.start()
        forwards.append(forward)

    for load in gate_up:
        load.wait()
    acc[0] = dot_t(xbuf[core], wg[core])
    acc[1] = dot_t(xbuf[core], wu[core])

    trow = lax.broadcasted_iota(jnp.int32, (total_rows, total_rows), 0)
    tcol = lax.broadcasted_iota(jnp.int32, (total_rows, total_rows), 1)
    spread = (trow // ROWS == tcol // ROWS) & ((tcol % ROWS == count) | (tcol % ROWS == count + 1))
    spread = jnp.where(spread, 1.0, 0.0).astype(BF16)

    def squares(c):
        value = xbuf[c, :, 0:HD].astype(F32)
        for k in range(1, nz):
            value += xbuf[c, :, k * cols : k * cols + HD].astype(F32)
        return value

    first = squares(core)
    for i in range(nz):
        k = arrival[i]
        kcols = pl.ds(pl.multiple_of(k * cols, cols), cols)
        pltpu.make_async_remote_copy(
            src_ref=xbuf.at[other, :, kcols], dst_ref=xbuf.at[other, :, kcols],
            send_sem=fsend.at[k], recv_sem=frecv.at[k], device_id=peer(me, twin), device_id_type=MESH,
        ).wait_recv()
    high, low = split_two(first + squares(other))
    square = jnp.dot(spread, high, preferred_element_type=F32) + jnp.dot(
        spread, low, preferred_element_type=F32
    )
    lrow = lax.broadcasted_iota(jnp.int32, (total_rows, HD), 0)
    llane = lax.broadcasted_iota(jnp.int32, (total_rows, HD), 1)
    square = jnp.sum(jnp.where(lrow % ROWS == llane, square, 0.0), axis=-1, keepdims=True)
    row_scale = lax.rsqrt(square / width + 1e-06)
    scales[...] = jnp.broadcast_to(row_scale, scales.shape)
    gate = (acc[0] + dot_t(xbuf[other], wg[other])) * row_scale
    up = (acc[1] + dot_t(xbuf[other], wu[other])) * row_scale
    inner = (silu(gate) * up * routing[...]).astype(BF16)
    load_wd.wait()

    def down(e):
        where = pl.ds(pl.multiple_of(e * cols, cols), cols)
        return jnp.dot(inner, wd[:, where], preferred_element_type=F32)

    pairs = []

    def give(i):
        k = (z + far_first(i, nz)) % nz
        ybuf[other, k] = packed(down(k * 2 + other), ns).astype(BF16)
        pair = pltpu.make_async_remote_copy(
            src_ref=ybuf.at[other, k], dst_ref=ypair.at[k],
            send_sem=psend.at[k], recv_sem=precv.at[k], device_id=peer(me, twin), device_id_type=MESH,
        )
        pair.start()
        pairs.append(pair)

    give(0)
    give(1)
    for i in range(nz):
        k = (z + far_first(i, nz)) % nz
        if i + 2 < nz:
            give(i + 2)
        sums[...] = packed(down(k * 2 + core), ns)
        pairs[i].wait_recv()
        ybuf[core, k] = (sums[...] + ypair[k].astype(F32)).astype(BF16)

        def push5(n, _):
            to = seq_far(n)
            pltpu.make_async_remote_copy(
                src_ref=ybuf.at[core, k, to], dst_ref=r5.at[back],
                send_sem=send5, recv_sem=recv5.at[z],
                device_id=peer(to, k * 2 + core), device_id_type=MESH,
            ).start()
            return 0

        lax.fori_loop(0, ns - 1 if i == nz - 1 else ns, push5, 0)
    r5[back] = ybuf[core, z, me]

    for load in shared_in:
        load.wait()
    load_sd.wait()
    gate = jnp.zeros((ROWS, sg.shape[1]), F32)
    up = jnp.zeros((ROWS, sg.shape[1]), F32)
    for c in range(2):
        rows = xbuf[c, my_rows, :]
        gate += dot_t(rows, sg[c])
        up += dot_t(rows, su[c])
    own_scale = scales[my_rows, 0:1]
    gate, up = gate * own_scale, up * own_scale
    inner = jnp.where(
        lax.broadcasted_iota(jnp.int32, gate.shape, 0) < count, silu(gate) * up, 0.0
    ).astype(BF16)
    for e in range(ne):
        shared[e] = jnp.dot(
            inner, sd[:, e * cols : (e + 1) * cols], preferred_element_type=F32
        ).astype(BF16)

    def push6(i, _):
        to = exp_far(i)
        pltpu.make_async_remote_copy(
            src_ref=shared.at[to], dst_ref=r6.at[exp], send_sem=send6, recv_sem=recv6,
            device_id=peer(me, to), device_id_type=MESH,
        ).start()
        return 0

    lax.fori_loop(0, ne - 1, push6, 0)
    r6[exp] = shared[exp]
    all6 = pltpu.make_async_remote_copy(
        src_ref=shared.at[pl.ds(0, ne - 1)], dst_ref=r6.at[pl.ds(0, ne - 1)],
        send_sem=send6, recv_sem=recv6, device_id=peer(me, (exp + 1) % ne), device_id_type=MESH,
    )
    all6.wait_recv()
    result = residual
    for e in range(ne):
        result += r6[e].astype(F32)

    routed = jnp.zeros(r5.shape[1:], F32)
    for i in range(nz):
        k = arrival[i]
        span = pl.ds(0, ns - (1 if i == nz - 1 else 0))
        pltpu.make_async_remote_copy(
            src_ref=r5.at[span], dst_ref=r5.at[span],
            send_sem=send5, recv_sem=recv5.at[k], device_id=peer(me, twin), device_id_type=MESH,
        ).wait_recv()
        for n in range(ns):
            routed += r5[k * ns + n].astype(F32)
    tail = jnp.concatenate([routed[0:4, cols:], routed[4:8, cols:]], axis=1)
    result = result[0:count] + jnp.concatenate([routed[:, 0:cols], tail], axis=0)
    for b in range(requests):
        out_ref[b] = result[b * steps : (b + 1) * steps, :]

    all_kv = whole(kv_ref, kvsend, kvrecv)
    all_kv.wait_recv()
    all_kv.wait_send()
    keep_kv.wait()
    all_q.wait_send()
    all_c.wait_send()
    all2.wait_send()
    all3.wait_send()
    rest = pl.ds(0, nz * ns - 1)
    pltpu.make_async_remote_copy(
        src_ref=r5.at[rest], dst_ref=r5.at[rest],
        send_sem=send5, recv_sem=recv5.at[0], device_id=peer(me, twin), device_id_type=MESH,
    ).wait_send()
    all6.wait_send()
    for i in range(nz):
        span = pl.ds(0, total_rows - (ROWS if i == nz - 1 else 0))
        pltpu.make_async_remote_copy(
            src_ref=xbuf.at[core, span, 0:cols], dst_ref=xbuf.at[core, span, 0:cols],
            send_sem=send4.at[i], recv_sem=recv4.at[i], device_id=peer(me, twin), device_id_type=MESH,
        ).wait_send()
    for i in range(nz):
        forwards[i].wait_send()
        pairs[i].wait_send()


def patch_kernel(
    req_any, blk_any, lens_any, kv_any, hidden_any, key_ref, value_ref,
    key_out, value_out, hidden_out,
    req_ref, blk_ref, lens_ref, kv_ref, hidden_ref, kbuf, vbuf, fresh_rows, small_sem, in_sem, out_sem,
    *, requests, steps, group,
):
    pool, block, cols = key_ref.shape
    ns = kv_any.shape[0]
    starts = list(range(0, pool, group))
    sizes = [min(group, pool - s) for s in starts]

    def copies(g, into):
        span = pl.ds(starts[g], sizes[g])
        pairs = ((key_ref, kbuf, key_out), (value_ref, vbuf, value_out))
        result = []
        for n, (source, buf, target) in enumerate(pairs):
            if into:
                result.append(pltpu.make_async_copy(source.at[span], buf.at[span], in_sem.at[n, g]))
            else:
                result.append(pltpu.make_async_copy(buf.at[span], target.at[span], out_sem.at[n, g]))
        return result

    small = []
    pairs = (
        (kv_any, kv_ref), (req_any, req_ref), (blk_any, blk_ref), (lens_any, lens_ref),
        (hidden_any, hidden_ref),
    )
    for n, (source, buf) in enumerate(pairs):
        load = pltpu.make_async_copy(source, buf, small_sem.at[n])
        load.start()
        small.append(load)
    for g in range(len(starts)):
        for c in copies(g, True):
            c.start()
    for load in small:
        load.wait()
    hidden_out[...] = hidden_ref[...]
    for s in range(ns):
        kv = kv_ref[s].astype(F32)
        for b in range(requests):
            fresh_rows[s * requests + b] = kv[b * steps : (b + 1) * steps, :]
    window = 2 * ROWS
    wrow = lax.broadcasted_iota(jnp.int32, (window, cols), 0)
    for g in range(len(starts)):
        for c in copies(g, True):
            c.wait()

        def patch(i, _):
            s = starts[g] + i
            request = jnp.maximum(req_ref[s], 0)
            offset = lens_ref[request] - blk_ref[s] * block

            @pl.when((req_ref[s] >= 0) & (offset > -steps) & (offset < block))
            def _():
                first = jnp.clip(offset // ROWS * ROWS, 0, block - window)
                first = pl.multiple_of(first, ROWS)
                rel = wrow + first - offset
                for n, buf in enumerate((kbuf, vbuf)):
                    tile = buf[s, pl.ds(first, window), :].astype(F32)
                    for t in range(steps):
                        one = fresh_rows[request, t : t + 1, n * cols : (n + 1) * cols]
                        tile = jnp.where(rel == t, one, tile)
                    buf[s, pl.ds(first, window), :] = tile.astype(BF16)

            return 0

        lax.fori_loop(0, sizes[g], patch, 0)
        for c in copies(g, False):
            c.start()
    for g in range(len(starts)):
        for c in copies(g, False):
            c.wait()


def body(
    hidden_in, cache_lens, slot_request, slot_block, key_cache, value_cache, attn_gain,
    query_weight, key_weight, value_weight, out_weight, ffn_gain, expert_ids, expert_weights,
    gate_experts, up_experts, down_experts, gate_shared, up_shared, down_shared,
):
    requests, steps, width = hidden_in.shape
    ns = lax.axis_size("seq")
    ne = lax.axis_size("exp")
    nz = ne // 2
    cols = query_weight.shape[1]
    own_experts, _, fe = gate_experts.shape
    sf = gate_shared.shape[1]
    experts = own_experts * ns
    pool, block, _ = key_cache.shape
    hr = cols // HD * steps
    total_rows = ns * ROWS
    padded = -(-pool * hr // 128) * 128

    exponent = np.arange(HD // 2) * (2.0 / HD)
    frequency = np.power(10000.0, -exponent).astype(np.float32)
    frequency = jnp.asarray(np.concatenate([frequency, frequency])[None, :])

    vmem = pl.BlockSpec(memory_space=pltpu.VMEM)
    anys = pl.BlockSpec(memory_space=pl.ANY)
    dma = pltpu.SemaphoreType.DMA

    hidden, new_kv = pl.pallas_call(
        layer_kernel,
        out_shape=(
            jax.ShapeDtypeStruct((requests, steps, cols), F32),
            jax.ShapeDtypeStruct((ns, ROWS, 2 * cols), BF16),
        ),
        in_specs=[anys] * 21,
        out_specs=(vmem, anys),
        scratch_shapes=[
            pltpu.SMEM(cache_lens.shape, jnp.int32),
            pltpu.SMEM(slot_request.shape, jnp.int32),
            pltpu.SMEM(slot_block.shape, jnp.int32),
            pltpu.VMEM((1, HD), F32),
            pltpu.VMEM(hidden_in.shape, F32),
            pltpu.VMEM((1, width), F32),
            pltpu.VMEM(expert_ids.shape, jnp.int32),
            pltpu.VMEM(expert_weights.shape, F32),
            pltpu.VMEM((1, width), F32),
            pltpu.VMEM((3, width, cols), BF16),
            pltpu.VMEM((ns, ROWS, cols), BF16),
            pltpu.VMEM((ROWS, 2 * cols), BF16),
            pltpu.VMEM((ns, ROWS, 2 * experts), BF16),
            pltpu.VMEM((ROWS, 2 * experts), F32),
            pltpu.VMEM(key_cache.shape, BF16),
            pltpu.VMEM(key_cache.shape, BF16),
            pltpu.VMEM((padded, total_rows), F32),
            pltpu.VMEM((ns * requests * hr, padded), BF16),
            pltpu.VMEM((padded, cols), F32),
            pltpu.VMEM((ns, (requests + 2) * hr, HD), BF16),
            pltpu.VMEM((padded, HD), F32),
            pltpu.VMEM((cols, width), BF16),
            pltpu.VMEM((2, own_experts * fe, width // 2), BF16),
            pltpu.VMEM((2, own_experts * fe, width // 2), BF16),
            pltpu.VMEM((own_experts * fe, width), BF16),
            pltpu.VMEM((2, sf, width // 2), BF16),
            pltpu.VMEM((2, sf, width // 2), BF16),
            pltpu.VMEM((sf, width), BF16),
            pltpu.VMEM((ns, (requests + 2) * hr, HD), BF16),
            pltpu.VMEM((ROWS, width), F32),
            pltpu.VMEM((ne, ROWS, cols), BF16),
            pltpu.VMEM((ne, ROWS, cols), BF16),
            pltpu.VMEM((2, total_rows, nz * cols), BF16),
            pltpu.VMEM((2, total_rows, own_experts * fe), F32),
            pltpu.VMEM((total_rows, own_experts * fe), F32),
            pltpu.VMEM((total_rows, HD), F32),
            pltpu.VMEM((2, nz, ns, 8, cols + cols // 2), BF16),
            pltpu.VMEM((nz, ns, 8, cols + cols // 2), BF16),
            pltpu.VMEM((ns, 8, cols + cols // 2), F32),
            pltpu.VMEM((nz * ns, 8, cols + cols // 2), BF16),
            pltpu.VMEM((ne, ROWS, cols), BF16),
            pltpu.VMEM((ne, ROWS, cols), BF16),
            dma((9,)), dma((3,)), dma((2, 4)), dma,
            dma, dma, dma, dma, dma, dma,
            dma((3 + 8 * nz,)),
            dma, dma, dma, dma, dma((nz,)),
            dma((nz,)), dma((nz,)), dma((nz,)), dma((nz,)), dma((nz,)),
            dma, dma((nz,)), dma, dma,
        ],
        compiler_params=pltpu.CompilerParams(collective_id=0, has_side_effects=True),
        name="layer",
    )(
        cache_lens, slot_request, slot_block, frequency, hidden_in, attn_gain[None, :],
        expert_ids, expert_weights, ffn_gain[None, :],
        query_weight, key_weight, value_weight, key_cache, value_cache, out_weight,
        jnp.swapaxes(gate_experts, 1, 2).reshape(own_experts * fe, width),
        jnp.swapaxes(up_experts, 1, 2).reshape(own_experts * fe, width),
        down_experts.reshape(own_experts * fe, width),
        gate_shared.T, up_shared.T, down_shared,
    )

    group = 8
    groups = -(-pool // group)
    key_out, value_out, hidden_out = pl.pallas_call(
        functools.partial(patch_kernel, requests=requests, steps=steps, group=group),
        out_shape=(
            jax.ShapeDtypeStruct(key_cache.shape, BF16),
            jax.ShapeDtypeStruct(value_cache.shape, BF16),
            jax.ShapeDtypeStruct(hidden.shape, F32),
        ),
        in_specs=[anys] * 7,
        out_specs=(anys, anys, vmem),
        scratch_shapes=[
            pltpu.SMEM(slot_request.shape, jnp.int32),
            pltpu.SMEM(slot_block.shape, jnp.int32),
            pltpu.SMEM(cache_lens.shape, jnp.int32),
            pltpu.VMEM(new_kv.shape, BF16),
            pltpu.VMEM(hidden.shape, F32),
            pltpu.VMEM(key_cache.shape, BF16),
            pltpu.VMEM(key_cache.shape, BF16),
            pltpu.VMEM((ns * requests, steps, 2 * cols), F32),
            dma((5,)),
            dma((2, groups)),
            dma((2, groups)),
        ],
        name="patch",
    )(slot_request, slot_block, cache_lens, new_kv, hidden, key_cache, value_cache)
    return (hidden_out, key_out, value_out)


def solution(mesh):
    in_specs = (
        P("seq", None, None),
        P(),
        P("seq"),
        P("seq"),
        P("seq", None, "exp"),
        P("seq", None, "exp"),
        P(),
        P(None, "exp"),
        P(None, "exp"),
        P(None, "exp"),
        P("exp", None),
        P(),
        P("seq", None, None),
        P("seq", None, None),
        P("seq", None, "exp"),
        P("seq", None, "exp"),
        P("seq", "exp", None),
        P(None, "exp"),
        P(None, "exp"),
        P("exp", None),
    )
    out_specs = (P("seq", None, "exp"), P("seq", None, "exp"), P("seq", None, "exp"))
    return jax.shard_map(body, mesh=mesh, in_specs=in_specs, out_specs=out_specs, check_vma=False)
```
